32 devices in a mesh: patch: 8 (over z, x), var: 4 (over y, core).
Axes of the slice: x: 2, y: 2, z: 4, core: 2. Of those that a mesh axis runs over, the one named last changes fastest.
Arguments:
- pixels: bfloat16 [48, 4, 8192], P('var', None, 'patch'), may hold values from -6 to 6
- embed: float32 [48, 5, 1024], P('var', None, 'patch'), may hold values from -3 to 3
- query: float32 [1024], P(('patch', 'var')), may hold values from -9 to 9
- w_query: float32 [1024, 1024], P(('patch', 'var')), may hold values from -0.1875 to 0.1875
- w_key: float32 [1024, 1024], P(('patch', 'var')), may hold values from -0.1875 to 0.1875
- w_value: float32 [1024, 1024], P(('patch', 'var')), may hold values from -0.1875 to 0.1875
- w_out: float32 [1024, 1024], P('patch', 'var'), may hold values from -0.5 to 0.5
- b_out: float32 [1024], P(('patch', 'var')), may hold values from -3 to 3
- pos_embed: float32 [2048, 1024], P('patch', 'var'), may hold values from -3 to 3
- w_lead: float32 [1024], P(('patch', 'var')), may hold values from -3 to 3
- avail: int32 [4, 48], replicated, may hold values from 0 to 1, as said below
- lengths: int32 [4], replicated, may hold values from 1024 to 2048, as said below
- lead_hours: int32 [4], replicated, may hold values from 6 to 168
- cotangent: bfloat16 [8192, 1024], P('patch', 'var'), may hold values from -6 to 6
Outputs:
- mixed: bfloat16 [8192, 1024], P('patch', 'var')
- grad_pixels: bfloat16 [48, 4, 8192], P('var', None, 'patch')
- grad_embed: float32 [48, 5, 1024], P('var', None, 'patch')
- grad_query: float32 [1024], P(('patch', 'var'))
- grad_w_query: float32 [1024, 1024], P(('patch', 'var'))
- grad_w_key: float32 [1024, 1024], P(('patch', 'var'))
- grad_w_value: float32 [1024, 1024], P(('patch', 'var'))
- grad_w_out: float32 [1024, 1024], P('patch', 'var')
- grad_b_out: float32 [1024], P(('patch', 'var'))
- grad_pos_embed: float32 [2048, 1024], P('patch', 'var')
- grad_w_lead: float32 [1024], P(('patch', 'var'))
The draws below stay inside these ranges and needn't reach their ends.
Inputs may be any that keep to these rules, and one draw needn't show every extreme that they name: `avail`: every sample has at least one available variable. `lengths`: at least one group is full.
All inputs are finite; a program needn't handle non-finite values.
Results may differ from the reference program's by a relative error of at most 0.018.
Values may be sent and summed in bfloat16 or wider, within the bound.
No kernel may reach another device: no remote copies, remote signals or barrier semaphores. Data moves between devices by JAX's collectives and lax.ppermute only.
A program may use at most 256 MiB of HBM per device.

```python
import math
import jax
import jax.numpy as jnp
from jax import lax

D = 1024
HEADS = 16
VARS = 48
PIX = 4
GROUP = 2048
TOKENS = 8192
SAMPLES = 4


def draw_avail(key, part):
    key_bits, key_force = jax.random.split(jax.random.fold_in(key, 11))
    drawn = jax.random.randint(key_bits, (SAMPLES, VARS), 0, 4)
    forced = jax.random.randint(key_force, (SAMPLES, 1), 0, VARS)
    labels = jnp.arange(VARS, dtype=jnp.int32)[None, :]
    return jnp.where((drawn < 3) | (labels == forced), 1, 0).astype(jnp.int32)


def draw_lengths(key, part):
    key_len, key_full = jax.random.split(jax.random.fold_in(key, 23))
    drawn = jax.random.randint(key_len, (SAMPLES,), GROUP // 2, GROUP + 1)
    full_at = jax.random.randint(key_full, (), 0, SAMPLES)
    return jnp.where(jnp.arange(SAMPLES, dtype=jnp.int32) == full_at, GROUP, drawn).astype(jnp.int32)


def touch_ends(values, own_key, least, high):
    dims = values.shape
    place = [jax.random.randint(jax.random.fold_in(own_key, axis), (), 0, dims[axis]) for axis in range(len(dims))]
    values = values.at[tuple(place)].set(least)
    longest = dims.index(max(dims))
    place[longest] = (place[longest] + 1) % dims[longest]
    return values.at[tuple(place)].set(high)


def block_levels(own_key, dims, cuts, least, high):
    def one(dim, parts):
        steps = jax.random.uniform(jax.random.fold_in(jax.random.fold_in(own_key, 6), dim), (parts,), jnp.float32, least / len(cuts), high / len(cuts))
        return jnp.repeat(jnp.exp(steps), dims[dim] // parts).reshape((-1,) + (1,) * (len(dims) - dim - 1))

    level = one(*cuts[0])
    for cut in cuts[1:]:
        level = level * one(*cut)
    return level


def gaussian(rng, dims, width, most, cuts=(), kind=jnp.bfloat16):
    array = width * jax.random.normal(rng, dims, jnp.float32)
    if cuts:
        array = array * block_levels(rng, dims, cuts, -0.22, 0.18)
    return jnp.clip(array, -most, most).astype(kind)


def setup_inputs(seed: int = 0) -> dict:
    arg_keys = jax.random.split(jax.random.key(seed), 15)
    return {
        "pixels": gaussian(arg_keys[0], (VARS, PIX, TOKENS), 1.0, 6.0, ((0, 4), (2, 8))),
        "embed": gaussian(arg_keys[1], (VARS, 5, D), 4 ** -0.5, 3.0, ((0, 4), (2, 8)), jnp.float32),
        "query": gaussian(arg_keys[2], (D,), 1.5, 9.0, ((0, 32),), jnp.float32),
        "w_query": gaussian(arg_keys[3], (D, D), D ** -0.5, 0.1875, ((0, 32),), jnp.float32),
        "w_key": gaussian(arg_keys[4], (D, D), D ** -0.5, 0.1875, ((0, 32),), jnp.float32),
        "w_value": gaussian(arg_keys[5], (D, D), D ** -0.5, 0.1875, ((0, 32),), jnp.float32),
        "w_out": gaussian(arg_keys[6], (D, D), (D // 8) ** -0.5, 0.5, ((0, 8), (1, 4)), jnp.float32),
        "b_out": gaussian(arg_keys[7], (D,), 0.5, 3.0, ((0, 32),), jnp.float32),
        "pos_embed": gaussian(arg_keys[8], (GROUP, D), 0.5, 3.0, ((0, 8), (1, 4)), jnp.float32),
        "w_lead": gaussian(arg_keys[9], (D,), 0.5, 3.0, ((0, 32),), jnp.float32),
        "avail": draw_avail(jax.random.fold_in(arg_keys[14], 71), 0),
        "lengths": draw_lengths(jax.random.fold_in(arg_keys[14], 71), 0),
        "lead_hours": touch_ends(jax.random.randint(arg_keys[12], (SAMPLES,), 6, 169), jax.random.fold_in(arg_keys[12], 1), 6, 168).astype(jnp.int32),
        "cotangent": gaussian(arg_keys[13], (TOKENS, D), 1.0, 6.0, ((0, 8), (1, 4))),
    }


highest = lax.Precision.HIGHEST

@jax.custom_vjp
def low(v):
    return lax.optimization_barrier(v.astype(jnp.bfloat16)).astype(jnp.float32)

@jax.custom_vjp
def low_back(v):
    return v

def low_keep(v):
    return (low(v), None)

def low_pass(kept, grad):
    return (grad,)

def back_keep(v):
    return (v, None)

def back_low(kept, grad):
    return (low(grad),)
low.defvjp(low_keep, low_pass)
low_back.defvjp(back_keep, back_low)

def group_forward(pix, avail_row, length, lead, emb, fold, value_w, out_w, bias, pos, lead_w):
    token = jnp.einsum('vpt,vpd->vtd', pix, emb[:, :4], precision=highest) + emb[:, 4][:, None, :]
    token = low_back(low(token))
    scores = low_back(jnp.einsum('vtd,dh->vth', token, fold, precision=highest))
    values = low_back(low(jnp.einsum('vtd,de->vte', token, value_w, precision=highest)))
    present = (avail_row > 0)[:, None, None]
    masked = jnp.where(present, scores, -1e+30)
    top = lax.optimization_barrier(jnp.max(masked, axis=0))
    weight = jnp.where(present, jnp.exp(masked - top), 0.0)
    total = lax.optimization_barrier(jnp.sum(weight, axis=0))
    prob = weight / total
    count = values.shape[0]
    rows = values.shape[1]
    attended = jnp.einsum('vth,vthe->the', prob, values.reshape(count, rows, HEADS, D // HEADS), precision=highest).reshape(rows, D)
    attended = low_back(low(attended))
    mixed = jnp.dot(attended, out_w, precision=highest) + bias + pos + lead / 100.0 * lead_w
    valid = (jnp.arange(rows) < length)[:, None]
    return jnp.where(valid, mixed, 0.0)

def forward(pixels, embed, query, w_query, w_key, w_value, w_out, b_out, pos_embed, w_lead, avail, lengths, lead_hours):
    emb = low(embed)
    qvec = jnp.dot(low(query), low(w_query), precision=highest)
    hsize = D // HEADS
    fold = jnp.einsum('dhe,he->dh', low(w_key).reshape(D, HEADS, hsize), qvec.reshape(HEADS, hsize), precision=highest)
    fold = low(fold / math.sqrt(hsize))
    value_w = low(w_value)
    out_w = low(w_out)
    bias = low(b_out)
    pos = low(pos_embed)
    lead_w = low(w_lead)
    blocks = pixels.reshape(VARS, PIX, SAMPLES, GROUP).transpose(2, 0, 1, 3)
    step_fn = jax.checkpoint(group_forward)

    def scan_step(carry, items):
        pix, avail_row, length, lead = items
        return (carry, step_fn(pix, avail_row, length, lead, emb, fold, value_w, out_w, bias, pos, lead_w))
    carry, outs = lax.scan(scan_step, 0, (blocks, avail, lengths, lead_hours.astype(jnp.float32)))
    return outs.reshape(TOKENS, D)

def reference(pixels, embed, query, w_query, w_key, w_value, w_out, b_out, pos_embed, w_lead, avail, lengths, lead_hours, cotangent):
    floats = (pixels.astype(jnp.float32), embed, query, w_query, w_key, w_value, w_out, b_out, pos_embed, w_lead)

    def closed(*values):
        return forward(*values, avail, lengths, lead_hours)
    mixed, pull = jax.vjp(closed, *floats)
    grads = pull(cotangent.astype(jnp.float32))
    return (mixed.astype(jnp.bfloat16), grads[0].astype(jnp.bfloat16), grads[1], grads[2], grads[3], grads[4], grads[5], grads[6], grads[7], grads[8], grads[9])
```

```python
import functools
import math

import jax
import jax.numpy as jnp
from jax import lax
from jax.experimental import pallas as pl
from jax.experimental.pallas import tpu as pltpu
from jax.sharding import PartitionSpec as P

D = 1024
HEADS = 16
HS = D // HEADS
GROUP = 2048
F32 = jnp.float32
BF16 = jnp.bfloat16
NEG = -1e30


def exchange(x, axis, groups=None):
    return lax.all_to_all(x, axis, 0, 0, tiled=True, axis_index_groups=groups)


def spread(x, axis):
    n = lax.axis_size(axis)
    return exchange(jnp.broadcast_to(x[None], (n,) + x.shape).reshape((n * x.shape[0],) + x.shape[1:]), axis)


def flip(x, axis, bit):
    n = lax.axis_size(axis)
    return lax.ppermute(x, axis, [(i, i ^ bit) for i in range(n)])


def hi_lo(x):
    hi = x.astype(BF16)
    return hi, (x - hi.astype(F32)).astype(BF16)


def nt(a, b):
    return lax.dot_general(a, b, (((1,), (1,)), ((), ())), preferred_element_type=F32)


def tn(a, b):
    return lax.dot_general(a, b, (((0,), (0,)), ((), ())), preferred_element_type=F32)


def nn(a, b):
    return jnp.dot(a, b, preferred_element_type=F32)


def forward_kernel(tile, x_ref, ef_ref, vwt_ref, mask_ref, att_ref, prob_ref):
    nv = x_ref.shape[1]
    heads = prob_ref.shape[0]
    present = mask_ref[...] > 0.5

    def step(i, carry):
        cols = pl.ds(pl.multiple_of(i * tile, tile), tile)
        xs = [x_ref[p, :, cols].astype(F32) for p in range(4)]
        for h in range(heads):
            s = jnp.broadcast_to(ef_ref[4, :, h : h + 1], (nv, tile))
            for p in range(4):
                s = s + ef_ref[p, :, h : h + 1] * xs[p]
            s = jnp.where(present, s, NEG)
            w = jnp.where(present, jnp.exp(s - jnp.max(s, axis=0, keepdims=True)), 0.0)
            prob = w / jnp.sum(w, axis=0, keepdims=True)
            prob_ref[h, :, cols] = prob
            a = jnp.concatenate([(prob * x).astype(BF16) for x in xs] + [prob.astype(BF16)], axis=0)
            att_ref[h * HS : (h + 1) * HS, cols] = nn(vwt_ref[h * HS : (h + 1) * HS, :], a).astype(BF16)
        return carry

    lax.fori_loop(0, x_ref.shape[2] // tile, step, 0)


def backward_kernel(tile, x_ref, ef_ref, vw_ref, prob_ref, grad_ref, gx_ref, gv_ref, gs_ref, acc_ref):
    nv = x_ref.shape[1]
    heads = prob_ref.shape[0]
    gv_ref[...] = jnp.zeros_like(gv_ref)
    acc_ref[...] = jnp.zeros_like(acc_ref)

    def step(i, carry):
        cols = pl.ds(pl.multiple_of(i * tile, tile), tile)
        xs = [x_ref[p, :, cols].astype(F32) for p in range(4)]
        gx = [jnp.zeros((nv, tile), F32) for _ in range(4)]
        for h in range(heads):
            hc = slice(h * HS, (h + 1) * HS)
            prob = prob_ref[h, :, cols]
            gh = grad_ref[hc, cols]
            g = nn(vw_ref[:, hc], gh)
            gp = [g[p * nv : (p + 1) * nv] for p in range(5)]
            gprob = gp[4]
            for p in range(4):
                gprob = gprob + xs[p] * gp[p]
            inner = jnp.sum(prob * gprob, axis=0, keepdims=True)
            gs = prob * (gprob - inner)
            for p in range(4):
                gx[p] = gx[p] + prob * gp[p] + ef_ref[p, :, h : h + 1] * gs
            a = jnp.concatenate([(prob * x).astype(BF16) for x in xs] + [prob.astype(BF16)], axis=0)
            gv_ref[:, hc] += nt(a, gh)
            for p in range(5):
                t = gs if p == 4 else gs * xs[p]
                part = t[:, :128]
                for k in range(1, tile // 128):
                    part = part + t[:, k * 128 : (k + 1) * 128]
                acc_ref[p * heads + h] += part
        for p in range(4):
            gx_ref[p, :, cols] = gx[p].astype(BF16)
        return carry

    lax.fori_loop(0, x_ref.shape[2] // tile, step, 0)
    for p in range(5):
        gs_ref[p * nv : (p + 1) * nv, :] = jnp.concatenate(
            [jnp.sum(acc_ref[p * heads + h], axis=1, keepdims=True) for h in range(heads)], axis=1
        )


def attention_forward(x, ef, vwt, mask):
    nv, rows = x.shape[1:]
    cw = vwt.shape[0]
    heads = cw // HS
    return pl.pallas_call(
        functools.partial(forward_kernel, 256),
        out_shape=(
            jax.ShapeDtypeStruct((cw, rows), BF16),
            jax.ShapeDtypeStruct((heads, nv, rows), F32),
        ),
        name="attention_forward",
        cost_estimate=pl.CostEstimate(flops=heads * nv * rows * 800, bytes_accessed=3 << 20, transcendentals=0),
    )(x, ef, vwt, mask)


def attention_backward(x, ef, vw, prob, grad):
    nv, rows = x.shape[1:]
    cw = grad.shape[0]
    heads = cw // HS
    return pl.pallas_call(
        functools.partial(backward_kernel, 256),
        out_shape=(
            jax.ShapeDtypeStruct((4, nv, rows), BF16),
            jax.ShapeDtypeStruct((5 * nv, cw), F32),
            jax.ShapeDtypeStruct((5 * nv, heads), F32),
        ),
        scratch_shapes=[pltpu.VMEM((5 * heads, nv, 128), F32)],
        name="attention_backward",
        cost_estimate=pl.CostEstimate(flops=heads * nv * rows * 1600, bytes_accessed=3 << 20, transcendentals=0),
    )(x, ef, vw, prob, grad)


def shards(pixels, embed, query, w_query, w_key, w_value, w_out, b_out, pos_embed, w_lead, avail, lengths, lead_hours, cotangent):
    n_p = lax.axis_size("patch")
    n_j = lax.axis_size("var")
    p_id = lax.axis_index("patch")
    j_id = lax.axis_index("var")
    vl, _, rows = pixels.shape
    nv = vl * n_j
    cw = w_out.shape[1]
    hl = cw // HS
    dp = embed.shape[2]
    rl = w_value.shape[0]
    eb = -(-5 * vl // 16) * 16 if (5 * vl) % 16 else 5 * vl + 16
    scale = 1.0 / math.sqrt(HS)

    row0 = p_id * rows
    sample = row0 // GROUP
    pos0 = row0 % GROUP
    length = lax.dynamic_index_in_dim(lengths, sample, 0, False)
    lead = lax.dynamic_index_in_dim(lead_hours, sample, 0, False).astype(F32) / 100.0
    mask = lax.dynamic_index_in_dim(avail, sample, 0, False).astype(F32)[:, None]
    valid = (pos0 + jnp.arange(rows, dtype=jnp.int32) < length)[:, None]
    grad_rows = jnp.where(valid, cotangent, jnp.zeros_like(cotangent))
    colsum = jnp.sum(grad_rows.astype(F32), axis=0)

    q_low = query.astype(BF16)
    wq_low = w_query.astype(BF16)
    v_low = w_value.astype(BF16)
    k_low = w_key.astype(BF16)
    q_part = nn(q_low[None, :], wq_low).reshape(n_j, 1, cw)
    q_hi, q_lo = hi_lo(q_part)
    e_own = embed.astype(BF16).reshape(5 * vl, dp)
    e_pad = jnp.broadcast_to(jnp.pad(e_own, ((0, 0), (0, cw - dp)))[None], (n_j, 5 * vl, cw))

    def by_dest(w):
        return w.reshape(rl, n_j, cw).transpose(1, 0, 2)

    tail = jnp.zeros((n_j, eb - 5 * vl - 2, cw), BF16)
    pack = jnp.concatenate([e_pad, q_hi, q_lo, tail, by_dest(v_low), by_dest(k_low)], axis=1)
    got = exchange(pack.reshape(-1, cw), "var").reshape(n_j, eb + 2 * rl, cw)
    e_all = got[:, : 5 * vl, :dp].reshape(5 * nv, dp)
    q_sum = jnp.sum(got[:, 5 * vl : 5 * vl + 2].astype(F32), axis=(0, 1))
    v_blk = got[:, eb : eb + rl].reshape(dp, cw)
    k_blk = got[:, eb + rl :].reshape(dp, cw)

    part = nn(e_all, jnp.concatenate([v_blk, k_blk], axis=1)).astype(BF16)
    small = jnp.stack([q_sum, colsum, lead * colsum])
    s_hi, s_lo = hi_lo(small)
    rc = -(-(5 * nv + 3) // (16 * n_p)) * 16 if n_p <= 8 else -(-(5 * nv + 3) // (8 * n_p)) * 8
    full = rc * n_p
    part = jnp.concatenate(
        [part, jnp.concatenate([s_hi, s_lo], axis=1), jnp.zeros((full - 5 * nv - 3, 2 * cw), BF16)], axis=0
    )
    got2 = exchange(part, "patch").reshape(n_p, rc, 2 * cw)
    total2 = jnp.sum(got2.astype(F32), axis=0)
    extra = (p_id * rc + jnp.arange(rc) >= 5 * nv)[:, None]
    both_hi, both_lo = hi_lo(total2[:, :cw] + total2[:, cw:])
    chunk = jnp.where(extra, jnp.concatenate([both_hi, both_lo], axis=1), total2.astype(BF16))
    vk = spread(chunk, "patch")
    small = vk[5 * nv : 5 * nv + 3].astype(F32)
    small = small[:, :cw] + small[:, cw:]
    qvec = small[0]
    vw_nat = vk[: 5 * nv, :cw]
    ke_nat = vk[: 5 * nv, cw:].astype(F32)
    ef_nat = jnp.sum((ke_nat * (qvec * scale)[None]).reshape(5 * nv, hl, HS), axis=2)
    vw = vw_nat.reshape(nv, 5, cw).transpose(1, 0, 2).reshape(5 * nv, cw)
    ef = ef_nat.reshape(nv, 5, hl).transpose(1, 0, 2)

    pix = lax.all_gather(pixels, "var", axis=0, tiled=True).transpose(1, 0, 2)

    att, prob = attention_forward(pix, ef, vw.T, mask)

    wo = spread(w_out.astype(BF16), "patch")
    held = nt(wo, grad_rows).reshape(n_j, cw, rows)
    bit = 1
    while bit < n_j:
        mine = (j_id // bit) % 2
        pair = held.reshape(held.shape[0] // 2, 2, cw, rows)
        keep = lax.dynamic_index_in_dim(pair, mine, 1, False)
        send = lax.dynamic_index_in_dim(pair, 1 - mine, 1, False).astype(BF16)
        held = keep + flip(send, "var", bit).astype(F32)
        bit *= 2
    grad_att = held.reshape(cw, rows).astype(BF16)

    gx, gv, gs = attention_backward(pix, ef, vw, prob, grad_att)

    gx = gx.reshape(4, n_j, vl, rows).transpose(1, 2, 0, 3).reshape(nv, 4, rows)
    gx = exchange(gx, "var").reshape(n_j, vl, 4, rows)
    grad_pixels = jnp.sum(gx.astype(F32), axis=0).astype(BF16)

    blocks = [att]
    bit = 1
    while bit < n_j:
        blocks = blocks + [flip(b, "var", bit) for b in blocks]
        bit *= 2
    wo_blocks = wo.reshape(n_j, cw, cw)
    result = None
    gwo = []
    for k, b in enumerate(blocks):
        term = tn(b, lax.dynamic_index_in_dim(wo_blocks, j_id ^ k, 0, False))
        result = term if result is None else result + term
        gwo.append(nn(b, grad_rows).astype(BF16))
    gwo = jnp.stack(gwo)
    bit = 1
    while bit < n_j:
        pair = gwo.reshape(n_j // (2 * bit), 2, bit, cw, cw)
        gwo = jnp.where((j_id // bit) % 2 == 1, pair[:, ::-1], pair).reshape(n_j, cw, cw)
        bit *= 2
    gwo = exchange(gwo.reshape(D, cw), "patch").reshape(n_p, dp, cw)
    grad_w_out = jnp.sum(gwo.astype(F32), axis=0)

    parts = GROUP // rows
    owners = n_p // parts
    per = pos_embed.shape[0]
    groups = [[parts * i + k for i in range(owners)] for k in range(parts)]
    there = [(k * owners + i, parts * i + k) for i in range(owners) for k in range(parts)]
    back = [(b, a) for a, b in there]
    pos = lax.ppermute(pos_embed.astype(BF16), "patch", there)
    pos = exchange(jnp.broadcast_to(pos[None], (owners, per, cw)).reshape(rows, cw), "patch", groups)
    gpos = exchange(grad_rows, "patch", groups).reshape(owners, per, cw)
    gpos = jnp.sum(gpos.astype(F32), axis=0).astype(BF16)
    grad_pos = lax.ppermute(gpos, "patch", back).astype(F32)

    bl_hi, bl_lo = hi_lo(jnp.stack([b_out, w_lead]))
    del bl_lo
    bl = lax.all_gather(bl_hi, ("patch", "var"), axis=1, tiled=True)
    bl = lax.dynamic_slice_in_dim(bl, j_id * cw, cw, 1).astype(F32)
    result = result + bl[0] + pos.astype(F32) + lead * bl[1]
    mixed = jnp.where(valid, result, 0.0).astype(BF16)

    gs_hi, gs_lo = hi_lo(gs)
    z = jnp.concatenate([gv.astype(BF16), gs_hi, gs_lo, jnp.zeros((5 * nv, 128 - 2 * hl), BF16)], axis=1)
    z = z.reshape(5, nv, cw + 128).transpose(1, 0, 2).reshape(5 * nv, cw + 128)
    z = jnp.concatenate([z, jnp.zeros((full - 5 * nv, cw + 128), BF16)], axis=0)
    z = jnp.sum(exchange(z, "patch").reshape(n_p, rc, cw + 128).astype(F32), axis=0)
    gst_hi, gst_lo = hi_lo(z[:, cw : cw + hl] + z[:, cw + hl : cw + 2 * hl])
    z = jnp.concatenate([z[:, :cw].astype(BF16), gst_hi, gst_lo, jnp.zeros((rc, 128 - 2 * hl), BF16)], axis=1)
    z = spread(z, "patch")
    gst = z[: 5 * nv, cw : cw + hl].astype(F32) + z[: 5 * nv, cw + hl : cw + 2 * hl].astype(F32)
    gq_own = jnp.sum(jnp.repeat(gst, HS, axis=1) * ke_nat, axis=0) * scale
    fold = jnp.sum((k_blk.astype(F32) * (qvec * scale)[None]).reshape(dp, hl, HS), axis=2)
    rows4 = jnp.stack([gq_own, qvec, small[1], small[2]])
    r_hi, r_lo = hi_lo(rows4)
    lanes = jnp.pad(fold.astype(BF16), ((0, 8), (0, 128 - hl)))
    last = jnp.concatenate(
        [z[: 5 * nv], jnp.concatenate([jnp.concatenate([r_hi, r_lo], axis=0), jnp.zeros((8, 128), BF16)], axis=1)], axis=0
    )
    last = jnp.concatenate([last, jnp.pad(lanes[:dp], ((0, 0), (cw, 0)))], axis=0)
    allz = lax.all_gather(last, "var", axis=0, tiled=False)
    zz = allz[:, : 5 * nv, :cw]
    gsa = allz[:, : 5 * nv, cw : cw + hl].astype(F32) + allz[:, : 5 * nv, cw + hl : cw + 2 * hl].astype(F32)
    rowsa = allz[:, 5 * nv : 5 * nv + 4, :cw].astype(F32) + allz[:, 5 * nv + 4 : 5 * nv + 8, :cw].astype(F32)
    rowsa = rowsa.transpose(1, 0, 2).reshape(4, D)
    gq, qv = rowsa[0], rowsa[1]
    folda = allz[:, 5 * nv + 8 :, cw : cw + hl].astype(F32)
    e_mine = lax.dynamic_slice_in_dim(e_all, j_id * rl, rl, 1)
    grad_w_value = jnp.einsum("rd,jrc->djc", e_mine, zz, preferred_element_type=F32).reshape(rl, D)
    gfold = jnp.einsum("rd,jrh->djh", e_mine.astype(F32), gsa, precision=lax.Precision.HIGHEST).reshape(rl, HEADS)
    grad_w_key = jnp.repeat(gfold, HS, axis=1) * (qv * scale)[None]
    v_rows = lax.all_gather(v_low, "var", axis=0, tiled=True)
    z_mine = lax.dynamic_slice_in_dim(zz, j_id * 5 * vl, 5 * vl, 1)
    gs_mine = lax.dynamic_slice_in_dim(gsa, j_id * 5 * vl, 5 * vl, 1)
    ge = jnp.einsum("jrc,djc->rd", z_mine, v_rows.reshape(dp, n_j, cw), preferred_element_type=F32)
    ge = ge + jnp.einsum("jrh,jdh->rd", gs_mine, folda, precision=lax.Precision.HIGHEST)
    grad_embed = ge.reshape(vl, 5, dp)
    grad_w_query = q_low.astype(F32)[:, None] * gq[None, :]
    grad_query = jnp.sum(wq_low.astype(F32) * gq[None, :], axis=1)
    out0 = (p_id * n_j + j_id) * rl
    grad_bias = lax.dynamic_slice_in_dim(rowsa[2], out0, rl)
    grad_lead = lax.dynamic_slice_in_dim(rowsa[3], out0, rl)
    return (
        mixed,
        grad_pixels,
        grad_embed,
        grad_query,
        grad_w_query,
        grad_w_key,
        grad_w_value,
        grad_w_out,
        grad_bias,
        grad_pos,
        grad_lead,
    )


def solution(mesh):
    both = P(("patch", "var"))
    rows2 = P(("patch", "var"), None)
    return jax.shard_map(
        shards,
        mesh=mesh,
        in_specs=(
            P("var", None, "patch"),
            P("var", None, "patch"),
            both,
            rows2,
            rows2,
            rows2,
            P("patch", "var"),
            both,
            P("patch", "var"),
            both,
            P(),
            P(),
            P(),
            P("patch", "var"),
        ),
        out_specs=(
            P("patch", "var"),
            P("var", None, "patch"),
            P("var", None, "patch"),
            both,
            rows2,
            rows2,
            rows2,
            P("patch", "var"),
            both,
            P("patch", "var"),
            both,
        ),
        check_vma=False,
    )
```

```python
import functools
import math

import jax
import jax.numpy as jnp
from jax import lax
from jax.experimental import pallas as pl
from jax.experimental.pallas import tpu as pltpu
from jax.sharding import PartitionSpec as P

D = 1024
HEADS = 16
HS = D // HEADS
GROUP = 2048
F32 = jnp.float32
BF16 = jnp.bfloat16
NEG = -1e30
SCALE = 1.0 / math.sqrt(HS)


def exchange(x, axis):
    return lax.all_to_all(x, axis, 0, 0, tiled=True)


def flip(x, axis, bit):
    n = lax.axis_size(axis)
    return lax.ppermute(x, axis, [(i, i ^ bit) for i in range(n)])


def nt(a, b):
    return lax.dot_general(a, b, (((1,), (1,)), ((), ())), preferred_element_type=F32)


def tn(a, b):
    return lax.dot_general(a, b, (((0,), (0,)), ((), ())), preferred_element_type=F32)


def nn(a, b):
    return jnp.dot(a, b, preferred_element_type=F32)


def pad16(n):
    return -(-n // 16) * 16


def log2(n):
    return n.bit_length() - 1


def split(value):
    hi = value.astype(BF16).astype(F32)
    return hi, value - hi


def put_pair(ref, row, lanes, value):
    ref[row : row + 1, :lanes], ref[row : row + 1, lanes : 2 * lanes] = split(value)


def put_rows(ref, block, row, lanes, value):
    ref[block, row : row + 1, :lanes], ref[block, row + 1 : row + 2, :lanes] = split(value)


def reversed_bits(x, bits):
    out = 0
    for b in range(bits):
        out = out | (((x >> b) & 1) << (bits - 1 - b))
    return out


def rows_kernel(length_ref, lead_ref, cot_ref, out_ref, sums_ref):
    rows = cot_ref.shape[0]
    row0 = lax.axis_index("patch") * rows
    sample = row0 // GROUP
    pos = row0 % GROUP + lax.broadcasted_iota(jnp.int32, cot_ref.shape, 0)
    kept = jnp.where(pos < length_ref[sample], cot_ref[...].astype(F32), 0.0)
    out_ref[...] = kept.astype(BF16)
    total = jnp.sum(kept, axis=0, keepdims=True)
    sums_ref[0:1, :] = total
    sums_ref[1:2, :] = total * (lead_ref[sample].astype(F32) / 100.0)


def pack_kernel(eb, v_ref, k_ref, wq_ref, q_ref, e_ref, b_ref, l_ref, *refs):
    outs, tmp_ref = refs[:-1], refs[-1]
    cw = outs[0].shape[1]
    rl = v_ref.shape[0]
    _, vl, dp = e_ref.shape
    spare = 5 * vl
    j = lax.axis_index("var")
    q = jnp.broadcast_to(q_ref[...].astype(BF16), (16, rl))
    tmp_ref[...] = jnp.zeros_like(tmp_ref)
    for p in range(5):
        tmp_ref[p * vl : (p + 1) * vl, :dp] = e_ref[p]
    own = lax.broadcasted_iota(jnp.int32, (1, dp), 1) // rl == j
    for i, ref in enumerate((b_ref, l_ref)):
        tiled = jnp.concatenate([ref[...]] * (dp // rl), axis=1)
        tmp_ref[spare + 2 + i : spare + 3 + i, :dp] = jnp.where(own, tiled, 0.0)
    for k, out_ref in enumerate(outs):
        cols = pl.ds(pl.multiple_of((j ^ k) * cw, 128), cw)
        hi, lo = split(nn(q, wq_ref[:, cols].astype(BF16))[0:1])
        tmp_ref[spare : spare + 1, :] = hi
        tmp_ref[spare + 1 : spare + 2, :] = lo
        tmp_ref[eb : eb + rl, :] = v_ref[:, cols]
        tmp_ref[eb + rl : eb + 2 * rl, :] = k_ref[:, cols]
        out_ref[...] = tmp_ref[...].astype(BF16)


def place(ref, at, j, size, parts, lanes):
    if size % 16 == 0:
        for k, part in enumerate(parts):
            ref[pl.ds(pl.multiple_of((j ^ k) * size, size), size), lanes] = part
        return
    for s in range(len(parts)):
        value = parts[0]
        for k in range(1, len(parts)):
            value = jnp.where(j ^ k == s, parts[k], value)
        ref[s * size : (s + 1) * size, lanes] = value


def product_kernel(eb, vl, rl, dp, *refs):
    n = len(refs) - 6
    got, (sums_ref, out_ref, e_ref, kb_ref, w_ref, p_ref) = refs[:n], refs[n:]
    cw = got[0].shape[1]
    spare = 5 * vl
    p_id = lax.axis_index("patch")
    j = lax.axis_index("var")
    live = lax.broadcasted_iota(jnp.int32, (eb, dp), 0) < spare
    small = jnp.zeros((4, cw), F32)
    vs = []
    ks = []
    for k in range(n):
        g = got[k][...].astype(F32)
        small = small + g[spare : spare + 4]
        vs.append(g[eb : eb + rl])
        ks.append(g[eb + rl : eb + 2 * rl])
        e_ref[pl.ds(pl.multiple_of((j ^ k) * eb, eb), eb), :] = jnp.where(live, g[:eb, :dp], 0.0).astype(BF16)
    place(w_ref, 0, j, rl, vs, slice(0, cw))
    place(w_ref, 0, j, rl, ks, slice(cw, 2 * cw))
    w = w_ref[...].astype(BF16)
    kb_ref[...] = w[:, cw:]
    p_ref[...] = nn(e_ref[...], w)
    put_pair(p_ref, spare, cw, small[0:1] + small[1:2])
    put_pair(p_ref, spare + 1, cw, sums_ref[0:1])
    put_pair(p_ref, spare + 2, cw, sums_ref[1:2])
    per = cw // dp
    here = (lax.broadcasted_iota(jnp.int32, (1, cw), 1) // dp == p_id % per) & (p_id // per == j)
    for i in range(2):
        tiled = jnp.concatenate([small[2 + i : 3 + i, :dp]] * per, axis=1)
        p_ref[spare + 3 : spare + 4, i * cw : (i + 1) * cw] = jnp.where(here, tiled, 0.0)
    out_ref[...] = p_ref[...].astype(BF16)


def sum_kernel(vl, got_ref, out_ref):
    n_p, rc, lanes = got_ref.shape
    cw = lanes // 2
    total = got_ref[0].astype(F32)
    for s in range(1, n_p):
        total = total + got_ref[s].astype(F32)
    row = lax.axis_index("patch") * rc + lax.broadcasted_iota(jnp.int32, (rc, cw), 0)
    paired = (row >= 5 * vl) & (row < 5 * vl + 3)
    a, b = total[:, :cw], total[:, cw:]
    hi, lo = split(a + b)
    a, b = jnp.where(paired, hi, a).astype(BF16), jnp.where(paired, lo, b).astype(BF16)
    for s in range(n_p):
        out_ref[s, :, :cw] = a
        out_ref[s, :, cw:] = b


def forward_kernel(tile, eb, vk_ref, x_ref, avail_ref, att_ref, prob_ref, ef_ref, vw_ref, s_ref, vs_ref):
    nv, rows = x_ref.shape[1:]
    heads = prob_ref.shape[0]
    cw = att_ref.shape[0]
    n_j = vk_ref.shape[0] // eb
    vl = nv // n_j
    spare = 5 * vl
    j = lax.axis_index("var")
    for s in range(n_j):
        s_ref[s] = vk_ref[s * eb : (s + 1) * eb, :].astype(F32)
    q = (s_ref[0, spare : spare + 1, :cw] + s_ref[0, spare : spare + 1, cw:]) * SCALE
    for k in range(n_j):
        for p in range(5):
            vs_ref[p * nv + k * vl : p * nv + (k + 1) * vl, :] = s_ref[j ^ k, p * vl : (p + 1) * vl, :]
    vw_ref[...] = vs_ref[:, :cw].astype(BF16)
    for p in range(5):
        kq = vs_ref[p * nv : (p + 1) * nv, cw:] * q
        ef_ref[p] = jnp.concatenate(
            [jnp.sum(kq[:, h * HS : (h + 1) * HS], axis=1, keepdims=True) for h in range(heads)], axis=1
        )
    sample = lax.axis_index("patch") * rows // GROUP
    row = lax.broadcasted_iota(jnp.int32, (nv, nv), 0)
    shift = jnp.zeros((nv, nv), jnp.int32)
    for k in range(n_j):
        shift = jnp.where((row >= k * vl) & (row < (k + 1) * vl), ((j ^ k) - k) * vl, shift)
    same = row + shift == lax.broadcasted_iota(jnp.int32, (nv, nv), 1)
    flags = jnp.broadcast_to(avail_ref[pl.ds(sample, 1), :], (nv, nv))
    present = jnp.sum(jnp.where(same, flags.astype(F32), 0.0), axis=1, keepdims=True) > 0.5
    vw = [vw_ref[:, h * HS : (h + 1) * HS] for h in range(heads)]

    def step(i, carry):
        cols = pl.ds(pl.multiple_of(i * tile, tile), tile)
        xs = [x_ref[p, :, cols].astype(F32) for p in range(4)]
        for h in range(heads):
            s = jnp.broadcast_to(ef_ref[4, :, h : h + 1], (nv, tile))
            for p in range(4):
                s = s + ef_ref[p, :, h : h + 1] * xs[p]
            s = jnp.where(present, s, NEG)
            w = jnp.where(present, jnp.exp(s - jnp.max(s, axis=0, keepdims=True)), 0.0)
            prob = w / jnp.sum(w, axis=0, keepdims=True)
            prob_ref[h, :, cols] = prob
            a = jnp.concatenate([(prob * x).astype(BF16) for x in xs] + [prob.astype(BF16)], axis=0)
            att_ref[h * HS : (h + 1) * HS, cols] = tn(vw[h], a).astype(BF16)
        return carry

    lax.fori_loop(0, rows // tile, step, 0)


def partial_kernel(keep, lo_ref, hi_ref, rows_ref, out_ref, w_ref):
    half, dp, cw = lo_ref.shape
    p_id = lax.axis_index("patch")
    j = lax.axis_index("var")
    low = j & 1 if keep else 1 - (j & 1)
    per = cw // dp
    for b in range(out_ref.shape[0]):
        dest = 2 * ((j >> 1) ^ b) + low
        for t in range(per):
            block = reversed_bits((dest * per + t) ^ p_id, log2(2 * half))
            at = slice((b * per + t) * dp, (b * per + t + 1) * dp)

            @pl.when(block < half)
            def _(at=at, block=block):
                w_ref[at, :] = lo_ref[block]

            @pl.when(block >= half)
            def _(at=at, block=block):
                w_ref[at, :] = hi_ref[block - half]

    for b in range(out_ref.shape[0]):
        out_ref[b] = nt(w_ref[b * cw : (b + 1) * cw, :], rows_ref[...]).astype(BF16)


def head_rows(half, lo_ref, hi_ref, w_ref):
    p_id = lax.axis_index("patch")
    for q in range(2 * half):
        block = reversed_bits(q ^ p_id, log2(2 * half))
        dp = lo_ref.shape[1]
        at = slice(q * dp, (q + 1) * dp)

        @pl.when(block < half)
        def _(at=at, block=block):
            w_ref[at, :] = lo_ref[block]

        @pl.when(block >= half)
        def _(at=at, block=block):
            w_ref[at, :] = hi_ref[block - half]


def first_kernel(n, lo_ref, hi_ref, rows_ref, *refs):
    atts, (acc_ref, gwo_ref, w_ref) = refs[:n], refs[n:]
    cw = rows_ref.shape[1]
    j = lax.axis_index("var")
    head_rows(lo_ref.shape[0], lo_ref, hi_ref, w_ref)
    for k in range(n):
        w = w_ref[pl.ds(pl.multiple_of((j ^ k) * cw, cw), cw), :]
        term = tn(atts[k][...], w)
        acc_ref[...] = term if k == 0 else acc_ref[...] + term
        gwo_ref[k] = nn(atts[k][...], rows_ref[...]).astype(BF16)


def second_kernel(vl, n0, n_j, length_ref, lead_ref, lo_ref, hi_ref, rows_ref, acc_ref, gwo0_ref, vk_ref, plo_ref, phi_ref, *refs):
    atts, (out_ref, gwo_ref, w_ref, pos_ref) = refs[: n_j - n0], refs[n_j - n0 :]
    rows, cw = rows_ref.shape
    spare = 5 * vl
    base = pad16(spare) - 16
    row0 = lax.axis_index("patch") * rows
    sample = row0 // GROUP
    me = lax.axis_index("patch") // (GROUP // rows)
    j = lax.axis_index("var")
    head_rows(lo_ref.shape[0], lo_ref, hi_ref, w_ref)
    for k in range(n0):
        gwo_ref[j ^ k] = gwo0_ref[k]
    for k in range(n0, n_j):
        gwo_ref[j ^ k] = nn(atts[k - n0][...], rows_ref[...]).astype(BF16)
    half, per, _ = plo_ref.shape
    pos_ref[:half] = plo_ref[...]
    pos_ref[half:] = phi_ref[...]
    bl = vk_ref[base : base + 32, :].astype(F32)[spare - base + 3 : spare - base + 4]
    add = bl[:, :cw] + lead_ref[sample].astype(F32) / 100.0 * bl[:, cw:]
    for b in range(2 * half):
        at = slice(b * per, (b + 1) * per)
        total = acc_ref[at, :] + add + pos_ref[reversed_bits(b ^ me, log2(2 * half))].astype(F32)
        for k in range(n0, n_j):
            w = w_ref[pl.ds(pl.multiple_of((j ^ k) * cw, cw), cw), :]
            total = total + tn(atts[k - n0][:, at], w)
        pos = row0 % GROUP + b * per + lax.broadcasted_iota(jnp.int32, (per, cw), 0)
        out_ref[at, :] = jnp.where(pos < length_ref[sample], total, 0.0).astype(BF16)


def backward_kernel(tile, eb, n_j, x_ref, ef_ref, vw_ref, prob_ref, *refs):
    grads = refs[: -(n_j + 4)]
    gx_refs = refs[-(n_j + 4) : -4]
    z_ref, gv_ref, acc_ref, s_ref = refs[-4:]
    nv, rows = x_ref.shape[1:]
    heads = prob_ref.shape[0]
    vl = nv // n_j
    cw = gv_ref.shape[1]
    j = lax.axis_index("var")
    gv_ref[...] = jnp.zeros_like(gv_ref)
    acc_ref[...] = jnp.zeros_like(acc_ref)

    def step(i, carry):
        cols = pl.ds(pl.multiple_of(i * tile, tile), tile)
        xs = [x_ref[p, :, cols].astype(F32) for p in range(4)]
        gx = [jnp.zeros((nv, tile), F32) for _ in range(4)]
        for h in range(heads):
            hc = slice(h * HS, (h + 1) * HS)
            prob = prob_ref[h, :, cols]
            gh = grads[0][hc, cols].astype(F32)
            for ref in grads[1:]:
                gh = gh + ref[hc, cols].astype(F32)
            gh = gh.astype(BF16)
            g = nn(vw_ref[:, hc], gh)
            gp = [g[p * nv : (p + 1) * nv] for p in range(5)]
            gprob = gp[4]
            for p in range(4):
                gprob = gprob + xs[p] * gp[p]
            inner = jnp.sum(prob * gprob, axis=0, keepdims=True)
            gs = prob * (gprob - inner)
            for p in range(4):
                gx[p] = gx[p] + prob * gp[p] + ef_ref[p, :, h : h + 1] * gs
            a = jnp.concatenate([(prob * x).astype(BF16) for x in xs] + [prob.astype(BF16)], axis=0)
            gv_ref[:, hc] += nt(a, gh)
            for p in range(5):
                t = gs if p == 4 else gs * xs[p]
                part = t[:, :128]
                for k in range(1, tile // 128):
                    part = part + t[:, k * 128 : (k + 1) * 128]
                acc_ref[p * heads + h] += part
        for p in range(4):
            for k in range(n_j):
                gx_refs[k][p, :, cols] = gx[p][k * vl : (k + 1) * vl].astype(BF16)
        return carry

    lax.fori_loop(0, rows // tile, step, 0)
    s_ref[...] = jnp.zeros_like(s_ref)
    for p in range(5):
        gs = jnp.concatenate(
            [jnp.sum(acc_ref[p * heads + h], axis=1, keepdims=True) for h in range(heads)], axis=1
        )
        hi, lo = split(gs)
        pair = jnp.concatenate([hi, lo, jnp.zeros((nv, 128 - 2 * heads), F32)], axis=1)
        for k in range(n_j):
            at = slice(p * nv + k * vl, p * nv + (k + 1) * vl)
            s_ref[j ^ k, p * vl : (p + 1) * vl, :cw] = gv_ref[at, :]
            s_ref[j ^ k, p * vl : (p + 1) * vl, cw:] = pair[k * vl : (k + 1) * vl]
    for s in range(n_j):
        z_ref[s * eb : (s + 1) * eb, :] = s_ref[s].astype(BF16)


def sum_z_kernel(heads, got_ref, out_ref):
    n_p, rc, lanes = got_ref.shape
    cw = lanes - 128
    total = got_ref[0].astype(F32)
    for s in range(1, n_p):
        total = total + got_ref[s].astype(F32)
    main = total[:, :cw].astype(BF16)
    hi, lo = split(total[:, cw : cw + heads] + total[:, cw + heads : cw + 2 * heads])
    pair = jnp.concatenate([hi, lo, jnp.zeros((rc, 128 - 2 * heads), F32)], axis=1).astype(BF16)
    for s in range(n_p):
        out_ref[s, :, :cw] = main
        out_ref[s, :, cw:] = pair


def middle_kernel(eb, vl, z_ref, vk_ref, kb_ref, out_ref, s_ref):
    n_j = z_ref.shape[0] // eb
    dp, cw = kb_ref.shape
    heads = cw // HS
    spare = 5 * vl
    base = pad16(spare) - 16
    small = vk_ref[base : base + 32, :].astype(F32)[spare - base : spare - base + 3]
    small = small[:, :cw] + small[:, cw:]
    gq = [jnp.zeros((1, HS), F32) for _ in range(heads)]
    live = lax.broadcasted_iota(jnp.int32, (eb, 1), 0) < spare
    for s in range(n_j):
        z = z_ref[s * eb : (s + 1) * eb, :].astype(F32)
        s_ref[s] = z
        ke = jnp.where(live, vk_ref[s * eb : (s + 1) * eb, cw:].astype(F32), 0.0)
        gs = z[:, cw : cw + heads] + z[:, cw + heads : cw + 2 * heads]
        for h in range(heads):
            gq[h] = gq[h] + jnp.sum(ke[:, h * HS : (h + 1) * HS] * gs[:, h : h + 1], axis=0, keepdims=True)
    put_rows(s_ref, 0, spare, cw, jnp.concatenate(gq, axis=1) * SCALE)
    put_rows(s_ref, 0, spare + 2, cw, small[0:1])
    put_rows(s_ref, 1, spare, cw, small[1:2])
    put_rows(s_ref, 1, spare + 2, cw, small[2:3])
    head = lax.broadcasted_iota(jnp.int32, (8, cw), 0) == lax.broadcasted_iota(jnp.int32, (8, cw), 1) // HS
    hi, lo = split(jnp.where(head, small[0:1] * SCALE, 0.0))
    fold = nt(hi.astype(BF16), kb_ref[...]) + nt(lo.astype(BF16), kb_ref[...])
    s_ref[2, spare : spare + heads, :dp] = fold[:heads]
    for s in range(n_j):
        out_ref[s * eb : (s + 1) * eb, :] = s_ref[s].astype(BF16)


def own_rows(ref, index, size):
    if size % 8 == 0:
        return ref[pl.ds(pl.multiple_of(index * size, size), size), :]
    out = ref[:size, :]
    for k in range(1, ref.shape[0] // size):
        out = jnp.where(index == k, ref[k * size : (k + 1) * size, :], out)
    return out


def final_kernel(eb, vl, n_j, z_ref, e_ref, wq_ref, q_ref, *refs):
    vs = refs[:n_j]
    gwv_ref, gwk_ref, gwq_ref, gq_ref, ge_ref, gb_ref, gl_ref, s_ref, f_ref, v_ref = refs[n_j:]
    cw = z_ref.shape[2] - 128
    heads = cw // HS
    dp = v_ref.shape[0]
    rl = dp // n_j
    spare = 5 * vl
    p_id = lax.axis_index("patch")
    j = lax.axis_index("var")
    place(v_ref, 0, j, rl, [ref[...].astype(F32) for ref in vs], slice(0, D))
    own = pl.ds(pl.multiple_of(j * eb, eb), eb)
    base = pad16(spare) - 16
    at = spare - base
    gqs = []
    ge = jnp.zeros((eb, dp), F32)
    gb = []
    gl = []
    for s in range(n_j):
        s_ref[...] = tn(e_ref[...], z_ref[s])
        cols = slice(s * cw, (s + 1) * cw)
        picked = own_rows(s_ref, j, rl)
        gwv_ref[:, cols] = picked[:, :cw]
        pair = picked[:, cw:]
        gfold = (pair[:, :heads] + pair[:, heads : 2 * heads]) * SCALE
        rows0 = z_ref[s, base : base + 32, :].astype(F32)
        rows1 = z_ref[s, eb + base : eb + base + 32, :].astype(F32)
        rows2 = z_ref[s, 2 * eb + base : 2 * eb + base + 32, :].astype(F32)
        gqs.append(rows0[at : at + 1, :cw] + rows0[at + 1 : at + 2, :cw])
        qv = rows0[at + 2 : at + 3, :cw] + rows0[at + 3 : at + 4, :cw]
        gb.append(rows1[at : at + 1, :cw] + rows1[at + 1 : at + 2, :cw])
        gl.append(rows1[at + 2 : at + 3, :cw] + rows1[at + 3 : at + 4, :cw])
        gwk_ref[:, cols] = jnp.concatenate(
            [gfold[:, h : h + 1] * qv[:, h * HS : (h + 1) * HS] for h in range(heads)], axis=1
        )
        zo = z_ref[s, own, :]
        ge = ge + nt(zo[:, :cw], v_ref[:, cols].astype(BF16))
        gs = zo[:, cw : cw + heads].astype(F32) + zo[:, cw + heads : cw + 2 * heads].astype(F32)
        for h in range(heads):
            ge = ge + gs[:, h : h + 1] * rows2[at + h : at + h + 1, :dp]
    f_ref[...] = ge
    for p in range(5):
        ge_ref[p] = f_ref[p * vl : (p + 1) * vl, :]
    gq = jnp.concatenate(gqs, axis=1)
    gwq_ref[...] = q_ref[...].astype(BF16).astype(F32) * gq
    hi, lo = split(gq)
    wq = wq_ref[...].astype(BF16)
    both = jnp.concatenate([jnp.broadcast_to(hi, (8, D)), jnp.broadcast_to(lo, (8, D))], axis=0).astype(BF16)
    two = nt(both, wq)
    gq_ref[...] = two[0:1] + two[8:9]
    at_out = p_id * n_j + j
    for rows, ref in ((gb, gb_ref), (gl, gl_ref)):
        acc = jnp.zeros((1, rl), F32)
        for s in range(n_j):
            for g in range(cw // rl):
                acc = acc + jnp.where(at_out == s * (cw // rl) + g, rows[s][:, g * rl : (g + 1) * rl], 0.0)
        ref[...] = acc


def call(kernel, name, out_shape, args, scratch=(), flops=1 << 20, nbytes=1 << 20, smem=0, after=()):
    n = len(args)
    specs = [pl.BlockSpec(memory_space=pltpu.SMEM)] * smem + [pl.BlockSpec(memory_space=pltpu.VMEM)] * (n - smem)
    specs += [pl.BlockSpec(memory_space=pl.ANY)] * len(after)

    def body(*refs):
        kernel(*refs[:n], *refs[n + len(after) :])

    return pl.pallas_call(
        body,
        out_shape=out_shape,
        in_specs=specs,
        scratch_shapes=list(scratch),
        name=name,
        cost_estimate=pl.CostEstimate(flops=flops, bytes_accessed=nbytes, transcendentals=0),
    )(*args, *after)


def shape(dims, kind=F32):
    return jax.ShapeDtypeStruct(dims, kind)


def shards(pixels, embed, query, w_query, w_key, w_value, w_out, b_out, pos_embed, w_lead, avail, lengths, lead_hours, cotangent):
    n_p = lax.axis_size("patch")
    n_j = lax.axis_size("var")
    p_id = lax.axis_index("patch")
    vl, _, rows = pixels.shape
    nv = vl * n_j
    cw = w_out.shape[1]
    hl = cw // HS
    dp = embed.shape[2]
    rl = w_value.shape[0]
    eb = pad16(5 * vl + 4)
    nr = n_j * eb
    ch = pad16(eb + 2 * rl)
    rc = nr // n_p
    others = range(1, n_j)

    pack = call(
        functools.partial(pack_kernel, eb),
        "pack",
        [shape((ch, cw), BF16)] * n_j,
        (w_value, w_key, w_query, query[None, :], embed.transpose(1, 0, 2), b_out[None, :], w_lead[None, :]),
        [pltpu.VMEM((ch, cw), F32)],
    )
    got = [pack[0]] + [flip(pack[k], "var", k) for k in others]

    grad_rows, sums = call(
        rows_kernel, "rows", (shape((rows, cw), BF16), shape((2, cw))), (lengths, lead_hours, cotangent), smem=2
    )
    pix = [pixels] + [flip(pixels, "var", k) for k in others]
    pix = jnp.concatenate(pix, axis=0).transpose(1, 0, 2)

    part, e_all, k_blk = call(
        functools.partial(product_kernel, eb, vl, rl, dp),
        "product",
        (shape((nr, 2 * cw), BF16), shape((nr, dp), BF16), shape((dp, cw), BF16)),
        (*got, sums),
        [pltpu.VMEM((dp, 2 * cw), F32), pltpu.VMEM((nr, 2 * cw), F32)],
    )
    got2 = exchange(part, "patch").reshape(n_p, rc, 2 * cw)
    copies = call(functools.partial(sum_kernel, vl), "sum", shape((n_p, rc, 2 * cw), BF16), (got2,))
    vk = exchange(copies.reshape(nr, 2 * cw), "patch")

    wo_lo = w_out.astype(BF16)[None]
    wo_hi = flip(wo_lo, "patch", n_p // 2)
    bit = n_p // 4
    while bit:
        wo_lo = jnp.concatenate([wo_lo, wo_hi], axis=0)
        wo_hi = flip(wo_lo, "patch", bit)
        bit //= 2

    half = shape((n_j // 2, cw, rows), BF16)
    wide = [pltpu.VMEM((n_j // 2 * cw, cw), BF16)]
    send = call(
        functools.partial(partial_kernel, False), "partial_send", half, (wo_lo, wo_hi, grad_rows), wide, 1 << 29, after=(copies,)
    )
    sent = flip(send, "var", 1)
    keep = call(
        functools.partial(partial_kernel, True), "partial_keep", half, (wo_lo, wo_hi, grad_rows), wide, 1 << 29, after=(send,)
    )
    grads = [keep, sent]
    bit = 2
    while bit < n_j:
        grads = [g.reshape(g.shape[0] // 2, 2, cw, rows) for g in grads]
        send = sum(g[:, 1].astype(F32) for g in grads).astype(BF16)
        grads = [g[:, 0] for g in grads] + [flip(send, "var", bit)]
        bit *= 2
    grads = [g.reshape(cw, rows) for g in grads]

    att, prob, ef, vw = call(
        functools.partial(forward_kernel, 256, eb),
        "attention_forward",
        (shape((cw, rows), BF16), shape((hl, nv, rows)), shape((5, nv, hl)), shape((5 * nv, cw), BF16)),
        (vk, pix, avail),
        [pltpu.VMEM((n_j, eb, 2 * cw), F32), pltpu.VMEM((5 * nv, 2 * cw), F32)],
        hl * nv * rows * 800,
        3 << 20,
    )

    *gx, z = call(
        functools.partial(backward_kernel, 256, eb, n_j),
        "attention_backward",
        [shape((4, vl, rows), BF16)] * n_j + [shape((nr, cw + 128), BF16)],
        (pix, ef, vw, prob, *grads),
        [pltpu.VMEM((5 * nv, cw), F32), pltpu.VMEM((5 * hl, nv, 128), F32), pltpu.VMEM((n_j, eb, cw + 128), F32)],
        hl * nv * rows * 1600,
        3 << 20,
    )

    gx = [gx[0]] + [flip(gx[k], "var", k) for k in others]
    grad_pixels = sum(g.astype(F32) for g in gx).astype(BF16).transpose(1, 0, 2)

    blocks = [att]
    bit = 1
    while bit < n_j:
        blocks = blocks + [flip(b, "var", bit) for b in blocks]
        bit *= 2
    n0 = max(n_j // 2, 1)
    acc, gwo0 = call(
        functools.partial(first_kernel, n0),
        "out_first",
        (shape((rows, cw)), shape((n0, cw, cw), BF16)),
        (wo_lo, wo_hi, grad_rows, *blocks[:n0]),
        [pltpu.VMEM((D, cw), BF16)],
        1 << 30,
        2 << 20,
        after=(z,),
    )

    parts = GROUP // rows
    owners = n_p // parts
    per = pos_embed.shape[0]
    there = [(k * owners + i, parts * i + k) for i in range(owners) for k in range(parts)]
    back = [(b, a) for a, b in there]
    me = p_id // parts
    pos_lo = lax.ppermute(pos_embed.astype(BF16), "patch", there)[None]
    pos_hi = flip(pos_lo, "patch", n_p // 2)
    bit = n_p // 4
    while bit >= parts:
        pos_lo = jnp.concatenate([pos_lo, pos_hi], axis=0)
        pos_hi = flip(pos_lo, "patch", bit)
        bit //= 2
    gpos = grad_rows.reshape(owners, per, cw)
    bit = 1
    while bit < owners:
        pair = gpos.reshape(gpos.shape[0] // 2, 2, per, cw)
        mine = (me // bit) % 2
        send = lax.dynamic_index_in_dim(pair, 1 - mine, 1, False)
        keep = lax.dynamic_index_in_dim(pair, mine, 1, False)
        gpos = (keep.astype(F32) + flip(send, "patch", bit * parts).astype(F32)).astype(BF16)
        bit *= 2
    grad_pos = lax.ppermute(gpos.reshape(per, cw), "patch", back).astype(F32)

    mixed, gwo = call(
        functools.partial(second_kernel, vl, n0, n_j),
        "out_second",
        (shape((rows, cw), BF16), shape((n_j, cw, cw), BF16)),
        (lengths, lead_hours, wo_lo, wo_hi, grad_rows, acc, gwo0, vk, pos_lo, pos_hi, *blocks[n0:]),
        [pltpu.VMEM((D, cw), BF16), pltpu.VMEM((owners, per, cw), BF16)],
        1 << 30,
        2 << 20,
        smem=2,
    )

    got3 = exchange(z, "patch").reshape(n_p, rc, cw + 128)
    copies = call(functools.partial(sum_z_kernel, hl), "sum_z", shape((n_p, rc, cw + 128), BF16), (got3,))
    z = exchange(copies.reshape(nr, cw + 128), "patch")
    z = call(
        functools.partial(middle_kernel, eb, vl),
        "middle",
        shape((nr, cw + 128), BF16),
        (z, vk, k_blk),
        [pltpu.VMEM((n_j, eb, cw + 128), F32)],
    )
    gwo, z = lax.optimization_barrier((gwo, z))
    gwo = exchange(gwo.reshape(D, cw), "patch").reshape(n_p, dp, cw)
    grad_w_out = jnp.sum(gwo.astype(F32), axis=0)
    allz = lax.all_gather(z, "var", axis=0, tiled=False)
    v_low = w_value.astype(BF16)
    v_rows = [v_low] + [flip(v_low, "var", k) for k in others]
    gwv, gwk, gwq, gq, ge, gb, gl = call(
        functools.partial(final_kernel, eb, vl, n_j),
        "final",
        (
            shape((rl, D)),
            shape((rl, D)),
            shape((rl, D)),
            shape((1, rl)),
            shape((5, vl, dp)),
            shape((1, rl)),
            shape((1, rl)),
        ),
        (allz, e_all, w_query, query[:, None], *v_rows),
        [pltpu.VMEM((dp, cw + 128), F32), pltpu.VMEM((eb, dp), F32), pltpu.VMEM((dp, D), F32)],
    )
    return (
        mixed,
        grad_pixels,
        ge.transpose(1, 0, 2),
        gq.reshape(rl),
        gwq,
        gwk,
        gwv,
        grad_w_out,
        gb.reshape(rl),
        grad_pos,
        gl.reshape(rl),
    )


def solution(mesh):
    both = P(("patch", "var"))
    rows2 = P(("patch", "var"), None)
    return jax.shard_map(
        shards,
        mesh=mesh,
        in_specs=(
            P("var", None, "patch"),
            P("var", None, "patch"),
            both,
            rows2,
            rows2,
            rows2,
            P("patch", "var"),
            both,
            P("patch", "var"),
            both,
            P(),
            P(),
            P(),
            P("patch", "var"),
        ),
        out_specs=(
            P("patch", "var"),
            P("var", None, "patch"),
            P("var", None, "patch"),
            both,
            rows2,
            rows2,
            rows2,
            P("patch", "var"),
            both,
            P("patch", "var"),
            both,
        ),
        check_vma=False,
    )
```

```python
import functools
import math

import jax
import jax.numpy as jnp
from jax import lax
from jax.experimental import pallas as pl
from jax.experimental.pallas import tpu as pltpu
from jax.sharding import PartitionSpec as P

D = 1024
HEADS = 16
HS = D // HEADS
GROUP = 2048
F32 = jnp.float32
BF16 = jnp.bfloat16
NEG = -1e30
SCALE = 1.0 / math.sqrt(HS)


def exchange(x, axis):
    return lax.all_to_all(x, axis, 0, 0, tiled=True)


def flip(x, axis, bit):
    n = lax.axis_size(axis)
    return lax.ppermute(x, axis, [(i, i ^ bit) for i in range(n)])


def gate(x, after):
    return lax.optimization_barrier((x, after))[0]


def gather_var(x, last):
    n = lax.axis_size("var")
    blocks = {0: x}
    bit = n // 2
    while bit:
        for k, block in list(blocks.items()):
            blocks[k | bit] = flip(last(block) if bit == 1 and k else block, "var", bit)
        bit //= 2
    return [blocks[k] for k in range(n)]


def halve(x, bit, step):
    pair = x.reshape(x.shape[0] // 2, 2, *x.shape[1:])
    send = lax.dynamic_index_in_dim(pair, 1 - bit, 1, False)
    keep = lax.dynamic_index_in_dim(pair, bit, 1, False)
    return (keep.astype(F32) + flip(send, "patch", step).astype(F32)).astype(BF16)


def nt(a, b):
    return lax.dot_general(a, b, (((1,), (1,)), ((), ())), preferred_element_type=F32)


def tn(a, b):
    return lax.dot_general(a, b, (((0,), (0,)), ((), ())), preferred_element_type=F32)


def nn(a, b):
    return jnp.dot(a, b, preferred_element_type=F32)


def pad16(n):
    return -(-n // 16) * 16


def split(value):
    hi = value.astype(BF16).astype(F32)
    return hi, value - hi


def put_pair(ref, row, lanes, value):
    ref[row : row + 1, :lanes], ref[row : row + 1, lanes : 2 * lanes] = split(value)


def put_rows(ref, block, row, lanes, value):
    ref[block, row : row + 1, :lanes], ref[block, row + 1 : row + 2, :lanes] = split(value)


def rows_kernel(length_ref, lead_ref, cot_ref, pix_ref, out_ref, sums_ref, tmp_ref):
    rows, cw = cot_ref.shape
    vl = pix_ref.shape[0]
    vp = tmp_ref.shape[0] // 4
    row0 = lax.axis_index("patch") * rows
    sample = row0 // GROUP
    pos = row0 % GROUP + lax.broadcasted_iota(jnp.int32, cot_ref.shape, 0)
    kept = jnp.where(pos < length_ref[sample], cot_ref[...].astype(F32), 0.0)
    out_ref[:rows] = kept.astype(BF16)
    total = jnp.sum(kept, axis=0, keepdims=True)
    sums_ref[0:1, :] = total
    sums_ref[1:2, :] = total * (lead_ref[sample].astype(F32) / 100.0)
    tmp_ref[...] = jnp.zeros_like(tmp_ref)
    for v in range(vl):
        x = pix_ref[v].astype(F32)
        for p in range(4):
            tmp_ref[p * vp + v : p * vp + v + 1, :] = x[p : p + 1]
    for b in range(rows // cw):
        out_ref[rows + b * 4 * vp : rows + (b + 1) * 4 * vp, :] = tmp_ref[:, b * cw : (b + 1) * cw].astype(BF16)


def pack_kernel(eb, v_ref, k_ref, wq_ref, q_ref, e_ref, b_ref, l_ref, *refs):
    outs, tmp_ref = refs[:-1], refs[-1]
    cw = outs[0].shape[1]
    rl = v_ref.shape[0]
    _, vl, dp = e_ref.shape
    spare = 5 * vl
    j = lax.axis_index("var")
    q = jnp.broadcast_to(q_ref[...].astype(BF16), (16, rl))
    tmp_ref[...] = jnp.zeros_like(tmp_ref)
    for p in range(5):
        tmp_ref[p * vl : (p + 1) * vl, :dp] = e_ref[p]
    own = lax.broadcasted_iota(jnp.int32, (1, dp), 1) // rl == j
    for i, ref in enumerate((b_ref, l_ref)):
        tiled = jnp.concatenate([ref[...]] * (dp // rl), axis=1)
        tmp_ref[spare + 2 + i : spare + 3 + i, :dp] = jnp.where(own, tiled, 0.0)
    for k, out_ref in enumerate(outs):
        cols = pl.ds(pl.multiple_of((j ^ k) * cw, 128), cw)
        hi, lo = split(nn(q, wq_ref[:, cols].astype(BF16))[0:1])
        tmp_ref[spare : spare + 1, :] = hi
        tmp_ref[spare + 1 : spare + 2, :] = lo
        tmp_ref[eb : eb + rl, :] = k_ref[:, cols]
        for m in range(len(outs)):
            at = eb + (m + 1) * rl
            tmp_ref[at : at + rl, :] = v_ref[:, pl.ds(pl.multiple_of((j ^ k ^ m) * cw, 128), cw)]
        out_ref[...] = tmp_ref[...].astype(BF16)


def place(ref, at, j, size, parts, lanes):
    if size % 16 == 0:
        for k, part in enumerate(parts):
            ref[pl.ds(pl.multiple_of((j ^ k) * size, size), size), lanes] = part
        return
    for s in range(len(parts)):
        value = parts[0]
        for k in range(1, len(parts)):
            value = jnp.where(j ^ k == s, parts[k], value)
        ref[s * size : (s + 1) * size, lanes] = value


def product_kernel(eb, vl, rl, dp, *refs):
    n = len(refs) - 7
    got, (sums_ref, out_ref, e_ref, kb_ref, vb_ref, w_ref, p_ref) = refs[:n], refs[n:]
    cw = got[0].shape[1]
    spare = 5 * vl
    p_id = lax.axis_index("patch")
    j = lax.axis_index("var")
    live = lax.broadcasted_iota(jnp.int32, (eb, dp), 0) < spare
    small = jnp.zeros((4, cw), F32)
    gs = [got[k][...].astype(F32) for k in range(n)]
    for k in range(n):
        small = small + gs[k][spare : spare + 4]
        e_ref[pl.ds(pl.multiple_of((j ^ k) * eb, eb), eb), :] = jnp.where(live, gs[k][:eb, :dp], 0.0).astype(BF16)
    for m in range(n + 1):
        at = eb + m * rl
        place(w_ref, 0, j, rl, [g[at : at + rl] for g in gs], slice(m * cw, (m + 1) * cw))
    vb_ref[...] = w_ref[:, cw:].astype(BF16)
    w = jnp.concatenate([vb_ref[:, :cw], w_ref[:, :cw].astype(BF16)], axis=1)
    kb_ref[...] = w[:, cw:]
    p_ref[...] = nn(e_ref[...], w)
    put_pair(p_ref, spare, cw, small[0:1] + small[1:2])
    put_pair(p_ref, spare + 1, cw, sums_ref[0:1])
    put_pair(p_ref, spare + 2, cw, sums_ref[1:2])
    per = cw // dp
    here = (lax.broadcasted_iota(jnp.int32, (1, cw), 1) // dp == p_id % per) & (p_id // per == j)
    for i in range(2):
        tiled = jnp.concatenate([small[2 + i : 3 + i, :dp]] * per, axis=1)
        p_ref[spare + 3 : spare + 4, i * cw : (i + 1) * cw] = jnp.where(here, tiled, 0.0)
    out_ref[...] = p_ref[...].astype(BF16)


def sum_kernel(vl, got_ref, out_ref):
    n_p, rc, lanes = got_ref.shape
    cw = lanes // 2
    total = got_ref[0].astype(F32)
    for s in range(1, n_p):
        total = total + got_ref[s].astype(F32)
    row = lax.axis_index("patch") * rc + lax.broadcasted_iota(jnp.int32, (rc, cw), 0)
    paired = (row >= 5 * vl) & (row < 5 * vl + 3)
    a, b = total[:, :cw], total[:, cw:]
    hi, lo = split(a + b)
    a, b = jnp.where(paired, hi, a).astype(BF16), jnp.where(paired, lo, b).astype(BF16)
    for s in range(n_p):
        out_ref[s, :, :cw] = a
        out_ref[s, :, cw:] = b


def forward_kernel(tile, eb, vk_ref, x_ref, avail_ref, att_ref, prob_ref, ef_ref, vw_ref, s_ref, vs_ref):
    nv, rows = x_ref.shape[1:]
    heads = prob_ref.shape[0]
    cw = att_ref.shape[0]
    n_j = vk_ref.shape[0] // eb
    vl = nv // n_j
    spare = 5 * vl
    j = lax.axis_index("var")
    for s in range(n_j):
        s_ref[s] = vk_ref[s * eb : (s + 1) * eb, :].astype(F32)
    q = (s_ref[0, spare : spare + 1, :cw] + s_ref[0, spare : spare + 1, cw:]) * SCALE
    for k in range(n_j):
        for p in range(5):
            vs_ref[p * nv + k * vl : p * nv + (k + 1) * vl, :] = s_ref[j ^ k, p * vl : (p + 1) * vl, :]
    vw_ref[...] = vs_ref[:, :cw].astype(BF16)
    for p in range(5):
        kq = vs_ref[p * nv : (p + 1) * nv, cw:] * q
        ef_ref[p] = jnp.concatenate(
            [jnp.sum(kq[:, h * HS : (h + 1) * HS], axis=1, keepdims=True) for h in range(heads)], axis=1
        )
    sample = lax.axis_index("patch") * rows // GROUP
    row = lax.broadcasted_iota(jnp.int32, (nv, nv), 0)
    shift = jnp.zeros((nv, nv), jnp.int32)
    for k in range(n_j):
        shift = jnp.where((row >= k * vl) & (row < (k + 1) * vl), ((j ^ k) - k) * vl, shift)
    same = row + shift == lax.broadcasted_iota(jnp.int32, (nv, nv), 1)
    flags = jnp.broadcast_to(avail_ref[pl.ds(sample, 1), :], (nv, nv))
    present = jnp.sum(jnp.where(same, flags.astype(F32), 0.0), axis=1, keepdims=True) > 0.5
    vw = [vw_ref[:, h * HS : (h + 1) * HS] for h in range(heads)]

    def step(i, carry):
        cols = pl.ds(pl.multiple_of(i * tile, tile), tile)
        xs = [x_ref[p, :, cols].astype(F32) for p in range(4)]
        for h in range(heads):
            s = jnp.broadcast_to(ef_ref[4, :, h : h + 1], (nv, tile))
            for p in range(4):
                s = s + ef_ref[p, :, h : h + 1] * xs[p]
            s = jnp.where(present, s, NEG)
            w = jnp.where(present, jnp.exp(s - jnp.max(s, axis=0, keepdims=True)), 0.0)
            prob = w / jnp.sum(w, axis=0, keepdims=True)
            prob_ref[h, :, cols] = prob
            a = jnp.concatenate([(prob * x).astype(BF16) for x in xs] + [prob.astype(BF16)], axis=0)
            att_ref[h * HS : (h + 1) * HS, cols] = tn(vw[h], a).astype(BF16)
        return carry

    lax.fori_loop(0, rows // tile, step, 0)


def reversed_bits(x, bits):
    out = 0
    for b in range(bits):
        out = out | (((x >> b) & 1) << (bits - 1 - b))
    return out


def pixel_kernel(vl, cw, *refs):
    bufs, (out_ref, x_ref) = refs[:-2], refs[-2:]
    rows = out_ref.shape[2]
    vp = (bufs[0].shape[0] - rows) // (4 * (rows // cw))
    for k, buf in enumerate(bufs):
        for b in range(rows // cw):
            at = rows + b * 4 * vp
            x = buf[at : at + 4 * vp, :].astype(F32)
            for p in range(4):
                x_ref[p, k * vl : (k + 1) * vl, b * cw : (b + 1) * cw] = x[p * vp : p * vp + vl]
    for p in range(4):
        out_ref[p] = x_ref[p].astype(BF16)


def weight_kernel(n_j, vl, lo_ref, hi_ref, *refs):
    bufs, (full_ref, *chunks), (pix_ref, x_ref) = refs[:n_j], refs[n_j : 2 * n_j], refs[2 * n_j :]
    pixel_kernel(vl, full_ref.shape[1], *bufs, pix_ref, x_ref)
    half, dp, cw = lo_ref.shape
    p_id = lax.axis_index("patch")
    j = lax.axis_index("var")
    for q in range(2 * half):
        block = reversed_bits(q ^ p_id, (2 * half).bit_length() - 1)
        at = slice(q * dp, (q + 1) * dp)

        @pl.when(block < half)
        def _(at=at, block=block):
            full_ref[at, :] = lo_ref[block]

        @pl.when(block >= half)
        def _(at=at, block=block):
            full_ref[at, :] = hi_ref[block - half]

    for k, ref in enumerate(chunks):
        ref[...] = full_ref[pl.ds(pl.multiple_of((j ^ (k + 1)) * cw, cw), cw), :]


def grad_kernel(n_j, full_ref, *refs):
    ws, cots, (out_ref,) = refs[: n_j - 1], refs[n_j - 1 : -1], refs[-1:]
    cw, rows = out_ref.shape
    j = lax.axis_index("var")
    own = full_ref[pl.ds(pl.multiple_of(j * cw, cw), cw), :]
    tile = 256
    for i in range(rows // tile):
        at = slice(i * tile, (i + 1) * tile)
        total = nt(own, cots[0][at, :])
        for k in range(1, n_j):
            total = total + nt(ws[k - 1][...], cots[k][at, :])
        out_ref[:, at] = total.astype(BF16)


def weight_grad_kernel(n_j, buf_ref, *refs):
    atts, (send_ref, keep_ref, tmp_ref) = refs[:n_j], refs[n_j:]
    cw, rows = atts[0].shape
    half, dp, _ = send_ref.shape
    j = lax.axis_index("var")
    per = cw // dp
    for k in range(n_j):
        g = nn(atts[k][...], buf_ref[:rows, :]).astype(BF16)
        for t in range(per):
            tmp_ref[(j ^ k) * per + t] = g[t * dp : (t + 1) * dp]
    own = lax.axis_index("patch") & 1
    for b in range(half):
        send_ref[b] = tmp_ref[2 * b + 1 - own]
        keep_ref[b] = tmp_ref[2 * b + own]


def halve_kernel(bit, keep_ref, got_ref, send_ref, next_ref):
    own = jnp.where(lax.axis_index("patch") & bit, 1, 0)
    for b in range(send_ref.shape[0]):
        for ref, i in ((send_ref, 1 - own), (next_ref, own)):
            ref[b] = (keep_ref[2 * b + i].astype(F32) + got_ref[2 * b + i].astype(F32)).astype(BF16)


def mixed_kernel(vl, n_j, length_ref, lead_ref, w_ref, vk_ref, plo_ref, phi_ref, *refs):
    atts, (out_ref, pos_ref) = refs[:n_j], refs[n_j:]
    rows, cw = out_ref.shape
    spare = 5 * vl
    base = pad16(spare) - 16
    row0 = lax.axis_index("patch") * rows
    sample = row0 // GROUP
    me = lax.axis_index("patch") // (GROUP // rows)
    j = lax.axis_index("var")
    half, per, _ = plo_ref.shape
    pos_ref[:half] = plo_ref[...]
    pos_ref[half:] = phi_ref[...]
    bl = vk_ref[base : base + 32, :].astype(F32)[spare - base + 3 : spare - base + 4]
    add = bl[:, :cw] + lead_ref[sample].astype(F32) / 100.0 * bl[:, cw:]
    for b in range(2 * half):
        at = slice(b * per, (b + 1) * per)
        total = add + pos_ref[reversed_bits(b ^ me, (2 * half).bit_length() - 1)].astype(F32)
        for k in range(n_j):
            w = w_ref[pl.ds(pl.multiple_of((j ^ k) * cw, cw), cw), :]
            total = total + tn(atts[k][:, at], w)
        pos = row0 % GROUP + b * per + lax.broadcasted_iota(jnp.int32, (per, cw), 0)
        out_ref[at, :] = jnp.where(pos < length_ref[sample], total, 0.0).astype(BF16)


def backward_kernel(tile, eb, n_j, vp, x_ref, ef_ref, vw_ref, prob_ref, grad_ref, *refs):
    outs, (z_ref, gv_ref, acc_ref, s_ref) = refs[:-4], refs[-4:]
    nv, rows = x_ref.shape[1:]
    heads = prob_ref.shape[0]
    vl = nv // n_j
    cw = gv_ref.shape[1]
    j = lax.axis_index("var")
    gv_ref[...] = jnp.zeros_like(gv_ref)
    acc_ref[...] = jnp.zeros_like(acc_ref)
    blank = jnp.zeros((vp - vl, tile), F32)

    def step(i, carry):
        cols = pl.ds(pl.multiple_of(i * tile, tile), tile)
        xs = [x_ref[p, :, cols].astype(F32) for p in range(4)]
        gx = [jnp.zeros((nv, tile), F32) for _ in range(4)]
        for h in range(heads):
            hc = slice(h * HS, (h + 1) * HS)
            prob = prob_ref[h, :, cols]
            gh = grad_ref[hc, cols]
            g = nn(vw_ref[:, hc], gh)
            gp = [g[p * nv : (p + 1) * nv] for p in range(5)]
            gprob = gp[4]
            for p in range(4):
                gprob = gprob + xs[p] * gp[p]
            inner = jnp.sum(prob * gprob, axis=0, keepdims=True)
            gs = prob * (gprob - inner)
            for p in range(4):
                gx[p] = gx[p] + prob * gp[p] + ef_ref[p, :, h : h + 1] * gs
            a = jnp.concatenate([(prob * x).astype(BF16) for x in xs] + [prob.astype(BF16)], axis=0)
            gv_ref[:, hc] += nt(a, gh)
            for p in range(5):
                t = gs if p == 4 else gs * xs[p]
                part = t[:, :128]
                for k in range(1, tile // 128):
                    part = part + t[:, k * 128 : (k + 1) * 128]
                acc_ref[p * heads + h] += part
        for k, ref in enumerate(outs):
            piece = jnp.concatenate([t for p in range(4) for t in (gx[p][k * vl : (k + 1) * vl], blank)], axis=0)
            ref[:, cols] = piece.astype(BF16)
        return carry

    lax.fori_loop(0, rows // tile, step, 0)
    s_ref[...] = jnp.zeros_like(s_ref)
    for p in range(5):
        gs = jnp.concatenate(
            [jnp.sum(acc_ref[p * heads + h], axis=1, keepdims=True) for h in range(heads)], axis=1
        )
        hi, lo = split(gs)
        pair = jnp.concatenate([hi, lo, jnp.zeros((nv, 128 - 2 * heads), F32)], axis=1)
        for k in range(n_j):
            at = slice(p * nv + k * vl, p * nv + (k + 1) * vl)
            s_ref[j ^ k, p * vl : (p + 1) * vl, :cw] = gv_ref[at, :]
            s_ref[j ^ k, p * vl : (p + 1) * vl, cw:] = pair[k * vl : (k + 1) * vl]
    for s in range(n_j):
        z_ref[s * eb : (s + 1) * eb, :] = s_ref[s].astype(BF16)


def sum_z_kernel(heads, got_ref, out_ref):
    n_p, rc, lanes = got_ref.shape
    cw = lanes - 128
    total = got_ref[0].astype(F32)
    for s in range(1, n_p):
        total = total + got_ref[s].astype(F32)
    main = total[:, :cw].astype(BF16)
    hi, lo = split(total[:, cw : cw + heads] + total[:, cw + heads : cw + 2 * heads])
    pair = jnp.concatenate([hi, lo, jnp.zeros((rc, 128 - 2 * heads), F32)], axis=1).astype(BF16)
    for s in range(n_p):
        out_ref[s, :, :cw] = main
        out_ref[s, :, cw:] = pair


def middle_kernel(eb, vl, n_j, z_ref, vk_ref, kb_ref, e_ref, v_ref, *refs):
    chunks, (g_ref, ge_ref, s_ref) = refs[:n_j], refs[n_j:]
    dp, cw = kb_ref.shape
    rl = dp // n_j
    heads = cw // HS
    spare = 5 * vl
    half = eb // 2
    j = lax.axis_index("var")
    base = pad16(spare) - 16
    small = vk_ref[base : base + 32, :].astype(F32)[spare - base : spare - base + 3]
    small = small[:, :cw] + small[:, cw:]
    qvec = small[0:1] * SCALE
    g = tn(e_ref[...], z_ref[...])
    gfold = g[:, cw : cw + heads] + g[:, cw + heads : cw + 2 * heads]
    g_ref[:, :cw] = g[:, :cw]
    g_ref[:, cw:] = jnp.concatenate(
        [gfold[:, h : h + 1] * qvec[:, h * HS : (h + 1) * HS] for h in range(heads)], axis=1
    )
    pair = z_ref[:, cw:].astype(F32)
    gs = pair[:, :heads] + pair[:, heads : 2 * heads]
    live = lax.broadcasted_iota(jnp.int32, (n_j * eb, 1), 0) % eb < spare
    ke = jnp.where(live, vk_ref[:, cw:].astype(F32), 0.0)
    gq = jnp.concatenate(
        [jnp.sum(ke[:, h * HS : (h + 1) * HS] * gs[:, h : h + 1], axis=0, keepdims=True) for h in range(heads)], axis=1
    ) * SCALE
    head = lax.broadcasted_iota(jnp.int32, (8, cw), 0) == lax.broadcasted_iota(jnp.int32, (8, cw), 1) // HS
    hi, lo = split(jnp.where(head, qvec, 0.0))
    fold = nt(hi.astype(BF16), kb_ref[...]) + nt(lo.astype(BF16), kb_ref[...])
    ge = nt(z_ref[:, :cw], v_ref[:, :cw])
    for h in range(heads):
        ge = ge + gs[:, h : h + 1] * fold[h : h + 1, :]
    ge_ref[...] = ge
    s_ref[...] = jnp.zeros_like(s_ref)
    at = 2 * rl + half
    for i, row in enumerate((gq, small[1:2], small[2:3])):
        s_ref[at + 2 * i : at + 2 * i + 1, :], s_ref[at + 2 * i + 1 : at + 2 * i + 2, :] = split(row)
    for k in range(n_j):
        rows = own_rows(g_ref, j ^ k, rl)
        s_ref[:rl, :] = rows[:, :cw]
        s_ref[rl : 2 * rl, :] = rows[:, cw:]
        block = ge_ref[pl.ds(pl.multiple_of((j ^ k) * eb, eb), eb), :]
        s_ref[2 * rl : 2 * rl + half, :dp] = block[:half]
        s_ref[2 * rl : 2 * rl + half, cw // 2 : cw // 2 + dp] = block[half:]
        chunks[k][...] = s_ref[...].astype(BF16)


def own_rows(ref, index, size):
    if size % 8 == 0:
        return ref[pl.ds(pl.multiple_of(index * size, size), size), :]
    out = ref[:size, :]
    for k in range(1, ref.shape[0] // size):
        out = jnp.where(index == k, ref[k * size : (k + 1) * size, :], out)
    return out


def final_kernel(eb, vl, rl, dp, n_j, wq_ref, q_ref, *refs):
    chunks, (gwv_ref, gwk_ref, gwq_ref, gq_ref, ge_ref, gb_ref, gl_ref, f_ref, r_ref) = refs[:n_j], refs[n_j:]
    cw = chunks[0].shape[1]
    half = eb // 2
    j = lax.axis_index("var")
    at_out = lax.axis_index("patch") * n_j + j
    at = 2 * rl + half
    ge = jnp.zeros((half, cw), F32)
    gb = jnp.zeros((1, rl), F32)
    gl = jnp.zeros((1, rl), F32)
    for k in range(n_j):
        c = chunks[k][...].astype(F32)
        cols = pl.ds(pl.multiple_of((j ^ k) * cw, 128), cw)
        gwv_ref[:, cols] = c[:rl]
        gwk_ref[:, cols] = c[rl : 2 * rl]
        ge = ge + c[2 * rl : at]
        r_ref[0:1, cols] = c[at : at + 1] + c[at + 1 : at + 2]
        bias = c[at + 2 : at + 3] + c[at + 3 : at + 4]
        lead = c[at + 4 : at + 5] + c[at + 5 : at + 6]
        for g in range(cw // rl):
            here = at_out == (j ^ k) * (cw // rl) + g
            gb = gb + jnp.where(here, bias[:, g * rl : (g + 1) * rl], 0.0)
            gl = gl + jnp.where(here, lead[:, g * rl : (g + 1) * rl], 0.0)
    f_ref[:half, :] = ge[:, :dp]
    f_ref[half:, :] = ge[:, cw // 2 : cw // 2 + dp]
    for p in range(5):
        ge_ref[p] = f_ref[p * vl : (p + 1) * vl, :]
    gq = r_ref[0:1, :]
    gwq_ref[...] = q_ref[...].astype(BF16).astype(F32) * gq
    hi, lo = split(gq)
    wq = wq_ref[...].astype(BF16)
    both = jnp.concatenate([jnp.broadcast_to(hi, (8, D)), jnp.broadcast_to(lo, (8, D))], axis=0).astype(BF16)
    two = nt(both, wq)
    gq_ref[...] = two[0:1] + two[8:9]
    gb_ref[...] = gb
    gl_ref[...] = gl


def call(kernel, name, out_shape, args, scratch=(), us=1.0, smem=0, after=(), first=False, spill=(), hbm=0):
    n = len(args)
    in_vmem = pl.BlockSpec(memory_space=pltpu.VMEM)
    specs = [pl.BlockSpec(memory_space=pltpu.SMEM)] * smem + [pl.BlockSpec() if first else in_vmem] * (n - smem)
    specs[n - hbm :] = [pl.BlockSpec(memory_space=pl.ANY)] * hbm
    specs += [pl.BlockSpec(memory_space=pl.ANY)] * len(after)
    shapes = list(out_shape) if isinstance(out_shape, (list, tuple)) else [out_shape]
    outs = [pl.BlockSpec(memory_space=pltpu.HBM) if i in spill else in_vmem for i in range(len(shapes))]
    extra = [pltpu.VMEM(shapes[i].shape, shapes[i].dtype) for i in spill]
    if spill:
        extra.append(pltpu.SemaphoreType.DMA((len(spill),)))

    def body(*refs):
        ins, rest = refs[:n], refs[n + len(after) :]
        results, rest = list(rest[: len(shapes)]), rest[len(shapes) :]
        local, sems = rest[: len(spill)], rest[len(extra) - 1 : len(extra)]
        rest = rest[len(extra) :]
        copies = []
        for c, i in enumerate(spill):
            copies.append(pltpu.make_async_copy(local[c], results[i], sems[0].at[c]))
            results[i] = local[c]
        kernel(*ins, *results, *rest)
        for copy in copies:
            copy.start()
        for copy in copies:
            copy.wait()

    result = pl.pallas_call(
        body,
        out_shape=shapes,
        in_specs=specs,
        out_specs=outs,
        scratch_shapes=[*extra, *scratch],
        name=name,
        compiler_params=None if first else pltpu.CompilerParams(vmem_limit_bytes=12 << 20),
        cost_estimate=pl.CostEstimate(flops=int(us * 1.153e9), bytes_accessed=1 << 16, transcendentals=0),
    )(*args, *after)
    return result if isinstance(out_shape, (list, tuple)) else result[0]


def shape(dims, kind=F32):
    return jax.ShapeDtypeStruct(dims, kind)


def shards(pixels, embed, query, w_query, w_key, w_value, w_out, b_out, pos_embed, w_lead, avail, lengths, lead_hours, cotangent):
    n_p = lax.axis_size("patch")
    n_j = lax.axis_size("var")
    p_id = lax.axis_index("patch")
    vl, _, rows = pixels.shape
    nv = vl * n_j
    cw = w_out.shape[1]
    hl = cw // HS
    dp = embed.shape[2]
    rl = w_value.shape[0]
    eb = pad16(5 * vl + 4)
    nr = n_j * eb
    ch = pad16(eb + (n_j + 1) * rl)
    vp = -(-vl // 8) * 8
    rc = nr // n_p
    others = range(1, n_j)

    pack = call(
        functools.partial(pack_kernel, eb),
        "pack",
        [shape((ch, cw), BF16)] * n_j,
        (w_value, w_key, w_query, query[None, :], embed.transpose(1, 0, 2), b_out[None, :], w_lead[None, :]),
        [pltpu.VMEM((ch, cw), F32)],
        first=True,
    )
    got = [pack[0]] + [flip(pack[k], "var", k) for k in others]

    buf, sums = call(
        rows_kernel,
        "rows",
        (shape((rows + 4 * vp * (rows // cw), cw), BF16), shape((2, cw))),
        (lengths, lead_hours, cotangent, pixels),
        [pltpu.VMEM((4 * vp, rows), F32)],
        smem=2,
        after=(pack[0],),
    )

    wo_lo = gate(w_out, pack[0]).astype(BF16)[None]
    bit = n_p // 2
    wo_hi = flip(wo_lo, "patch", bit)
    wo_steps = [wo_hi]
    while bit > 1:
        bit //= 2
        wo_lo = jnp.concatenate([gate(wo_lo, got[-1]), wo_hi], axis=0)
        wo_hi = flip(wo_lo, "patch", bit)
        wo_steps.append(wo_hi)

    part, e_all, k_blk, v_blk = call(
        functools.partial(product_kernel, eb, vl, rl, dp),
        "product",
        (shape((nr, 2 * cw), BF16), shape((nr, dp), BF16), shape((dp, cw), BF16), shape((dp, D), BF16)),
        (*got, sums),
        [pltpu.VMEM((dp, (n_j + 1) * cw), F32), pltpu.VMEM((nr, 2 * cw), F32)],
        us=1.0,
        spill=(1, 2, 3),
    )
    got2 = exchange(gate(part, wo_steps[-2]), "patch").reshape(n_p, rc, 2 * cw)
    copies = call(functools.partial(sum_kernel, vl), "sum", shape((n_p, rc, 2 * cw), BF16), (got2,), after=(wo_hi,))
    vk = exchange(copies.reshape(nr, 2 * cw), "patch")

    bufs = gather_var(gate(buf, part), lambda x: gate(x, copies))

    wo, *chunks, pix = call(
        functools.partial(weight_kernel, n_j, vl),
        "weight",
        [shape((D, cw), BF16)] + [shape((cw, cw), BF16)] * (n_j - 1) + [shape((4, nv, rows), BF16)],
        (wo_lo, wo_hi, *bufs),
        [pltpu.VMEM((4, nv, rows), F32)],
        after=(copies,),
    )
    chunks = [flip(c, "var", k + 1) for k, c in enumerate(chunks)]
    grad_att = call(
        functools.partial(grad_kernel, n_j), "grad_att", shape((cw, rows), BF16), (wo, *chunks, *bufs)
    )

    parts = GROUP // rows
    owners = n_p // parts
    per = pos_embed.shape[0]
    me = p_id // parts
    there = [(k * owners + i, parts * i + k) for i in range(owners) for k in range(parts)]
    back = [(b, a) for a, b in there]
    pos_lo = lax.ppermute(gate(pos_embed, wo).astype(BF16), "patch", there)[None]
    gpos = gate(buf, wo)[:rows].reshape(owners, per, cw)
    gpos = halve(gpos, me % 2, parts)

    att, prob, ef, vw = call(
        functools.partial(forward_kernel, 256, eb),
        "attention_forward",
        (
            shape((cw, rows), BF16),
            shape((hl, nv, rows)),
            shape((5, nv, hl)),
            shape((5 * nv, cw), BF16),
        ),
        (vk, pix, avail),
        [pltpu.VMEM((n_j, eb, 2 * cw), F32), pltpu.VMEM((5 * nv, 2 * cw), F32)],
        after=(*chunks, gpos),
    )

    *gx, z = call(
        functools.partial(backward_kernel, 256, eb, n_j, vp),
        "attention_backward",
        [shape((4 * vp, rows), BF16)] * n_j + [shape((nr, cw + 128), BF16)],
        (pix, ef, vw, prob, grad_att),
        [pltpu.VMEM((5 * nv, cw), F32), pltpu.VMEM((5 * hl, nv, 128), F32), pltpu.VMEM((n_j, eb, cw + 128), F32)],
        spill=tuple(range(1, n_j + 1)),
    )

    bit = n_p // 2
    pos_hi = flip(gate(pos_lo, z), "patch", bit)
    step = 2
    while step < owners:
        gpos = halve(gate(gpos, z), (me // step) % 2, parts * step)
        step *= 2

    got3 = exchange(z, "patch").reshape(n_p, rc, cw + 128)
    gx = [gx[0]] + [flip(gx[k], "var", k) for k in others]
    grad_pixels = sum(g.astype(F32) for g in gx).astype(BF16).reshape(4, vp, rows)[:, :vl].transpose(1, 0, 2)
    atts = gather_var(att, lambda x: gate(x, z))
    size = n_p // 2
    send, keep = call(
        functools.partial(weight_grad_kernel, n_j), "weight_grad", [shape((size, dp, cw), BF16)] * 2, (buf, *atts), [pltpu.VMEM((n_p, dp, cw), BF16)]
    )
    copies_z = call(
        functools.partial(sum_z_kernel, hl), "sum_z", shape((n_p, rc, cw + 128), BF16), (got3,), after=(send, *gx[1:])
    )
    z = exchange(copies_z.reshape(nr, cw + 128), "patch")

    step = 1
    halves = []
    while size > 1:
        size //= 2
        send, keep = call(
            functools.partial(halve_kernel, 2 * step),
            "halve",
            [shape((size, dp, cw), BF16)] * 2,
            (keep, flip(send, "patch", step)),
        )
        halves.append(send)
        step *= 2
    grad_w_out = (keep.astype(F32) + flip(send, "patch", step).astype(F32)).reshape(dp, cw)
    while bit > parts:
        bit //= 2
        pos_lo = jnp.concatenate([gate(pos_lo, copies_z), pos_hi], axis=0)
        pos_hi = flip(pos_lo, "patch", bit)
    grad_pos = lax.ppermute(gate(gpos, copies_z).reshape(per, cw), "patch", back)
    mixed = call(
        functools.partial(mixed_kernel, vl, n_j),
        "mixed",
        shape((rows, cw), BF16),
        (lengths, lead_hours, wo, vk, pos_lo, pos_hi, *atts),
        [pltpu.VMEM((owners, per, cw), BF16)],
        smem=2,
        after=(copies_z,),
    )
    fh = pad16(2 * rl + eb // 2 + 6)
    last = call(
        functools.partial(middle_kernel, eb, vl, n_j),
        "middle",
        [shape((fh, cw), BF16)] * n_j,
        (z, vk, k_blk, e_all, v_blk),
        [pltpu.VMEM((dp, 2 * cw), F32), pltpu.VMEM((nr, dp), F32), pltpu.VMEM((fh, cw), F32)],
        after=(halves[0],),
    )
    last = [last[0]] + [flip(last[k], "var", k) for k in others]
    gwv, gwk, gwq, gq, ge, gb, gl = call(
        functools.partial(final_kernel, eb, vl, rl, dp, n_j),
        "final",
        (
            shape((rl, D)),
            shape((rl, D)),
            shape((rl, D)),
            shape((1, rl)),
            shape((5, vl, dp)),
            shape((1, rl)),
            shape((1, rl)),
        ),
        (w_query, query[:, None], *last),
        [pltpu.VMEM((eb, dp), F32), pltpu.VMEM((8, D), F32)],
    )
    return (
        mixed,
        grad_pixels,
        ge.transpose(1, 0, 2),
        gq.reshape(rl),
        gwq,
        gwk,
        gwv,
        grad_w_out,
        gb.reshape(rl),
        grad_pos.astype(F32),
        gl.reshape(rl),
    )


def solution(mesh):
    both = P(("patch", "var"))
    rows2 = P(("patch", "var"), None)
    return jax.shard_map(
        shards,
        mesh=mesh,
        in_specs=(
            P("var", None, "patch"),
            P("var", None, "patch"),
            both,
            rows2,
            rows2,
            rows2,
            P("patch", "var"),
            both,
            P("patch", "var"),
            both,
            P(),
            P(),
            P(),
            P("patch", "var"),
        ),
        out_specs=(
            P("patch", "var"),
            P("var", None, "patch"),
            P("var", None, "patch"),
            both,
            rows2,
            rows2,
            rows2,
            P("patch", "var"),
            both,
            P("patch", "var"),
            both,
        ),
        check_vma=False,
    )
```

```python
import functools
import math

import jax
import jax.numpy as jnp
from jax import lax
from jax.experimental import pallas as pl
from jax.experimental.pallas import tpu as pltpu
from jax.sharding import PartitionSpec as P

D = 1024
HEADS = 16
HS = D // HEADS
GROUP = 2048
F32 = jnp.float32
BF16 = jnp.bfloat16
NEG = -1e30
SCALE = 1.0 / math.sqrt(HS)


def exchange(x, axis):
    return lax.all_to_all(x, axis, 0, 0, tiled=True)


def flip(x, axis, bit):
    n = lax.axis_size(axis)
    return lax.ppermute(x, axis, [(i, i ^ bit) for i in range(n)])


def gate(x, after):
    return lax.optimization_barrier((x, after))[0]


def gather_var(x, last):
    n = lax.axis_size("var")
    blocks = {0: x}
    bit = n // 2
    while bit:
        for k, block in list(blocks.items()):
            blocks[k | bit] = flip(last(block) if bit == 1 and k else block, "var", bit)
        bit //= 2
    return [blocks[k] for k in range(n)]


def halve(x, bit, step):
    pair = x.reshape(x.shape[0] // 2, 2, *x.shape[1:])
    send = lax.dynamic_index_in_dim(pair, 1 - bit, 1, False)
    keep = lax.dynamic_index_in_dim(pair, bit, 1, False)
    return keep, flip(send, "patch", step)


def joined(keep, got):
    return (keep.astype(F32) + got.astype(F32)).astype(BF16)


def nt(a, b):
    return lax.dot_general(a, b, (((1,), (1,)), ((), ())), preferred_element_type=F32)


def tn(a, b):
    return lax.dot_general(a, b, (((0,), (0,)), ((), ())), preferred_element_type=F32)


def nn(a, b):
    return jnp.dot(a, b, preferred_element_type=F32)


def pad16(n):
    return -(-n // 16) * 16


def split(value):
    hi = value.astype(BF16).astype(F32)
    return hi, value - hi


def put_pair(ref, row, lanes, value):
    ref[row : row + 1, :lanes], ref[row : row + 1, lanes : 2 * lanes] = split(value)


def put_rows(ref, block, row, lanes, value):
    ref[block, row : row + 1, :lanes], ref[block, row + 1 : row + 2, :lanes] = split(value)


def rows_kernel(length_ref, lead_ref, cot_ref, pix_ref, out_ref, sums_ref, tmp_ref):
    rows, cw = cot_ref.shape
    vl = pix_ref.shape[0]
    vp = tmp_ref.shape[0] // 4
    row0 = lax.axis_index("patch") * rows
    sample = row0 // GROUP
    pos = row0 % GROUP + lax.broadcasted_iota(jnp.int32, cot_ref.shape, 0)
    kept = jnp.where(pos < length_ref[sample], cot_ref[...].astype(F32), 0.0)
    out_ref[:rows] = kept.astype(BF16)
    total = jnp.sum(kept, axis=0, keepdims=True)
    sums_ref[0:1, :] = total
    sums_ref[1:2, :] = total * (lead_ref[sample].astype(F32) / 100.0)
    tmp_ref[...] = jnp.zeros_like(tmp_ref)
    for v in range(vl):
        x = pix_ref[v].astype(F32)
        for p in range(4):
            tmp_ref[p * vp + v : p * vp + v + 1, :] = x[p : p + 1]
    for b in range(rows // cw):
        out_ref[rows + b * 4 * vp : rows + (b + 1) * 4 * vp, :] = tmp_ref[:, b * cw : (b + 1) * cw].astype(BF16)


def pack_kernel(eb, v_ref, k_ref, wq_ref, q_ref, e_ref, b_ref, l_ref, wo_ref, *refs):
    outs, wo_low_ref, tmp_ref = refs[:-2], refs[-2], refs[-1]
    wo_low_ref[0] = wo_ref[...].astype(BF16)
    cw = outs[0].shape[1]
    rl = v_ref.shape[0]
    _, vl, dp = e_ref.shape
    spare = 5 * vl
    j = lax.axis_index("var")
    q = jnp.broadcast_to(q_ref[...].astype(BF16), (16, rl))
    tmp_ref[...] = jnp.zeros_like(tmp_ref)
    for p in range(5):
        tmp_ref[p * vl : (p + 1) * vl, :dp] = e_ref[p]
    own = lax.broadcasted_iota(jnp.int32, (1, dp), 1) // rl == j
    for i, ref in enumerate((b_ref, l_ref)):
        tiled = jnp.concatenate([ref[...]] * (dp // rl), axis=1)
        tmp_ref[spare + 2 + i : spare + 3 + i, :dp] = jnp.where(own, tiled, 0.0)
    for k, out_ref in enumerate(outs):
        cols = pl.ds(pl.multiple_of((j ^ k) * cw, 128), cw)
        hi, lo = split(nn(q, wq_ref[:, cols].astype(BF16))[0:1])
        tmp_ref[spare : spare + 1, :] = hi
        tmp_ref[spare + 1 : spare + 2, :] = lo
        tmp_ref[eb : eb + rl, :] = k_ref[:, cols]
        tmp_ref[eb + rl : eb + 2 * rl, :] = v_ref[:, cols]
        out_ref[...] = tmp_ref[...].astype(BF16)


def place(ref, at, j, size, parts, lanes):
    if size % 16 == 0:
        for k, part in enumerate(parts):
            ref[pl.ds(pl.multiple_of((j ^ k) * size, size), size), lanes] = part
        return
    for s in range(len(parts)):
        value = parts[0]
        for k in range(1, len(parts)):
            value = jnp.where(j ^ k == s, parts[k], value)
        ref[s * size : (s + 1) * size, lanes] = value


def product_kernel(eb, vl, rl, dp, *refs):
    n = len(refs) - 5
    got, (sums_ref, out_ref, ekv_ref, w_ref, p_ref) = refs[:n], refs[n:]
    cw = got[0].shape[1]
    spare = 5 * vl
    lanes = -(-dp // 128) * 128
    p_id = lax.axis_index("patch")
    j = lax.axis_index("var")
    live = lax.broadcasted_iota(jnp.int32, (eb, dp), 0) < spare
    small = jnp.zeros((4, cw), F32)
    gs = [got[k][...].astype(F32) for k in range(n)]
    for k in range(n):
        small = small + gs[k][spare : spare + 4]
        at = pl.ds(pl.multiple_of((j ^ k) * eb, eb), eb)
        ekv_ref[at, :dp] = jnp.where(live, gs[k][:eb, :dp], 0.0).astype(BF16)
    for m in range(2):
        at = eb + m * rl
        place(w_ref, 0, j, rl, [g[at : at + rl] for g in gs], slice(m * cw, (m + 1) * cw))
    key, value = w_ref[:, :cw].astype(BF16), w_ref[:, cw:].astype(BF16)
    ekv_ref[:dp, lanes : lanes + cw] = key
    ekv_ref[dp : 2 * dp, lanes : lanes + cw] = value
    p_ref[...] = nn(ekv_ref[:, :dp], jnp.concatenate([value, key], axis=1))
    put_pair(p_ref, spare, cw, small[0:1] + small[1:2])
    put_pair(p_ref, spare + 1, cw, sums_ref[0:1])
    put_pair(p_ref, spare + 2, cw, sums_ref[1:2])
    per = cw // dp
    here = (lax.broadcasted_iota(jnp.int32, (1, cw), 1) // dp == p_id % per) & (p_id // per == j)
    for i in range(2):
        tiled = jnp.concatenate([small[2 + i : 3 + i, :dp]] * per, axis=1)
        p_ref[spare + 3 : spare + 4, i * cw : (i + 1) * cw] = jnp.where(here, tiled, 0.0)
    out_ref[...] = p_ref[...].astype(BF16)


def sum_kernel(vl, got_ref, out_ref):
    n_p, rc, lanes = got_ref.shape
    cw = lanes // 2
    total = got_ref[0].astype(F32)
    for s in range(1, n_p):
        total = total + got_ref[s].astype(F32)
    row = lax.axis_index("patch") * rc + lax.broadcasted_iota(jnp.int32, (rc, cw), 0)
    paired = (row >= 5 * vl) & (row < 5 * vl + 3)
    a, b = total[:, :cw], total[:, cw:]
    hi, lo = split(a + b)
    a, b = jnp.where(paired, hi, a).astype(BF16), jnp.where(paired, lo, b).astype(BF16)
    for s in range(n_p):
        out_ref[s, :, :cw] = a
        out_ref[s, :, cw:] = b


def forward_kernel(tile, eb, vk_ref, x_ref, avail_ref, att_ref, prob_ref, ef_ref, vw_ref, s_ref, vs_ref):
    nv, rows = x_ref.shape[1:]
    heads = prob_ref.shape[0]
    cw = att_ref.shape[0]
    n_j = vk_ref.shape[0] // eb
    vl = nv // n_j
    spare = 5 * vl
    j = lax.axis_index("var")
    for s in range(n_j):
        s_ref[s] = vk_ref[s * eb : (s + 1) * eb, :].astype(F32)
    q = (s_ref[0, spare : spare + 1, :cw] + s_ref[0, spare : spare + 1, cw:]) * SCALE
    for k in range(n_j):
        for p in range(5):
            vs_ref[p * nv + k * vl : p * nv + (k + 1) * vl, :] = s_ref[j ^ k, p * vl : (p + 1) * vl, :]
    vw_ref[...] = vs_ref[:, :cw].astype(BF16)
    for p in range(5):
        kq = vs_ref[p * nv : (p + 1) * nv, cw:] * q
        ef_ref[p] = jnp.concatenate(
            [jnp.sum(kq[:, h * HS : (h + 1) * HS], axis=1, keepdims=True) for h in range(heads)], axis=1
        )
    sample = lax.axis_index("patch") * rows // GROUP
    row = lax.broadcasted_iota(jnp.int32, (nv, nv), 0)
    shift = jnp.zeros((nv, nv), jnp.int32)
    for k in range(n_j):
        shift = jnp.where((row >= k * vl) & (row < (k + 1) * vl), ((j ^ k) - k) * vl, shift)
    same = row + shift == lax.broadcasted_iota(jnp.int32, (nv, nv), 1)
    flags = jnp.broadcast_to(avail_ref[pl.ds(sample, 1), :], (nv, nv))
    present = jnp.sum(jnp.where(same, flags.astype(F32), 0.0), axis=1, keepdims=True) > 0.5
    vw = [vw_ref[:, h * HS : (h + 1) * HS] for h in range(heads)]

    def step(i, carry):
        cols = pl.ds(pl.multiple_of(i * tile, tile), tile)
        xs = [x_ref[p, :, cols].astype(F32) for p in range(4)]
        for h in range(heads):
            s = jnp.broadcast_to(ef_ref[4, :, h : h + 1], (nv, tile))
            for p in range(4):
                s = s + ef_ref[p, :, h : h + 1] * xs[p]
            s = jnp.where(present, s, NEG)
            w = jnp.where(present, jnp.exp(s - jnp.max(s, axis=0, keepdims=True)), 0.0)
            prob = w / jnp.sum(w, axis=0, keepdims=True)
            prob_ref[h, :, cols] = prob
            a = jnp.concatenate([(prob * x).astype(BF16) for x in xs] + [prob.astype(BF16)], axis=0)
            att_ref[h * HS : (h + 1) * HS, cols] = tn(vw[h], a).astype(BF16)
        return carry

    lax.fori_loop(0, rows // tile, step, 0)


def reversed_bits(x, bits):
    out = 0
    for b in range(bits):
        out = out | (((x >> b) & 1) << (bits - 1 - b))
    return out


def pixel_kernel(vl, cw, *refs):
    bufs, (out_ref, x_ref) = refs[:-2], refs[-2:]
    rows = out_ref.shape[2]
    vp = (bufs[0].shape[0] - rows) // (4 * (rows // cw))
    for k, buf in enumerate(bufs):
        for b in range(rows // cw):
            at = rows + b * 4 * vp
            x = buf[at : at + 4 * vp, :].astype(F32)
            for p in range(4):
                x_ref[p, k * vl : (k + 1) * vl, b * cw : (b + 1) * cw] = x[p * vp : p * vp + vl]
    for p in range(4):
        out_ref[p] = x_ref[p].astype(BF16)


def weight_kernel(lo_ref, hi_ref, full_ref, *chunks):
    half, dp, cw = lo_ref.shape
    p_id = lax.axis_index("patch")
    j = lax.axis_index("var")
    for q in range(2 * half):
        block = reversed_bits(q ^ p_id, (2 * half).bit_length() - 1)
        at = slice(q * dp, (q + 1) * dp)

        @pl.when(block < half)
        def _(at=at, block=block):
            full_ref[at, :] = lo_ref[block]

        @pl.when(block >= half)
        def _(at=at, block=block):
            full_ref[at, :] = hi_ref[block - half]

    for k, ref in enumerate(chunks):
        ref[...] = full_ref[pl.ds(pl.multiple_of((j ^ (k + 1)) * cw, cw), cw), :]


def grad_kernel(n_j, full_ref, *refs):
    ws, cots, (out_ref,) = refs[: n_j - 1], refs[n_j - 1 : -1], refs[-1:]
    cw, rows = out_ref.shape
    j = lax.axis_index("var")
    own = full_ref[pl.ds(pl.multiple_of(j * cw, cw), cw), :]
    tile = 256
    for i in range(rows // tile):
        at = slice(i * tile, (i + 1) * tile)
        total = nt(own, cots[0][at, :])
        for k in range(1, n_j):
            total = total + nt(ws[k - 1][...], cots[k][at, :])
        out_ref[:, at] = total.astype(BF16)


def weight_grad_kernel(n_j, buf_ref, *refs):
    atts, (send_ref, keep_ref, tmp_ref) = refs[:n_j], refs[n_j:]
    cw, rows = atts[0].shape
    half, dp, _ = keep_ref.shape
    j = lax.axis_index("var")
    per = cw // dp
    for k in range(n_j):
        g = nn(atts[k][...], buf_ref[:rows, :]).astype(BF16)
        for t in range(per):
            tmp_ref[(j ^ k) * per + t] = g[t * dp : (t + 1) * dp]
    own = lax.axis_index("patch") & 1
    for b in range(half):
        send_ref[b * dp : (b + 1) * dp, :] = tmp_ref[2 * b + 1 - own]
        keep_ref[b] = tmp_ref[2 * b + own]


def halve_kernel(bit, g_ref, got_ref, *refs):
    count, dp, cw = g_ref.shape
    own = jnp.where(lax.axis_index("patch") & (2 * bit), 1, 0)

    def g_sum(b):
        at = pl.ds(pl.multiple_of(b * dp, dp), dp)
        return g_ref[b].astype(F32) + got_ref[at, :].astype(F32)

    if count == 1:
        pos_ref, out_ref, pos_out_ref = refs
        out_ref[...] = g_sum(0)
        pos_out_ref[...] = pos_ref[...].astype(F32)
        return
    send_ref, g_next = refs
    for b in range(g_next.shape[0]):
        send_ref[b * dp : (b + 1) * dp, :] = g_sum(2 * b + 1 - own).astype(BF16)
        g_next[b] = g_sum(2 * b + own).astype(BF16)


def pixel_add_kernel(keep_ref, got_ref, next_ref, send_ref):
    for i in range(next_ref.shape[0]):
        next_ref[i] = (keep_ref[2 * i].astype(F32) + got_ref[2 * i].astype(F32)).astype(BF16)
        send_ref[i] = (keep_ref[2 * i + 1].astype(F32) + got_ref[2 * i + 1].astype(F32)).astype(BF16)


def mixed_kernel(vl, n_j, length_ref, lead_ref, w_ref, vk_ref, plo_ref, phi_ref, pk_ref, pg_ref, *refs):
    atts, (out_ref, px_ref, pos_ref, s_ref, x_ref) = refs[:n_j], refs[n_j:]
    s_ref[...] = pk_ref[0].astype(F32) + pg_ref[0].astype(F32)
    vp = s_ref.shape[0] // 4
    for v in range(vl):
        for p in range(4):
            x_ref[4 * v + p : 4 * v + p + 1, :] = s_ref[p * vp + v : p * vp + v + 1, :]
    for v in range(vl):
        px_ref[v] = x_ref[4 * v : 4 * v + 4, :].astype(BF16)
    rows, cw = out_ref.shape
    spare = 5 * vl
    base = pad16(spare) - 16
    row0 = lax.axis_index("patch") * rows
    sample = row0 // GROUP
    me = lax.axis_index("patch") // (GROUP // rows)
    j = lax.axis_index("var")
    half, per, _ = plo_ref.shape
    pos_ref[:half] = plo_ref[...]
    pos_ref[half:] = phi_ref[...]
    bl = vk_ref[base : base + 32, :].astype(F32)[spare - base + 3 : spare - base + 4]
    add = bl[:, :cw] + lead_ref[sample].astype(F32) / 100.0 * bl[:, cw:]
    for b in range(2 * half):
        at = slice(b * per, (b + 1) * per)
        total = add + pos_ref[reversed_bits(b ^ me, (2 * half).bit_length() - 1)].astype(F32)
        for k in range(n_j):
            w = w_ref[pl.ds(pl.multiple_of((j ^ k) * cw, cw), cw), :]
            total = total + tn(atts[k][:, at], w)
        pos = row0 % GROUP + b * per + lax.broadcasted_iota(jnp.int32, (per, cw), 0)
        out_ref[at, :] = jnp.where(pos < length_ref[sample], total, 0.0).astype(BF16)


def backward_kernel(tile, eb, n_j, vp, x_ref, ef_ref, vw_ref, prob_ref, grad_ref, *refs):
    outs, (z_ref, gv_ref, acc_ref, s_ref) = refs[:-4], refs[-4:]
    nv, rows = x_ref.shape[1:]
    heads = prob_ref.shape[0]
    vl = nv // n_j
    cw = gv_ref.shape[1]
    j = lax.axis_index("var")
    gv_ref[...] = jnp.zeros_like(gv_ref)
    acc_ref[...] = jnp.zeros_like(acc_ref)
    blank = jnp.zeros((vp - vl, tile), F32)

    def step(i, carry):
        cols = pl.ds(pl.multiple_of(i * tile, tile), tile)
        xs = [x_ref[p, :, cols].astype(F32) for p in range(4)]
        gx = [jnp.zeros((nv, tile), F32) for _ in range(4)]
        for h in range(heads):
            hc = slice(h * HS, (h + 1) * HS)
            prob = prob_ref[h, :, cols]
            gh = grad_ref[hc, cols]
            g = nn(vw_ref[:, hc], gh)
            gp = [g[p * nv : (p + 1) * nv] for p in range(5)]
            gprob = gp[4]
            for p in range(4):
                gprob = gprob + xs[p] * gp[p]
            inner = jnp.sum(prob * gprob, axis=0, keepdims=True)
            gs = prob * (gprob - inner)
            for p in range(4):
                gx[p] = gx[p] + prob * gp[p] + ef_ref[p, :, h : h + 1] * gs
            a = jnp.concatenate([(prob * x).astype(BF16) for x in xs] + [prob.astype(BF16)], axis=0)
            gv_ref[:, hc] += nt(a, gh)
            for p in range(5):
                t = gs if p == 4 else gs * xs[p]
                part = t[:, :128]
                for k in range(1, tile // 128):
                    part = part + t[:, k * 128 : (k + 1) * 128]
                acc_ref[p * heads + h] += part
        for k in range(n_j):
            ref = outs[k & 1].at[k >> 1]
            piece = jnp.concatenate([t for p in range(4) for t in (gx[p][k * vl : (k + 1) * vl], blank)], axis=0)
            ref[:, cols] = piece.astype(BF16)
        return carry

    lax.fori_loop(0, rows // tile, step, 0)
    s_ref[...] = jnp.zeros_like(s_ref)
    for p in range(5):
        gs = jnp.concatenate(
            [jnp.sum(acc_ref[p * heads + h], axis=1, keepdims=True) for h in range(heads)], axis=1
        )
        hi, lo = split(gs)
        pair = jnp.concatenate([hi, lo, jnp.zeros((nv, 128 - 2 * heads), F32)], axis=1)
        for k in range(n_j):
            at = slice(p * nv + k * vl, p * nv + (k + 1) * vl)
            s_ref[j ^ k, p * vl : (p + 1) * vl, :cw] = gv_ref[at, :]
            s_ref[j ^ k, p * vl : (p + 1) * vl, cw:] = pair[k * vl : (k + 1) * vl]
    for s in range(n_j):
        z_ref[s * eb : (s + 1) * eb, :] = s_ref[s].astype(BF16)


def sum_z_kernel(heads, got_ref, out_ref):
    n_p, rc, lanes = got_ref.shape
    cw = lanes - 128
    total = got_ref[0].astype(F32)
    for s in range(1, n_p):
        total = total + got_ref[s].astype(F32)
    main = total[:, :cw].astype(BF16)
    hi, lo = split(total[:, cw : cw + heads] + total[:, cw + heads : cw + 2 * heads])
    pair = jnp.concatenate([hi, lo, jnp.zeros((rc, 128 - 2 * heads), F32)], axis=1).astype(BF16)
    for s in range(n_p):
        out_ref[s, :, :cw] = main
        out_ref[s, :, cw:] = pair


def middle_kernel(eb, vl, n_j, dp, z_ref, vk_ref, ekv_ref, *refs):
    chunks, (g_ref, ge_ref, s_ref) = refs[:n_j], refs[n_j:]
    cw = z_ref.shape[1] - 128
    lanes = -(-dp // 128) * 128
    key, value = ekv_ref[:dp, lanes : lanes + cw], ekv_ref[dp : 2 * dp, lanes : lanes + cw]
    rl = dp // n_j
    heads = cw // HS
    spare = 5 * vl
    half = eb // 2
    j = lax.axis_index("var")
    base = pad16(spare) - 16
    small = vk_ref[base : base + 32, :].astype(F32)[spare - base : spare - base + 3]
    small = small[:, :cw] + small[:, cw:]
    qvec = small[0:1] * SCALE
    g = tn(ekv_ref[:, :dp], z_ref[...])
    gfold = g[:, cw : cw + heads] + g[:, cw + heads : cw + 2 * heads]
    g_ref[:, :cw] = g[:, :cw]
    g_ref[:, cw:] = jnp.concatenate(
        [gfold[:, h : h + 1] * qvec[:, h * HS : (h + 1) * HS] for h in range(heads)], axis=1
    )
    pair = z_ref[:, cw:].astype(F32)
    gs = pair[:, :heads] + pair[:, heads : 2 * heads]
    live = lax.broadcasted_iota(jnp.int32, (n_j * eb, 1), 0) % eb < spare
    ke = jnp.where(live, vk_ref[:, cw:].astype(F32), 0.0)
    gq = jnp.concatenate(
        [jnp.sum(ke[:, h * HS : (h + 1) * HS] * gs[:, h : h + 1], axis=0, keepdims=True) for h in range(heads)], axis=1
    ) * SCALE
    head = lax.broadcasted_iota(jnp.int32, (8, cw), 0) == lax.broadcasted_iota(jnp.int32, (8, cw), 1) // HS
    hi, lo = split(jnp.where(head, qvec, 0.0))
    fold = nt(hi.astype(BF16), key) + nt(lo.astype(BF16), key)
    ge = nt(z_ref[:, :cw], value)
    for h in range(heads):
        ge = ge + gs[:, h : h + 1] * fold[h : h + 1, :]
    ge_ref[...] = ge
    s_ref[...] = jnp.zeros_like(s_ref)
    at = 2 * rl + half
    for i, row in enumerate((gq, small[1:2], small[2:3])):
        s_ref[at + 2 * i : at + 2 * i + 1, :], s_ref[at + 2 * i + 1 : at + 2 * i + 2, :] = split(row)
    for k in range(n_j):
        rows = own_rows(g_ref, j ^ k, rl)
        s_ref[:rl, :] = rows[:, :cw]
        s_ref[rl : 2 * rl, :] = rows[:, cw:]
        block = ge_ref[pl.ds(pl.multiple_of((j ^ k) * eb, eb), eb), :]
        s_ref[2 * rl : 2 * rl + half, :dp] = block[:half]
        s_ref[2 * rl : 2 * rl + half, cw // 2 : cw // 2 + dp] = block[half:]
        chunks[k][...] = s_ref[...].astype(BF16)


def own_rows(ref, index, size):
    if size % 8 == 0:
        return ref[pl.ds(pl.multiple_of(index * size, size), size), :]
    out = ref[:size, :]
    for k in range(1, ref.shape[0] // size):
        out = jnp.where(index == k, ref[k * size : (k + 1) * size, :], out)
    return out


def final_kernel(eb, vl, rl, dp, n_j, wq_ref, q_ref, *refs):
    chunks, (gwv_ref, gwk_ref, gwq_ref, gq_ref, ge_ref, gb_ref, gl_ref, f_ref, r_ref) = refs[:n_j], refs[n_j:]
    cw = chunks[0].shape[1]
    half = eb // 2
    j = lax.axis_index("var")
    at_out = lax.axis_index("patch") * n_j + j
    at = 2 * rl + half
    ge = jnp.zeros((half, cw), F32)
    gb = jnp.zeros((1, rl), F32)
    gl = jnp.zeros((1, rl), F32)
    for k in range(n_j):
        c = chunks[k][...].astype(F32)
        cols = pl.ds(pl.multiple_of((j ^ k) * cw, 128), cw)
        gwv_ref[:, cols] = c[:rl]
        gwk_ref[:, cols] = c[rl : 2 * rl]
        ge = ge + c[2 * rl : at]
        r_ref[0:1, cols] = c[at : at + 1] + c[at + 1 : at + 2]
        bias = c[at + 2 : at + 3] + c[at + 3 : at + 4]
        lead = c[at + 4 : at + 5] + c[at + 5 : at + 6]
        for g in range(cw // rl):
            here = at_out == (j ^ k) * (cw // rl) + g
            gb = gb + jnp.where(here, bias[:, g * rl : (g + 1) * rl], 0.0)
            gl = gl + jnp.where(here, lead[:, g * rl : (g + 1) * rl], 0.0)
    f_ref[:half, :] = ge[:, :dp]
    f_ref[half:, :] = ge[:, cw // 2 : cw // 2 + dp]
    for p in range(5):
        ge_ref[p] = f_ref[p * vl : (p + 1) * vl, :]
    gq = r_ref[0:1, :]
    gwq_ref[...] = q_ref[...].astype(BF16).astype(F32) * gq
    hi, lo = split(gq)
    wq = wq_ref[...].astype(BF16)
    both = jnp.concatenate([jnp.broadcast_to(hi, (8, D)), jnp.broadcast_to(lo, (8, D))], axis=0).astype(BF16)
    two = nt(both, wq)
    gq_ref[...] = two[0:1] + two[8:9]
    gb_ref[...] = gb
    gl_ref[...] = gl


def call(kernel, name, out_shape, args, scratch=(), us=0.01, smem=0, after=(), first=False, spill=(), hbm=0):
    n = len(args)
    in_vmem = pl.BlockSpec(memory_space=pltpu.VMEM)
    specs = [pl.BlockSpec(memory_space=pltpu.SMEM)] * smem + [pl.BlockSpec() if first else in_vmem] * (n - smem)
    specs[n - hbm :] = [pl.BlockSpec(memory_space=pl.ANY)] * hbm
    specs += [pl.BlockSpec(memory_space=pl.ANY)] * len(after)
    shapes = list(out_shape) if isinstance(out_shape, (list, tuple)) else [out_shape]
    outs = [pl.BlockSpec(memory_space=pltpu.HBM) if i in spill else in_vmem for i in range(len(shapes))]
    extra = [pltpu.VMEM(shapes[i].shape, shapes[i].dtype) for i in spill]
    if spill:
        extra.append(pltpu.SemaphoreType.DMA((len(spill),)))

    def body(*refs):
        ins, rest = refs[:n], refs[n + len(after) :]
        results, rest = list(rest[: len(shapes)]), rest[len(shapes) :]
        local, sems = rest[: len(spill)], rest[len(extra) - 1 : len(extra)]
        rest = rest[len(extra) :]
        copies = []
        for c, i in enumerate(spill):
            copies.append(pltpu.make_async_copy(local[c], results[i], sems[0].at[c]))
            results[i] = local[c]
        kernel(*ins, *results, *rest)
        for copy in copies:
            copy.start()
        for copy in copies:
            copy.wait()

    result = pl.pallas_call(
        body,
        out_shape=shapes,
        in_specs=specs,
        out_specs=outs,
        scratch_shapes=[*extra, *scratch],
        name=name,
        compiler_params=None if first else pltpu.CompilerParams(vmem_limit_bytes=12 << 20),
        cost_estimate=pl.CostEstimate(flops=int(us * 1.153e9), bytes_accessed=1 << 16, transcendentals=0),
    )(*args, *after)
    return result if isinstance(out_shape, (list, tuple)) else result[0]


def shape(dims, kind=F32):
    return jax.ShapeDtypeStruct(dims, kind)


def shards(pixels, embed, query, w_query, w_key, w_value, w_out, b_out, pos_embed, w_lead, avail, lengths, lead_hours, cotangent):
    n_p = lax.axis_size("patch")
    n_j = lax.axis_size("var")
    p_id = lax.axis_index("patch")
    vl, _, rows = pixels.shape
    nv = vl * n_j
    cw = w_out.shape[1]
    hl = cw // HS
    dp = embed.shape[2]
    rl = w_value.shape[0]
    eb = pad16(5 * vl + 4)
    nr = n_j * eb
    ch = pad16(eb + 2 * rl)
    vp = -(-vl // 8) * 8
    rc = nr // n_p
    others = range(1, n_j)

    *pack, wo_lo = call(
        functools.partial(pack_kernel, eb),
        "pack",
        [shape((ch, cw), BF16)] * n_j + [shape((1, dp, cw), BF16)],
        (w_value, w_key, w_query, query[None, :], embed.transpose(1, 0, 2), b_out[None, :], w_lead[None, :], w_out),
        [pltpu.VMEM((ch, cw), F32)],
        first=True,
    )
    got = [pack[0]] + [flip(pack[k], "var", k) for k in others]

    buf, sums = call(
        rows_kernel,
        "rows",
        (shape((rows + 4 * vp * (rows // cw), cw), BF16), shape((2, cw))),
        (lengths, lead_hours, cotangent, pixels),
        [pltpu.VMEM((4 * vp, rows), F32)],
        smem=2,
        after=(pack[0],),
    )

    bit = n_p // 2
    wo_hi = flip(wo_lo, "patch", bit)
    wo_steps = [wo_hi]
    while bit > 1:
        bit //= 2
        wo_lo = jnp.concatenate([gate(wo_lo, got[-1]), wo_hi], axis=0)
        wo_hi = flip(wo_lo, "patch", bit)
        wo_steps.append(wo_hi)

    part, ekv = call(
        functools.partial(product_kernel, eb, vl, rl, dp),
        "product",
        (shape((nr, 2 * cw), BF16), shape((nr, -(-dp // 128) * 128 + cw), BF16)),
        (*got, sums),
        [pltpu.VMEM((dp, 2 * cw), F32), pltpu.VMEM((nr, 2 * cw), F32)],
        us=0.01,
    )
    got2 = exchange(part, "patch").reshape(n_p, rc, 2 * cw)
    wo, *chunks = call(
        weight_kernel, "weight", [shape((D, cw), BF16)] + [shape((cw, cw), BF16)] * (n_j - 1), (wo_lo, wo_hi)
    )
    copies = call(functools.partial(sum_kernel, vl), "sum", shape((n_p, rc, 2 * cw), BF16), (got2,), after=(wo,))
    vk = exchange(copies.reshape(nr, 2 * cw), "patch")

    bufs = gather_var(gate(buf, part), lambda x: gate(x, copies))
    pix = call(
        functools.partial(pixel_kernel, vl, cw),
        "pixels",
        shape((4, nv, rows), BF16),
        bufs,
        [pltpu.VMEM((4, nv, rows), F32)],
    )

    chunks = [flip(c, "var", k + 1) for k, c in enumerate(chunks)]
    grad_att = call(
        functools.partial(grad_kernel, n_j), "grad_att", shape((cw, rows), BF16), (wo, *chunks, *bufs), after=(vk,)
    )

    parts = GROUP // rows
    owners = n_p // parts
    per = pos_embed.shape[0]
    there = [(k * owners + i, parts * i + k) for i in range(owners) for k in range(parts)]
    back = [(b, a) for a, b in there]
    pos_lo = lax.ppermute(gate(pos_embed, chunks[0]).astype(BF16), "patch", there)[None]
    att, prob, ef, vw = call(
        functools.partial(forward_kernel, 256, eb),
        "attention_forward",
        (shape((cw, rows), BF16), shape((hl, nv, rows)), shape((5, nv, hl)), shape((5 * nv, cw), BF16)),
        (vk, pix, avail),
        [pltpu.VMEM((n_j, eb, 2 * cw), F32), pltpu.VMEM((5 * nv, 2 * cw), F32)],
        after=(grad_att, pos_lo),
    )
    px_keep, px_send, z = call(
        functools.partial(backward_kernel, 256, eb, n_j, vp),
        "attention_backward",
        [shape((n_j // 2, 4 * vp, rows), BF16)] * 2 + [shape((nr, cw + 128), BF16)],
        (pix, ef, vw, prob, grad_att),
        [pltpu.VMEM((5 * nv, cw), F32), pltpu.VMEM((5 * hl, nv, 128), F32), pltpu.VMEM((n_j, eb, cw + 128), F32)],
    )

    got3 = exchange(z, "patch").reshape(n_p, rc, cw + 128)
    me = p_id // parts
    pos_hi = flip(gate(pos_lo, z), "patch", n_p // 2)
    g_rows = halve(gate(buf, z)[:rows].reshape(owners, per, cw), me % 2, parts)
    atts = [att] + [flip(gate(att, z), "var", k) for k in others]
    copies_z = call(functools.partial(sum_z_kernel, hl), "sum_z", shape((n_p, rc, cw + 128), BF16), (got3,), after=(g_rows[1],))
    zs = exchange(copies_z.reshape(nr, cw + 128), "patch")

    size = n_p // 2
    send, g_keep = call(
        functools.partial(weight_grad_kernel, n_j),
        "weight_grad",
        [shape((size * dp, cw), BF16), shape((size, dp, cw), BF16)],
        (buf, *atts),
        [pltpu.VMEM((n_p, dp, cw), BF16)],
        after=(copies_z,),
    )
    step = 1
    size //= 2
    send, g_keep = call(
        functools.partial(halve_kernel, step),
        "halve",
        [shape((size * dp, cw), BF16), shape((size, dp, cw), BF16)],
        (g_keep, flip(send, "patch", step)),
    )
    bit = n_p // 2
    while bit > parts:
        bit //= 2
        pos_lo = jnp.concatenate([gate(pos_lo, copies_z), pos_hi], axis=0)
        pos_hi = flip(pos_lo, "patch", bit)
    turn = 2
    while turn < owners:
        g_rows = halve(gate(joined(*g_rows), copies_z), (me // turn) % 2, parts * turn)
        turn *= 2
    px_got = flip(gate(px_send, copies_z), "var", 1)
    fh = pad16(2 * rl + eb // 2 + 6)
    last = call(
        functools.partial(middle_kernel, eb, vl, n_j, dp),
        "middle",
        [shape((fh, cw), BF16)] * n_j,
        (zs, vk, ekv),
        [pltpu.VMEM((dp, 2 * cw), F32), pltpu.VMEM((nr, dp), F32), pltpu.VMEM((fh, cw), F32)],
        after=(send,),
    )

    def late(x):
        return gate(x, last[0])

    while size > 1:
        size //= 2
        step *= 2
        send, g_keep = call(
            functools.partial(halve_kernel, step),
            "halve",
            [shape((size * dp, cw), BF16), shape((size, dp, cw), BF16)],
            (g_keep, flip(send, "patch", step)),
            after=(last[0],),
        )
    grad_pos = lax.ppermute(joined(g_rows[0], late(g_rows[1])).reshape(per, cw), "patch", back)
    grad_w_out, grad_pos = call(
        functools.partial(halve_kernel, 2 * step),
        "halve",
        (shape((dp, cw)), shape((per, cw))),
        (g_keep, flip(send, "patch", 2 * step), grad_pos),
    )

    bit = 1
    while 2 * bit < n_j:
        bit *= 2
        px_keep, px_send = call(
            pixel_add_kernel,
            "pixel_add",
            [shape((n_j // (2 * bit), 4 * vp, rows), BF16)] * 2,
            (px_keep, px_got),
            after=(send,),
        )
        px_got = flip(px_send, "var", bit)
    mixed, grad_pixels = call(
        functools.partial(mixed_kernel, vl, n_j),
        "mixed",
        (shape((rows, cw), BF16), shape((vl, 4, rows), BF16)),
        (lengths, lead_hours, wo, vk, pos_lo, pos_hi, px_keep, px_got, *atts),
        [pltpu.VMEM((owners, per, cw), BF16), pltpu.VMEM((4 * vp, rows), F32), pltpu.VMEM((4 * vl, rows), F32)],
        smem=2,
        after=(send,),
    )

    last = [last[0]] + [flip(last[k], "var", k) for k in others]
    gwv, gwk, gwq, gq, ge, gb, gl = call(
        functools.partial(final_kernel, eb, vl, rl, dp, n_j),
        "final",
        (
            shape((rl, D)),
            shape((rl, D)),
            shape((rl, D)),
            shape((1, rl)),
            shape((5, vl, dp)),
            shape((1, rl)),
            shape((1, rl)),
        ),
        (w_query, query[:, None], *last),
        [pltpu.VMEM((eb, dp), F32), pltpu.VMEM((8, D), F32)],
        after=(mixed,),
    )
    return (
        mixed,
        grad_pixels,
        ge.transpose(1, 0, 2),
        gq.reshape(rl),
        gwq,
        gwk,
        gwv,
        grad_w_out,
        gb.reshape(rl),
        grad_pos,
        gl.reshape(rl),
    )


def solution(mesh):
    both = P(("patch", "var"))
    rows2 = P(("patch", "var"), None)
    return jax.shard_map(
        shards,
        mesh=mesh,
        in_specs=(
            P("var", None, "patch"),
            P("var", None, "patch"),
            both,
            rows2,
            rows2,
            rows2,
            P("patch", "var"),
            both,
            P("patch", "var"),
            both,
            P(),
            P(),
            P(),
            P("patch", "var"),
        ),
        out_specs=(
            P("patch", "var"),
            P("var", None, "patch"),
            P("var", None, "patch"),
            both,
            rows2,
            rows2,
            rows2,
            P("patch", "var"),
            both,
            P("patch", "var"),
            both,
        ),
        check_vma=False,
    )
```

```python
import functools
import math

import jax
import jax.numpy as jnp
from jax import lax
from jax.experimental import pallas as pl
from jax.experimental.pallas import tpu as pltpu
from jax.sharding import PartitionSpec as P

D = 1024
HEADS = 16
HS = D // HEADS
GROUP = 2048
F32 = jnp.float32
BF16 = jnp.bfloat16
NEG = -1e30
SCALE = 1.0 / math.sqrt(HS)


def exchange(x, axis):
    return lax.all_to_all(x, axis, 0, 0, tiled=True)


def flip(x, axis, bit):
    n = lax.axis_size(axis)
    return lax.ppermute(x, axis, [(i, i ^ bit) for i in range(n)])


def gate(x, after):
    return lax.optimization_barrier((x, after))[0]


def gather_var(x, last):
    n = lax.axis_size("var")
    blocks = {0: x}
    bit = n // 2
    while bit:
        for k, block in list(blocks.items()):
            blocks[k | bit] = flip(last(block) if bit == 1 and k else block, "var", bit)
        bit //= 2
    return [blocks[k] for k in range(n)]


def halve(x, bit, step):
    pair = x.reshape(x.shape[0] // 2, 2, *x.shape[1:])
    send = lax.dynamic_index_in_dim(pair, 1 - bit, 1, False)
    keep = lax.dynamic_index_in_dim(pair, bit, 1, False)
    return keep, flip(send, "patch", step)


def joined(keep, got):
    return (keep.astype(F32) + got.astype(F32)).astype(BF16)


def nt(a, b):
    return lax.dot_general(a, b, (((1,), (1,)), ((), ())), preferred_element_type=F32)


def tn(a, b):
    return lax.dot_general(a, b, (((0,), (0,)), ((), ())), preferred_element_type=F32)


def nn(a, b):
    return jnp.dot(a, b, preferred_element_type=F32)


def pad16(n):
    return -(-n // 16) * 16


def split(value):
    hi = value.astype(BF16).astype(F32)
    return hi, value - hi


def put_pair(ref, row, lanes, value):
    ref[row : row + 1, :lanes], ref[row : row + 1, lanes : 2 * lanes] = split(value)


def put_rows(ref, block, row, lanes, value):
    ref[block, row : row + 1, :lanes], ref[block, row + 1 : row + 2, :lanes] = split(value)


def rows_kernel(length_ref, lead_ref, cot_ref, pix_ref, out_ref, sums_ref, tmp_ref):
    rows, cw = cot_ref.shape
    vl = pix_ref.shape[0]
    vp = tmp_ref.shape[0] // 4
    row0 = lax.axis_index("patch") * rows
    sample = row0 // GROUP
    pos = row0 % GROUP + lax.broadcasted_iota(jnp.int32, cot_ref.shape, 0)
    kept = jnp.where(pos < length_ref[sample], cot_ref[...].astype(F32), 0.0)
    out_ref[:rows] = kept.astype(BF16)
    total = jnp.sum(kept, axis=0, keepdims=True)
    sums_ref[0:1, :] = total
    sums_ref[1:2, :] = total * (lead_ref[sample].astype(F32) / 100.0)
    tmp_ref[...] = jnp.zeros_like(tmp_ref)
    for v in range(vl):
        x = pix_ref[v].astype(F32)
        for p in range(4):
            tmp_ref[p * vp + v : p * vp + v + 1, :] = x[p : p + 1]
    for b in range(rows // cw):
        out_ref[rows + b * 4 * vp : rows + (b + 1) * 4 * vp, :] = tmp_ref[:, b * cw : (b + 1) * cw].astype(BF16)


def pack_kernel(eb, v_ref, k_ref, wq_ref, q_ref, e_ref, b_ref, l_ref, wo_ref, *refs):
    outs, wo_low_ref, tmp_ref = refs[:-2], refs[-2], refs[-1]
    wo_low_ref[0] = wo_ref[...].astype(BF16)
    cw = outs[0].shape[1]
    rl = v_ref.shape[0]
    _, vl, dp = e_ref.shape
    spare = 5 * vl
    j = lax.axis_index("var")
    q = jnp.broadcast_to(q_ref[...].astype(BF16), (16, rl))
    tmp_ref[...] = jnp.zeros_like(tmp_ref)
    for p in range(5):
        tmp_ref[p * vl : (p + 1) * vl, :dp] = e_ref[p]
    own = lax.broadcasted_iota(jnp.int32, (1, dp), 1) // rl == j
    for i, ref in enumerate((b_ref, l_ref)):
        tiled = jnp.concatenate([ref[...]] * (dp // rl), axis=1)
        tmp_ref[spare + 2 + i : spare + 3 + i, :dp] = jnp.where(own, tiled, 0.0)
    for k, out_ref in enumerate(outs):
        cols = pl.ds(pl.multiple_of((j ^ k) * cw, 128), cw)
        hi, lo = split(nn(q, wq_ref[:, cols].astype(BF16))[0:1])
        tmp_ref[spare : spare + 1, :] = hi
        tmp_ref[spare + 1 : spare + 2, :] = lo
        tmp_ref[eb : eb + rl, :] = k_ref[:, cols]
        tmp_ref[eb + rl : eb + 2 * rl, :] = v_ref[:, cols]
        out_ref[...] = tmp_ref[...].astype(BF16)


def place(ref, at, j, size, parts, lanes):
    if size % 16 == 0:
        for k, part in enumerate(parts):
            ref[pl.ds(pl.multiple_of((j ^ k) * size, size), size), lanes] = part
        return
    for s in range(len(parts)):
        value = parts[0]
        for k in range(1, len(parts)):
            value = jnp.where(j ^ k == s, parts[k], value)
        ref[s * size : (s + 1) * size, lanes] = value


def product_kernel(eb, vl, rl, dp, *refs):
    n = len(refs) - 5
    got, (sums_ref, out_ref, ekv_ref, w_ref, p_ref) = refs[:n], refs[n:]
    cw = got[0].shape[1]
    spare = 5 * vl
    lanes = -(-dp // 128) * 128
    p_id = lax.axis_index("patch")
    j = lax.axis_index("var")
    live = lax.broadcasted_iota(jnp.int32, (eb, dp), 0) < spare
    small = jnp.zeros((4, cw), F32)
    gs = [got[k][...].astype(F32) for k in range(n)]
    for k in range(n):
        small = small + gs[k][spare : spare + 4]
        at = pl.ds(pl.multiple_of((j ^ k) * eb, eb), eb)
        ekv_ref[at, :dp] = jnp.where(live, gs[k][:eb, :dp], 0.0).astype(BF16)
    for m in range(2):
        at = eb + m * rl
        place(w_ref, 0, j, rl, [g[at : at + rl] for g in gs], slice(m * cw, (m + 1) * cw))
    key, value = w_ref[:, :cw].astype(BF16), w_ref[:, cw:].astype(BF16)
    ekv_ref[:dp, lanes : lanes + cw] = key
    ekv_ref[dp : 2 * dp, lanes : lanes + cw] = value
    p_ref[...] = nn(ekv_ref[:, :dp], jnp.concatenate([value, key], axis=1))
    put_pair(p_ref, spare, cw, small[0:1] + small[1:2])
    put_pair(p_ref, spare + 1, cw, sums_ref[0:1])
    put_pair(p_ref, spare + 2, cw, sums_ref[1:2])
    per = cw // dp
    here = (lax.broadcasted_iota(jnp.int32, (1, cw), 1) // dp == p_id % per) & (p_id // per == j)
    for i in range(2):
        tiled = jnp.concatenate([small[2 + i : 3 + i, :dp]] * per, axis=1)
        p_ref[spare + 3 : spare + 4, i * cw : (i + 1) * cw] = jnp.where(here, tiled, 0.0)
    out_ref[...] = p_ref[...].astype(BF16)


def sum_kernel(vl, got_ref, out_ref):
    n_p, rc, lanes = got_ref.shape
    cw = lanes // 2
    total = got_ref[0].astype(F32)
    for s in range(1, n_p):
        total = total + got_ref[s].astype(F32)
    row = lax.axis_index("patch") * rc + lax.broadcasted_iota(jnp.int32, (rc, cw), 0)
    paired = (row >= 5 * vl) & (row < 5 * vl + 3)
    a, b = total[:, :cw], total[:, cw:]
    hi, lo = split(a + b)
    a, b = jnp.where(paired, hi, a).astype(BF16), jnp.where(paired, lo, b).astype(BF16)
    for s in range(n_p):
        out_ref[s, :, :cw] = a
        out_ref[s, :, cw:] = b


def forward_kernel(tile, eb, vk_ref, x_ref, avail_ref, att_ref, prob_ref, ef_ref, vw_ref, s_ref, vs_ref):
    nv, rows = x_ref.shape[1:]
    heads = prob_ref.shape[0]
    cw = att_ref.shape[0]
    n_j = vk_ref.shape[0] // eb
    vl = nv // n_j
    spare = 5 * vl
    j = lax.axis_index("var")
    for s in range(n_j):
        s_ref[s] = vk_ref[s * eb : (s + 1) * eb, :].astype(F32)
    q = (s_ref[0, spare : spare + 1, :cw] + s_ref[0, spare : spare + 1, cw:]) * SCALE
    for k in range(n_j):
        for p in range(5):
            vs_ref[p * nv + k * vl : p * nv + (k + 1) * vl, :] = s_ref[j ^ k, p * vl : (p + 1) * vl, :]
    vw_ref[...] = vs_ref[:, :cw].astype(BF16)
    for p in range(5):
        kq = vs_ref[p * nv : (p + 1) * nv, cw:] * q
        ef_ref[p] = jnp.concatenate(
            [jnp.sum(kq[:, h * HS : (h + 1) * HS], axis=1, keepdims=True) for h in range(heads)], axis=1
        )
    sample = lax.axis_index("patch") * rows // GROUP
    row = lax.broadcasted_iota(jnp.int32, (nv, nv), 0)
    shift = jnp.zeros((nv, nv), jnp.int32)
    for k in range(n_j):
        shift = jnp.where((row >= k * vl) & (row < (k + 1) * vl), ((j ^ k) - k) * vl, shift)
    same = row + shift == lax.broadcasted_iota(jnp.int32, (nv, nv), 1)
    flags = jnp.broadcast_to(avail_ref[pl.ds(sample, 1), :], (nv, nv))
    present = jnp.sum(jnp.where(same, flags.astype(F32), 0.0), axis=1, keepdims=True) > 0.5
    vw = [vw_ref[:, h * HS : (h + 1) * HS] for h in range(heads)]

    def step(i, carry):
        cols = pl.ds(pl.multiple_of(i * tile, tile), tile)
        xs = [x_ref[p, :, cols].astype(F32) for p in range(4)]
        for h in range(heads):
            s = jnp.broadcast_to(ef_ref[4, :, h : h + 1], (nv, tile))
            for p in range(4):
                s = s + ef_ref[p, :, h : h + 1] * xs[p]
            s = jnp.where(present, s, NEG)
            w = jnp.where(present, jnp.exp(s - jnp.max(s, axis=0, keepdims=True)), 0.0)
            prob = w / jnp.sum(w, axis=0, keepdims=True)
            prob_ref[h, :, cols] = prob
            a = jnp.concatenate([(prob * x).astype(BF16) for x in xs] + [prob.astype(BF16)], axis=0)
            att_ref[h * HS : (h + 1) * HS, cols] = tn(vw[h], a).astype(BF16)
        return carry

    lax.fori_loop(0, rows // tile, step, 0)


def reversed_bits(x, bits):
    out = 0
    for b in range(bits):
        out = out | (((x >> b) & 1) << (bits - 1 - b))
    return out


def pixel_kernel(vl, cw, *refs):
    bufs, (out_ref, x_ref) = refs[:-2], refs[-2:]
    rows = out_ref.shape[2]
    vp = (bufs[0].shape[0] - rows) // (4 * (rows // cw))
    for k, buf in enumerate(bufs):
        for b in range(rows // cw):
            at = rows + b * 4 * vp
            x = buf[at : at + 4 * vp, :].astype(F32)
            for p in range(4):
                x_ref[p, k * vl : (k + 1) * vl, b * cw : (b + 1) * cw] = x[p * vp : p * vp + vl]
    for p in range(4):
        out_ref[p] = x_ref[p].astype(BF16)


def weight_kernel(lo_ref, hi_ref, full_ref, *chunks):
    half, dp, cw = lo_ref.shape
    p_id = lax.axis_index("patch")
    j = lax.axis_index("var")
    for q in range(2 * half):
        block = reversed_bits(q ^ p_id, (2 * half).bit_length() - 1)
        at = slice(q * dp, (q + 1) * dp)

        @pl.when(block < half)
        def _(at=at, block=block):
            full_ref[at, :] = lo_ref[block]

        @pl.when(block >= half)
        def _(at=at, block=block):
            full_ref[at, :] = hi_ref[block - half]

    for k, ref in enumerate(chunks):
        ref[...] = full_ref[pl.ds(pl.multiple_of((j ^ (k + 1)) * cw, cw), cw), :]


def grad_kernel(n_j, full_ref, *refs):
    ws, cots, (out_ref,) = refs[: n_j - 1], refs[n_j - 1 : -1], refs[-1:]
    cw, rows = out_ref.shape
    j = lax.axis_index("var")
    own = full_ref[pl.ds(pl.multiple_of(j * cw, cw), cw), :]
    tile = 256
    for i in range(rows // tile):
        at = slice(i * tile, (i + 1) * tile)
        total = nt(own, cots[0][at, :])
        for k in range(1, n_j):
            total = total + nt(ws[k - 1][...], cots[k][at, :])
        out_ref[:, at] = total.astype(BF16)


def weight_grad_kernel(n_j, buf_ref, *refs):
    atts, (send_ref, keep_ref, tmp_ref) = refs[:n_j], refs[n_j:]
    cw, rows = atts[0].shape
    half, dp, _ = keep_ref.shape
    j = lax.axis_index("var")
    per = cw // dp
    for k in range(n_j):
        g = nn(atts[k][...], buf_ref[:rows, :]).astype(BF16)
        for t in range(per):
            tmp_ref[(j ^ k) * per + t] = g[t * dp : (t + 1) * dp]
    own = lax.axis_index("patch") & 1
    for b in range(half):
        send_ref[b * dp : (b + 1) * dp, :] = tmp_ref[2 * b + 1 - own]
        keep_ref[b] = tmp_ref[2 * b + own]


def halve_kernel(bit, g_ref, got_ref, *refs):
    count, dp, cw = g_ref.shape
    own = jnp.where(lax.axis_index("patch") & (2 * bit), 1, 0)

    def g_sum(b):
        at = pl.ds(pl.multiple_of(b * dp, dp), dp)
        return g_ref[b].astype(F32) + got_ref[at, :].astype(F32)

    if count == 1:
        pos_ref, out_ref, pos_out_ref = refs
        out_ref[...] = g_sum(0)
        pos_out_ref[...] = pos_ref[...].astype(F32)
        return
    send_ref, g_next = refs
    for b in range(g_next.shape[0]):
        send_ref[b * dp : (b + 1) * dp, :] = g_sum(2 * b + 1 - own).astype(BF16)
        g_next[b] = g_sum(2 * b + own).astype(BF16)


def pixel_add_kernel(keep_ref, got_ref, next_ref, send_ref):
    for i in range(next_ref.shape[0]):
        next_ref[i] = (keep_ref[2 * i].astype(F32) + got_ref[2 * i].astype(F32)).astype(BF16)
        send_ref[i] = (keep_ref[2 * i + 1].astype(F32) + got_ref[2 * i + 1].astype(F32)).astype(BF16)


def mixed_kernel(vl, n_j, length_ref, lead_ref, w_ref, vk_ref, plo_ref, phi_ref, *refs):
    atts, (out_ref, pos_ref) = refs[:n_j], refs[n_j:]
    rows, cw = out_ref.shape
    spare = 5 * vl
    base = pad16(spare) - 16
    row0 = lax.axis_index("patch") * rows
    sample = row0 // GROUP
    me = lax.axis_index("patch") // (GROUP // rows)
    j = lax.axis_index("var")
    half, per, _ = plo_ref.shape
    pos_ref[:half] = plo_ref[...]
    pos_ref[half:] = phi_ref[...]
    bl = vk_ref[base : base + 32, :].astype(F32)[spare - base + 3 : spare - base + 4]
    add = bl[:, :cw] + lead_ref[sample].astype(F32) / 100.0 * bl[:, cw:]
    for b in range(2 * half):
        at = slice(b * per, (b + 1) * per)
        total = add + pos_ref[reversed_bits(b ^ me, (2 * half).bit_length() - 1)].astype(F32)
        for k in range(n_j):
            w = w_ref[pl.ds(pl.multiple_of((j ^ k) * cw, cw), cw), :]
            total = total + tn(atts[k][:, at], w)
        pos = row0 % GROUP + b * per + lax.broadcasted_iota(jnp.int32, (per, cw), 0)
        out_ref[at, :] = jnp.where(pos < length_ref[sample], total, 0.0).astype(BF16)


def backward_kernel(tile, eb, n_j, vp, x_ref, ef_ref, vw_ref, prob_ref, grad_ref, *refs):
    outs, (z_ref, gv_ref, acc_ref, s_ref) = refs[:-4], refs[-4:]
    nv, rows = x_ref.shape[1:]
    heads = prob_ref.shape[0]
    vl = nv // n_j
    cw = gv_ref.shape[1]
    j = lax.axis_index("var")
    gv_ref[...] = jnp.zeros_like(gv_ref)
    acc_ref[...] = jnp.zeros_like(acc_ref)
    blank = jnp.zeros((vp - vl, tile), F32)

    def step(i, carry):
        cols = pl.ds(pl.multiple_of(i * tile, tile), tile)
        xs = [x_ref[p, :, cols].astype(F32) for p in range(4)]
        gx = [jnp.zeros((nv, tile), F32) for _ in range(4)]
        for h in range(heads):
            hc = slice(h * HS, (h + 1) * HS)
            prob = prob_ref[h, :, cols]
            gh = grad_ref[hc, cols]
            g = nn(vw_ref[:, hc], gh)
            gp = [g[p * nv : (p + 1) * nv] for p in range(5)]
            gprob = gp[4]
            for p in range(4):
                gprob = gprob + xs[p] * gp[p]
            inner = jnp.sum(prob * gprob, axis=0, keepdims=True)
            gs = prob * (gprob - inner)
            for p in range(4):
                gx[p] = gx[p] + prob * gp[p] + ef_ref[p, :, h : h + 1] * gs
            a = jnp.concatenate([(prob * x).astype(BF16) for x in xs] + [prob.astype(BF16)], axis=0)
            gv_ref[:, hc] += nt(a, gh)
            for p in range(5):
                t = gs if p == 4 else gs * xs[p]
                part = t[:, :128]
                for k in range(1, tile // 128):
                    part = part + t[:, k * 128 : (k + 1) * 128]
                acc_ref[p * heads + h] += part
        for k in range(n_j):
            ref = outs[k & 1].at[k >> 1]
            piece = jnp.concatenate([t for p in range(4) for t in (gx[p][k * vl : (k + 1) * vl], blank)], axis=0)
            ref[:, cols] = piece.astype(BF16)
        return carry

    lax.fori_loop(0, rows // tile, step, 0)
    s_ref[...] = jnp.zeros_like(s_ref)
    for p in range(5):
        gs = jnp.concatenate(
            [jnp.sum(acc_ref[p * heads + h], axis=1, keepdims=True) for h in range(heads)], axis=1
        )
        hi, lo = split(gs)
        pair = jnp.concatenate([hi, lo, jnp.zeros((nv, 128 - 2 * heads), F32)], axis=1)
        for k in range(n_j):
            at = slice(p * nv + k * vl, p * nv + (k + 1) * vl)
            s_ref[j ^ k, p * vl : (p + 1) * vl, :cw] = gv_ref[at, :]
            s_ref[j ^ k, p * vl : (p + 1) * vl, cw:] = pair[k * vl : (k + 1) * vl]
    for s in range(n_j):
        z_ref[s * eb : (s + 1) * eb, :] = s_ref[s].astype(BF16)


def sum_z_kernel(heads, got_ref, out_ref):
    n_p, rc, lanes = got_ref.shape
    cw = lanes - 128
    total = got_ref[0].astype(F32)
    for s in range(1, n_p):
        total = total + got_ref[s].astype(F32)
    main = total[:, :cw].astype(BF16)
    hi, lo = split(total[:, cw : cw + heads] + total[:, cw + heads : cw + 2 * heads])
    pair = jnp.concatenate([hi, lo, jnp.zeros((rc, 128 - 2 * heads), F32)], axis=1).astype(BF16)
    for s in range(n_p):
        out_ref[s, :, :cw] = main
        out_ref[s, :, cw:] = pair


def middle_kernel(eb, vl, n_j, dp, z_ref, vk_ref, ekv_ref, *refs):
    chunks, (g_ref, ge_ref, s_ref) = refs[:n_j], refs[n_j:]
    cw = z_ref.shape[1] - 128
    lanes = -(-dp // 128) * 128
    key, value = ekv_ref[:dp, lanes : lanes + cw], ekv_ref[dp : 2 * dp, lanes : lanes + cw]
    rl = dp // n_j
    heads = cw // HS
    spare = 5 * vl
    half = eb // 2
    j = lax.axis_index("var")
    base = pad16(spare) - 16
    small = vk_ref[base : base + 32, :].astype(F32)[spare - base : spare - base + 3]
    small = small[:, :cw] + small[:, cw:]
    qvec = small[0:1] * SCALE
    g = tn(ekv_ref[:, :dp], z_ref[...])
    gfold = g[:, cw : cw + heads] + g[:, cw + heads : cw + 2 * heads]
    g_ref[:, :cw] = g[:, :cw]
    g_ref[:, cw:] = jnp.concatenate(
        [gfold[:, h : h + 1] * qvec[:, h * HS : (h + 1) * HS] for h in range(heads)], axis=1
    )
    pair = z_ref[:, cw:].astype(F32)
    gs = pair[:, :heads] + pair[:, heads : 2 * heads]
    live = lax.broadcasted_iota(jnp.int32, (n_j * eb, 1), 0) % eb < spare
    ke = jnp.where(live, vk_ref[:, cw:].astype(F32), 0.0)
    gq = jnp.concatenate(
        [jnp.sum(ke[:, h * HS : (h + 1) * HS] * gs[:, h : h + 1], axis=0, keepdims=True) for h in range(heads)], axis=1
    ) * SCALE
    head = lax.broadcasted_iota(jnp.int32, (8, cw), 0) == lax.broadcasted_iota(jnp.int32, (8, cw), 1) // HS
    hi, lo = split(jnp.where(head, qvec, 0.0))
    fold = nt(hi.astype(BF16), key) + nt(lo.astype(BF16), key)
    ge = nt(z_ref[:, :cw], value)
    for h in range(heads):
        ge = ge + gs[:, h : h + 1] * fold[h : h + 1, :]
    ge_ref[...] = ge
    s_ref[...] = jnp.zeros_like(s_ref)
    at = 2 * rl + half
    for i, row in enumerate((gq, small[1:2], small[2:3])):
        s_ref[at + 2 * i : at + 2 * i + 1, :], s_ref[at + 2 * i + 1 : at + 2 * i + 2, :] = split(row)
    for k in range(n_j):
        rows = own_rows(g_ref, j ^ k, rl)
        s_ref[:rl, :] = rows[:, :cw]
        s_ref[rl : 2 * rl, :] = rows[:, cw:]
        block = ge_ref[pl.ds(pl.multiple_of((j ^ k) * eb, eb), eb), :]
        s_ref[2 * rl : 2 * rl + half, :dp] = block[:half]
        s_ref[2 * rl : 2 * rl + half, cw // 2 : cw // 2 + dp] = block[half:]
        chunks[k][...] = s_ref[...].astype(BF16)


def own_rows(ref, index, size):
    if size % 8 == 0:
        return ref[pl.ds(pl.multiple_of(index * size, size), size), :]
    out = ref[:size, :]
    for k in range(1, ref.shape[0] // size):
        out = jnp.where(index == k, ref[k * size : (k + 1) * size, :], out)
    return out


def final_kernel(eb, vl, rl, dp, n_j, wq_ref, q_ref, pk_ref, pg_ref, *refs):
    chunks, (gwv_ref, gwk_ref, gwq_ref, gq_ref, ge_ref, gb_ref, gl_ref, px_ref, f_ref, r_ref, s_ref, x_ref) = refs[:n_j], refs[n_j:]
    s_ref[...] = pk_ref[0].astype(F32) + pg_ref[0].astype(F32)
    vp = s_ref.shape[0] // 4
    for v in range(vl):
        for p in range(4):
            x_ref[4 * v + p : 4 * v + p + 1, :] = s_ref[p * vp + v : p * vp + v + 1, :]
    for v in range(vl):
        px_ref[v] = x_ref[4 * v : 4 * v + 4, :].astype(BF16)
    cw = chunks[0].shape[1]
    half = eb // 2
    j = lax.axis_index("var")
    at_out = lax.axis_index("patch") * n_j + j
    at = 2 * rl + half
    ge = jnp.zeros((half, cw), F32)
    gb = jnp.zeros((1, rl), F32)
    gl = jnp.zeros((1, rl), F32)
    for k in range(n_j):
        c = chunks[k][...].astype(F32)
        cols = pl.ds(pl.multiple_of((j ^ k) * cw, 128), cw)
        gwv_ref[:, cols] = c[:rl]
        gwk_ref[:, cols] = c[rl : 2 * rl]
        ge = ge + c[2 * rl : at]
        r_ref[0:1, cols] = c[at : at + 1] + c[at + 1 : at + 2]
        bias = c[at + 2 : at + 3] + c[at + 3 : at + 4]
        lead = c[at + 4 : at + 5] + c[at + 5 : at + 6]
        for g in range(cw // rl):
            here = at_out == (j ^ k) * (cw // rl) + g
            gb = gb + jnp.where(here, bias[:, g * rl : (g + 1) * rl], 0.0)
            gl = gl + jnp.where(here, lead[:, g * rl : (g + 1) * rl], 0.0)
    f_ref[:half, :] = ge[:, :dp]
    f_ref[half:, :] = ge[:, cw // 2 : cw // 2 + dp]
    for p in range(5):
        ge_ref[p] = f_ref[p * vl : (p + 1) * vl, :]
    gq = r_ref[0:1, :]
    gwq_ref[...] = q_ref[...].astype(BF16).astype(F32) * gq
    hi, lo = split(gq)
    wq = wq_ref[...].astype(BF16)
    both = jnp.concatenate([jnp.broadcast_to(hi, (8, D)), jnp.broadcast_to(lo, (8, D))], axis=0).astype(BF16)
    two = nt(both, wq)
    gq_ref[...] = two[0:1] + two[8:9]
    gb_ref[...] = gb
    gl_ref[...] = gl


def call(kernel, name, out_shape, args, scratch=(), us=0.01, smem=0, after=(), first=False, spill=(), hbm=0):
    n = len(args)
    in_vmem = pl.BlockSpec(memory_space=pltpu.VMEM)
    specs = [pl.BlockSpec(memory_space=pltpu.SMEM)] * smem + [pl.BlockSpec() if first else in_vmem] * (n - smem)
    specs[n - hbm :] = [pl.BlockSpec(memory_space=pl.ANY)] * hbm
    specs += [pl.BlockSpec(memory_space=pl.ANY)] * len(after)
    shapes = list(out_shape) if isinstance(out_shape, (list, tuple)) else [out_shape]
    outs = [pl.BlockSpec(memory_space=pltpu.HBM) if i in spill else in_vmem for i in range(len(shapes))]
    extra = [pltpu.VMEM(shapes[i].shape, shapes[i].dtype) for i in spill]
    if spill:
        extra.append(pltpu.SemaphoreType.DMA((len(spill),)))

    def body(*refs):
        ins, rest = refs[:n], refs[n + len(after) :]
        results, rest = list(rest[: len(shapes)]), rest[len(shapes) :]
        local, sems = rest[: len(spill)], rest[len(extra) - 1 : len(extra)]
        rest = rest[len(extra) :]
        copies = []
        for c, i in enumerate(spill):
            copies.append(pltpu.make_async_copy(local[c], results[i], sems[0].at[c]))
            results[i] = local[c]
        kernel(*ins, *results, *rest)
        for copy in copies:
            copy.start()
        for copy in copies:
            copy.wait()

    result = pl.pallas_call(
        body,
        out_shape=shapes,
        in_specs=specs,
        out_specs=outs,
        scratch_shapes=[*extra, *scratch],
        name=name,
        compiler_params=None if first else pltpu.CompilerParams(vmem_limit_bytes=12 << 20),
        cost_estimate=pl.CostEstimate(flops=int(us * 1.153e9), bytes_accessed=1 << 16, transcendentals=0),
    )(*args, *after)
    return result if isinstance(out_shape, (list, tuple)) else result[0]


def shape(dims, kind=F32):
    return jax.ShapeDtypeStruct(dims, kind)


def shards(pixels, embed, query, w_query, w_key, w_value, w_out, b_out, pos_embed, w_lead, avail, lengths, lead_hours, cotangent):
    n_p = lax.axis_size("patch")
    n_j = lax.axis_size("var")
    p_id = lax.axis_index("patch")
    vl, _, rows = pixels.shape
    nv = vl * n_j
    cw = w_out.shape[1]
    hl = cw // HS
    dp = embed.shape[2]
    rl = w_value.shape[0]
    eb = pad16(5 * vl + 4)
    nr = n_j * eb
    ch = pad16(eb + 2 * rl)
    vp = -(-vl // 8) * 8
    rc = nr // n_p
    others = range(1, n_j)

    *pack, wo_lo = call(
        functools.partial(pack_kernel, eb),
        "pack",
        [shape((ch, cw), BF16)] * n_j + [shape((1, dp, cw), BF16)],
        (w_value, w_key, w_query, query[None, :], embed.transpose(1, 0, 2), b_out[None, :], w_lead[None, :], w_out),
        [pltpu.VMEM((ch, cw), F32)],
        first=True,
    )
    got = [pack[0]] + [flip(pack[k], "var", k) for k in others]

    buf, sums = call(
        rows_kernel,
        "rows",
        (shape((rows + 4 * vp * (rows // cw), cw), BF16), shape((2, cw))),
        (lengths, lead_hours, cotangent, pixels),
        [pltpu.VMEM((4 * vp, rows), F32)],
        smem=2,
        after=(pack[0],),
    )

    bit = n_p // 2
    wo_hi = flip(wo_lo, "patch", bit)
    wo_steps = [wo_hi]
    while bit > 1:
        bit //= 2
        wo_lo = jnp.concatenate([gate(wo_lo, got[-1]), wo_hi], axis=0)
        wo_hi = flip(wo_lo, "patch", bit)
        wo_steps.append(wo_hi)

    part, ekv = call(
        functools.partial(product_kernel, eb, vl, rl, dp),
        "product",
        (shape((nr, 2 * cw), BF16), shape((nr, -(-dp // 128) * 128 + cw), BF16)),
        (*got, sums),
        [pltpu.VMEM((dp, 2 * cw), F32), pltpu.VMEM((nr, 2 * cw), F32)],
        us=0.01,
    )
    got2 = exchange(part, "patch").reshape(n_p, rc, 2 * cw)
    wo, *chunks = call(
        weight_kernel, "weight", [shape((D, cw), BF16)] + [shape((cw, cw), BF16)] * (n_j - 1), (wo_lo, wo_hi)
    )
    copies = call(functools.partial(sum_kernel, vl), "sum", shape((n_p, rc, 2 * cw), BF16), (got2,), after=(wo,))
    vk = exchange(copies.reshape(nr, 2 * cw), "patch")

    bufs = gather_var(gate(buf, part), lambda x: gate(x, copies))
    pix = call(
        functools.partial(pixel_kernel, vl, cw),
        "pixels",
        shape((4, nv, rows), BF16),
        bufs,
        [pltpu.VMEM((4, nv, rows), F32)],
    )

    chunks = [flip(c, "var", k + 1) for k, c in enumerate(chunks)]
    grad_att = call(
        functools.partial(grad_kernel, n_j), "grad_att", shape((cw, rows), BF16), (wo, *chunks, *bufs), after=(vk,)
    )

    parts = GROUP // rows
    owners = n_p // parts
    per = pos_embed.shape[0]
    there = [(k * owners + i, parts * i + k) for i in range(owners) for k in range(parts)]
    back = [(b, a) for a, b in there]
    pos_lo = lax.ppermute(gate(pos_embed, chunks[0]).astype(BF16), "patch", there)[None]
    att, prob, ef, vw = call(
        functools.partial(forward_kernel, 256, eb),
        "attention_forward",
        (shape((cw, rows), BF16), shape((hl, nv, rows)), shape((5, nv, hl)), shape((5 * nv, cw), BF16)),
        (vk, pix, avail),
        [pltpu.VMEM((n_j, eb, 2 * cw), F32), pltpu.VMEM((5 * nv, 2 * cw), F32)],
        after=(grad_att, pos_lo),
    )
    px_keep, px_send, z = call(
        functools.partial(backward_kernel, 256, eb, n_j, vp),
        "attention_backward",
        [shape((n_j // 2, 4 * vp, rows), BF16)] * 2 + [shape((nr, cw + 128), BF16)],
        (pix, ef, vw, prob, grad_att),
        [pltpu.VMEM((5 * nv, cw), F32), pltpu.VMEM((5 * hl, nv, 128), F32), pltpu.VMEM((n_j, eb, cw + 128), F32)],
    )

    got3 = exchange(z, "patch").reshape(n_p, rc, cw + 128)
    me = p_id // parts
    pos_hi = flip(gate(pos_lo, z), "patch", n_p // 2)
    g_rows = halve(gate(buf, z)[:rows].reshape(owners, per, cw), me % 2, parts)
    atts = [att] + [flip(gate(att, z), "var", k) for k in others]
    copies_z = call(functools.partial(sum_z_kernel, hl), "sum_z", shape((n_p, rc, cw + 128), BF16), (got3,), after=(g_rows[1],))
    zs = exchange(copies_z.reshape(nr, cw + 128), "patch")

    size = n_p // 2
    send, g_keep = call(
        functools.partial(weight_grad_kernel, n_j),
        "weight_grad",
        [shape((size * dp, cw), BF16), shape((size, dp, cw), BF16)],
        (buf, *atts),
        [pltpu.VMEM((n_p, dp, cw), BF16)],
        after=(copies_z,),
    )
    step = 1
    size //= 2
    send, g_keep = call(
        functools.partial(halve_kernel, step),
        "halve",
        [shape((size * dp, cw), BF16), shape((size, dp, cw), BF16)],
        (g_keep, flip(send, "patch", step)),
    )
    first = send
    bit = n_p // 2
    while bit > parts:
        bit //= 2
        pos_lo = jnp.concatenate([gate(pos_lo, copies_z), pos_hi], axis=0)
        pos_hi = flip(pos_lo, "patch", bit)
    turn = 2
    while turn < owners:
        g_rows = halve(gate(joined(*g_rows), copies_z), (me // turn) % 2, parts * turn)
        turn *= 2
    px_got = flip(gate(px_send, copies_z), "var", 1)
    fh = pad16(2 * rl + eb // 2 + 6)
    last = call(
        functools.partial(middle_kernel, eb, vl, n_j, dp),
        "middle",
        [shape((fh, cw), BF16)] * n_j,
        (zs, vk, ekv),
        [pltpu.VMEM((dp, 2 * cw), F32), pltpu.VMEM((nr, dp), F32), pltpu.VMEM((fh, cw), F32)],
        after=(),
    )

    def late(x):
        return gate(x, last[0])

    while size > 1:
        size //= 2
        step *= 2
        send, g_keep = call(
            functools.partial(halve_kernel, step),
            "halve",
            [shape((size * dp, cw), BF16), shape((size, dp, cw), BF16)],
            (g_keep, flip(send, "patch", step)),
            after=(last[0],),
        )
    grad_pos = lax.ppermute(joined(g_rows[0], gate(g_rows[1], first)).reshape(per, cw), "patch", back)
    grad_w_out, grad_pos = call(
        functools.partial(halve_kernel, 2 * step),
        "halve",
        (shape((dp, cw)), shape((per, cw))),
        (g_keep, flip(send, "patch", 2 * step), grad_pos),
    )

    bit = 1
    while 2 * bit < n_j:
        bit *= 2
        px_keep, px_send = call(
            pixel_add_kernel,
            "pixel_add",
            [shape((n_j // (2 * bit), 4 * vp, rows), BF16)] * 2,
            (px_keep, px_got),
            after=(first,),
        )
        px_got = flip(px_send, "var", bit)
    mixed = call(
        functools.partial(mixed_kernel, vl, n_j),
        "mixed",
        shape((rows, cw), BF16),
        (lengths, lead_hours, wo, vk, pos_lo, pos_hi, *atts),
        [pltpu.VMEM((owners, per, cw), BF16)],
        smem=2,
        after=(first,),
    )

    last = [last[0]] + [flip(last[k], "var", k) for k in others]
    gwv, gwk, gwq, gq, ge, gb, gl, grad_pixels = call(
        functools.partial(final_kernel, eb, vl, rl, dp, n_j),
        "final",
        (
            shape((rl, D)),
            shape((rl, D)),
            shape((rl, D)),
            shape((1, rl)),
            shape((5, vl, dp)),
            shape((1, rl)),
            shape((1, rl)),
            shape((vl, 4, rows), BF16),
        ),
        (w_query, query[:, None], px_keep, px_got, *last),
        [pltpu.VMEM((eb, dp), F32), pltpu.VMEM((8, D), F32), pltpu.VMEM((4 * vp, rows), F32), pltpu.VMEM((4 * vl, rows), F32)],
        after=(send,),
    )
    return (
        mixed,
        grad_pixels,
        ge.transpose(1, 0, 2),
        gq.reshape(rl),
        gwq,
        gwk,
        gwv,
        grad_w_out,
        gb.reshape(rl),
        grad_pos,
        gl.reshape(rl),
    )


def solution(mesh):
    both = P(("patch", "var"))
    rows2 = P(("patch", "var"), None)
    return jax.shard_map(
        shards,
        mesh=mesh,
        in_specs=(
            P("var", None, "patch"),
            P("var", None, "patch"),
            both,
            rows2,
            rows2,
            rows2,
            P("patch", "var"),
            both,
            P("patch", "var"),
            both,
            P(),
            P(),
            P(),
            P("patch", "var"),
        ),
        out_specs=(
            P("patch", "var"),
            P("var", None, "patch"),
            P("var", None, "patch"),
            both,
            rows2,
            rows2,
            rows2,
            P("patch", "var"),
            both,
            P("patch", "var"),
            both,
        ),
        check_vma=False,
    )
```

```python
import functools
import math

import jax
import jax.numpy as jnp
from jax import lax
from jax.experimental import pallas as pl
from jax.experimental.pallas import tpu as pltpu
from jax.sharding import PartitionSpec as P

D = 1024
HEADS = 16
HS = D // HEADS
GROUP = 2048
F32 = jnp.float32
BF16 = jnp.bfloat16
NEG = -1e30
SCALE = 1.0 / math.sqrt(HS)


def exchange(x, axis):
    return lax.all_to_all(x, axis, 0, 0, tiled=True)


def flip(x, axis, bit):
    n = lax.axis_size(axis)
    return lax.ppermute(x, axis, [(i, i ^ bit) for i in range(n)])


def gate(x, after):
    return lax.optimization_barrier((x, after))[0]


def gather_var(x, last):
    n = lax.axis_size("var")
    blocks = {0: x}
    bit = n // 2
    while bit:
        for k, block in list(blocks.items()):
            blocks[k | bit] = flip(last(block) if bit == 1 and k else block, "var", bit)
        bit //= 2
    return [blocks[k] for k in range(n)]


def halve(x, bit, step):
    pair = x.reshape(x.shape[0] // 2, 2, *x.shape[1:])
    send = lax.dynamic_index_in_dim(pair, 1 - bit, 1, False)
    keep = lax.dynamic_index_in_dim(pair, bit, 1, False)
    return keep, flip(send, "patch", step)


def joined(keep, got):
    return (keep.astype(F32) + got.astype(F32)).astype(BF16)


def nt(a, b):
    return lax.dot_general(a, b, (((1,), (1,)), ((), ())), preferred_element_type=F32)


def tn(a, b):
    return lax.dot_general(a, b, (((0,), (0,)), ((), ())), preferred_element_type=F32)


def nn(a, b):
    return jnp.dot(a, b, preferred_element_type=F32)


def pad16(n):
    return -(-n // 16) * 16


def split(value):
    hi = value.astype(BF16).astype(F32)
    return hi, value - hi


def put_pair(ref, row, lanes, value):
    ref[row : row + 1, :lanes], ref[row : row + 1, lanes : 2 * lanes] = split(value)


def put_rows(ref, block, row, lanes, value):
    ref[block, row : row + 1, :lanes], ref[block, row + 1 : row + 2, :lanes] = split(value)


def rows_kernel(length_ref, lead_ref, cot_ref, pix_ref, out_ref, sums_ref, tmp_ref):
    rows, cw = cot_ref.shape
    vl = pix_ref.shape[0]
    vp = tmp_ref.shape[0] // 4
    row0 = lax.axis_index("patch") * rows
    sample = row0 // GROUP
    pos = row0 % GROUP + lax.broadcasted_iota(jnp.int32, cot_ref.shape, 0)
    kept = jnp.where(pos < length_ref[sample], cot_ref[...].astype(F32), 0.0)
    out_ref[:rows] = kept.astype(BF16)
    total = jnp.sum(kept, axis=0, keepdims=True)
    sums_ref[0:1, :] = total
    sums_ref[1:2, :] = total * (lead_ref[sample].astype(F32) / 100.0)
    tmp_ref[...] = jnp.zeros_like(tmp_ref)
    for v in range(vl):
        x = pix_ref[v].astype(F32)
        for p in range(4):
            tmp_ref[p * vp + v : p * vp + v + 1, :] = x[p : p + 1]
    for b in range(rows // cw):
        out_ref[rows + b * 4 * vp : rows + (b + 1) * 4 * vp, :] = tmp_ref[:, b * cw : (b + 1) * cw].astype(BF16)


def pack_kernel(eb, v_ref, k_ref, wq_ref, q_ref, e_ref, b_ref, l_ref, wo_ref, *refs):
    outs, wo_low_ref, tmp_ref = refs[:-2], refs[-2], refs[-1]
    wo_low_ref[0] = wo_ref[...].astype(BF16)
    cw = outs[0].shape[1]
    rl = v_ref.shape[0]
    _, vl, dp = e_ref.shape
    spare = 5 * vl
    j = lax.axis_index("var")
    q = jnp.broadcast_to(q_ref[...].astype(BF16), (16, rl))
    tmp_ref[...] = jnp.zeros_like(tmp_ref)
    for p in range(5):
        tmp_ref[p * vl : (p + 1) * vl, :dp] = e_ref[p]
    own = lax.broadcasted_iota(jnp.int32, (1, dp), 1) // rl == j
    for i, ref in enumerate((b_ref, l_ref)):
        tiled = jnp.concatenate([ref[...]] * (dp // rl), axis=1)
        tmp_ref[spare + 2 + i : spare + 3 + i, :dp] = jnp.where(own, tiled, 0.0)
    for k, out_ref in enumerate(outs):
        cols = pl.ds(pl.multiple_of((j ^ k) * cw, 128), cw)
        hi, lo = split(nn(q, wq_ref[:, cols].astype(BF16))[0:1])
        tmp_ref[spare : spare + 1, :] = hi
        tmp_ref[spare + 1 : spare + 2, :] = lo
        tmp_ref[eb : eb + rl, :] = k_ref[:, cols]
        tmp_ref[eb + rl : eb + 2 * rl, :] = v_ref[:, cols]
        out_ref[...] = tmp_ref[...].astype(BF16)


def place(ref, at, j, size, parts, lanes):
    if size % 16 == 0:
        for k, part in enumerate(parts):
            ref[pl.ds(pl.multiple_of((j ^ k) * size, size), size), lanes] = part
        return
    for s in range(len(parts)):
        value = parts[0]
        for k in range(1, len(parts)):
            value = jnp.where(j ^ k == s, parts[k], value)
        ref[s * size : (s + 1) * size, lanes] = value


def product_kernel(eb, vl, rl, dp, *refs):
    n = len(refs) - 5
    got, (sums_ref, out_ref, ekv_ref, w_ref, p_ref) = refs[:n], refs[n:]
    cw = got[0].shape[1]
    spare = 5 * vl
    lanes = -(-dp // 128) * 128
    p_id = lax.axis_index("patch")
    j = lax.axis_index("var")
    live = lax.broadcasted_iota(jnp.int32, (eb, dp), 0) < spare
    small = jnp.zeros((4, cw), F32)
    gs = [got[k][...].astype(F32) for k in range(n)]
    for k in range(n):
        small = small + gs[k][spare : spare + 4]
        at = pl.ds(pl.multiple_of((j ^ k) * eb, eb), eb)
        ekv_ref[at, :dp] = jnp.where(live, gs[k][:eb, :dp], 0.0).astype(BF16)
    for m in range(2):
        at = eb + m * rl
        place(w_ref, 0, j, rl, [g[at : at + rl] for g in gs], slice(m * cw, (m + 1) * cw))
    key, value = w_ref[:, :cw].astype(BF16), w_ref[:, cw:].astype(BF16)
    ekv_ref[:dp, lanes : lanes + cw] = key
    ekv_ref[dp : 2 * dp, lanes : lanes + cw] = value
    p_ref[...] = nn(ekv_ref[:, :dp], jnp.concatenate([value, key], axis=1))
    put_pair(p_ref, spare, cw, small[0:1] + small[1:2])
    put_pair(p_ref, spare + 1, cw, sums_ref[0:1])
    put_pair(p_ref, spare + 2, cw, sums_ref[1:2])
    per = cw // dp
    here = (lax.broadcasted_iota(jnp.int32, (1, cw), 1) // dp == p_id % per) & (p_id // per == j)
    for i in range(2):
        tiled = jnp.concatenate([small[2 + i : 3 + i, :dp]] * per, axis=1)
        p_ref[spare + 3 : spare + 4, i * cw : (i + 1) * cw] = jnp.where(here, tiled, 0.0)
    out_ref[...] = p_ref[...].astype(BF16)


def sum_kernel(vl, got_ref, out_ref):
    n_p, rc, lanes = got_ref.shape
    cw = lanes // 2
    total = got_ref[0].astype(F32)
    for s in range(1, n_p):
        total = total + got_ref[s].astype(F32)
    row = lax.axis_index("patch") * rc + lax.broadcasted_iota(jnp.int32, (rc, cw), 0)
    paired = (row >= 5 * vl) & (row < 5 * vl + 3)
    a, b = total[:, :cw], total[:, cw:]
    hi, lo = split(a + b)
    a, b = jnp.where(paired, hi, a).astype(BF16), jnp.where(paired, lo, b).astype(BF16)
    for s in range(n_p):
        out_ref[s, :, :cw] = a
        out_ref[s, :, cw:] = b


def forward_kernel(tile, eb, vk_ref, x_ref, avail_ref, att_ref, prob_ref, ef_ref, vw_ref, s_ref, vs_ref):
    nv, rows = x_ref.shape[1:]
    heads = prob_ref.shape[0]
    cw = att_ref.shape[0]
    n_j = vk_ref.shape[0] // eb
    vl = nv // n_j
    spare = 5 * vl
    j = lax.axis_index("var")
    for s in range(n_j):
        s_ref[s] = vk_ref[s * eb : (s + 1) * eb, :].astype(F32)
    q = (s_ref[0, spare : spare + 1, :cw] + s_ref[0, spare : spare + 1, cw:]) * SCALE
    for k in range(n_j):
        for p in range(5):
            vs_ref[p * nv + k * vl : p * nv + (k + 1) * vl, :] = s_ref[j ^ k, p * vl : (p + 1) * vl, :]
    vw_ref[...] = vs_ref[:, :cw].astype(BF16)
    for p in range(5):
        kq = vs_ref[p * nv : (p + 1) * nv, cw:] * q
        ef_ref[p] = jnp.concatenate(
            [jnp.sum(kq[:, h * HS : (h + 1) * HS], axis=1, keepdims=True) for h in range(heads)], axis=1
        )
    sample = lax.axis_index("patch") * rows // GROUP
    row = lax.broadcasted_iota(jnp.int32, (nv, nv), 0)
    shift = jnp.zeros((nv, nv), jnp.int32)
    for k in range(n_j):
        shift = jnp.where((row >= k * vl) & (row < (k + 1) * vl), ((j ^ k) - k) * vl, shift)
    same = row + shift == lax.broadcasted_iota(jnp.int32, (nv, nv), 1)
    flags = jnp.broadcast_to(avail_ref[pl.ds(sample, 1), :], (nv, nv))
    present = jnp.sum(jnp.where(same, flags.astype(F32), 0.0), axis=1, keepdims=True) > 0.5
    vw = [vw_ref[:, h * HS : (h + 1) * HS] for h in range(heads)]

    def step(i, carry):
        cols = pl.ds(pl.multiple_of(i * tile, tile), tile)
        xs = [x_ref[p, :, cols].astype(F32) for p in range(4)]
        for h in range(heads):
            s = jnp.broadcast_to(ef_ref[4, :, h : h + 1], (nv, tile))
            for p in range(4):
                s = s + ef_ref[p, :, h : h + 1] * xs[p]
            s = jnp.where(present, s, NEG)
            w = jnp.where(present, jnp.exp(s - jnp.max(s, axis=0, keepdims=True)), 0.0)
            prob = w / jnp.sum(w, axis=0, keepdims=True)
            prob_ref[h, :, cols] = prob
            a = jnp.concatenate([(prob * x).astype(BF16) for x in xs] + [prob.astype(BF16)], axis=0)
            att_ref[h * HS : (h + 1) * HS, cols] = tn(vw[h], a).astype(BF16)
        return carry

    lax.fori_loop(0, rows // tile, step, 0)


def reversed_bits(x, bits):
    out = 0
    for b in range(bits):
        out = out | (((x >> b) & 1) << (bits - 1 - b))
    return out


def pixel_kernel(vl, cw, *refs):
    bufs, (out_ref, x_ref) = refs[:-2], refs[-2:]
    rows = out_ref.shape[2]
    vp = (bufs[0].shape[0] - rows) // (4 * (rows // cw))
    for k, buf in enumerate(bufs):
        for b in range(rows // cw):
            at = rows + b * 4 * vp
            x = buf[at : at + 4 * vp, :].astype(F32)
            for p in range(4):
                x_ref[p, k * vl : (k + 1) * vl, b * cw : (b + 1) * cw] = x[p * vp : p * vp + vl]
    for p in range(4):
        out_ref[p] = x_ref[p].astype(BF16)


def weight_kernel(lo_ref, hi_ref, full_ref, *chunks):
    half, dp, cw = lo_ref.shape
    p_id = lax.axis_index("patch")
    j = lax.axis_index("var")
    for q in range(2 * half):
        block = reversed_bits(q ^ p_id, (2 * half).bit_length() - 1)
        at = slice(q * dp, (q + 1) * dp)

        @pl.when(block < half)
        def _(at=at, block=block):
            full_ref[at, :] = lo_ref[block]

        @pl.when(block >= half)
        def _(at=at, block=block):
            full_ref[at, :] = hi_ref[block - half]

    for k, ref in enumerate(chunks):
        ref[...] = full_ref[pl.ds(pl.multiple_of((j ^ (k + 1)) * cw, cw), cw), :]


def grad_kernel(n_j, full_ref, *refs):
    ws, cots, (out_ref,) = refs[: n_j - 1], refs[n_j - 1 : -1], refs[-1:]
    cw, rows = out_ref.shape
    j = lax.axis_index("var")
    own = full_ref[pl.ds(pl.multiple_of(j * cw, cw), cw), :]
    tile = 256
    for i in range(rows // tile):
        at = slice(i * tile, (i + 1) * tile)
        total = nt(own, cots[0][at, :])
        for k in range(1, n_j):
            total = total + nt(ws[k - 1][...], cots[k][at, :])
        out_ref[:, at] = total.astype(BF16)


def weight_grad_kernel(n_j, buf_ref, *refs):
    atts, (send_ref, keep_ref, tmp_ref) = refs[:n_j], refs[n_j:]
    cw, rows = atts[0].shape
    half, dp, _ = keep_ref.shape
    j = lax.axis_index("var")
    per = cw // dp
    for k in range(n_j):
        g = nn(atts[k][...], buf_ref[:rows, :]).astype(BF16)
        for t in range(per):
            tmp_ref[(j ^ k) * per + t] = g[t * dp : (t + 1) * dp]
    own = lax.axis_index("patch") & 1
    for b in range(half):
        send_ref[b * dp : (b + 1) * dp, :] = tmp_ref[2 * b + 1 - own]
        keep_ref[b] = tmp_ref[2 * b + own]


def halve_kernel(bit, g_ref, got_ref, *refs):
    count, dp, cw = g_ref.shape
    own = jnp.where(lax.axis_index("patch") & (2 * bit), 1, 0)

    def g_sum(b):
        at = pl.ds(pl.multiple_of(b * dp, dp), dp)
        return g_ref[b].astype(F32) + got_ref[at, :].astype(F32)

    if count == 1:
        pos_ref, out_ref, pos_out_ref = refs
        out_ref[...] = g_sum(0)
        pos_out_ref[...] = pos_ref[...].astype(F32)
        return
    send_ref, g_next = refs
    for b in range(g_next.shape[0]):
        send_ref[b * dp : (b + 1) * dp, :] = g_sum(2 * b + 1 - own).astype(BF16)
        g_next[b] = g_sum(2 * b + own).astype(BF16)


def pixel_add_kernel(keep_ref, got_ref, next_ref, send_ref):
    for i in range(next_ref.shape[0]):
        next_ref[i] = (keep_ref[2 * i].astype(F32) + got_ref[2 * i].astype(F32)).astype(BF16)
        send_ref[i] = (keep_ref[2 * i + 1].astype(F32) + got_ref[2 * i + 1].astype(F32)).astype(BF16)


def mixed_kernel(vl, n_j, length_ref, lead_ref, w_ref, vk_ref, plo_ref, phi_ref, *refs):
    atts, (out_ref, pos_ref) = refs[:n_j], refs[n_j:]
    rows, cw = out_ref.shape
    spare = 5 * vl
    base = pad16(spare) - 16
    row0 = lax.axis_index("patch") * rows
    sample = row0 // GROUP
    me = lax.axis_index("patch") // (GROUP // rows)
    j = lax.axis_index("var")
    half, per, _ = plo_ref.shape
    pos_ref[:half] = plo_ref[...]
    pos_ref[half:] = phi_ref[...]
    bl = vk_ref[base : base + 32, :].astype(F32)[spare - base + 3 : spare - base + 4]
    add = bl[:, :cw] + lead_ref[sample].astype(F32) / 100.0 * bl[:, cw:]
    for b in range(2 * half):
        at = slice(b * per, (b + 1) * per)
        total = add + pos_ref[reversed_bits(b ^ me, (2 * half).bit_length() - 1)].astype(F32)
        for k in range(n_j):
            w = w_ref[pl.ds(pl.multiple_of((j ^ k) * cw, cw), cw), :]
            total = total + tn(atts[k][:, at], w)
        pos = row0 % GROUP + b * per + lax.broadcasted_iota(jnp.int32, (per, cw), 0)
        out_ref[at, :] = jnp.where(pos < length_ref[sample], total, 0.0).astype(BF16)


def backward_kernel(tile, eb, n_j, vp, x_ref, ef_ref, vw_ref, prob_ref, grad_ref, *refs):
    outs, (z_ref, gv_ref, acc_ref, s_ref) = refs[:-4], refs[-4:]
    nv, rows = x_ref.shape[1:]
    heads = prob_ref.shape[0]
    vl = nv // n_j
    cw = gv_ref.shape[1]
    j = lax.axis_index("var")
    gv_ref[...] = jnp.zeros_like(gv_ref)
    acc_ref[...] = jnp.zeros_like(acc_ref)
    blank = jnp.zeros((vp - vl, tile), F32)

    def step(i, carry):
        cols = pl.ds(pl.multiple_of(i * tile, tile), tile)
        xs = [x_ref[p, :, cols].astype(F32) for p in range(4)]
        gx = [jnp.zeros((nv, tile), F32) for _ in range(4)]
        for h in range(heads):
            hc = slice(h * HS, (h + 1) * HS)
            prob = prob_ref[h, :, cols]
            gh = grad_ref[hc, cols]
            g = nn(vw_ref[:, hc], gh)
            gp = [g[p * nv : (p + 1) * nv] for p in range(5)]
            gprob = gp[4]
            for p in range(4):
                gprob = gprob + xs[p] * gp[p]
            inner = jnp.sum(prob * gprob, axis=0, keepdims=True)
            gs = prob * (gprob - inner)
            for p in range(4):
                gx[p] = gx[p] + prob * gp[p] + ef_ref[p, :, h : h + 1] * gs
            a = jnp.concatenate([(prob * x).astype(BF16) for x in xs] + [prob.astype(BF16)], axis=0)
            gv_ref[:, hc] += nt(a, gh)
            for p in range(5):
                t = gs if p == 4 else gs * xs[p]
                part = t[:, :128]
                for k in range(1, tile // 128):
                    part = part + t[:, k * 128 : (k + 1) * 128]
                acc_ref[p * heads + h] += part
        for k in range(n_j):
            ref = outs[k & 1].at[k >> 1]
            piece = jnp.concatenate([t for p in range(4) for t in (gx[p][k * vl : (k + 1) * vl], blank)], axis=0)
            ref[:, cols] = piece.astype(BF16)
        return carry

    lax.fori_loop(0, rows // tile, step, 0)
    s_ref[...] = jnp.zeros_like(s_ref)
    for p in range(5):
        gs = jnp.concatenate(
            [jnp.sum(acc_ref[p * heads + h], axis=1, keepdims=True) for h in range(heads)], axis=1
        )
        hi, lo = split(gs)
        pair = jnp.concatenate([hi, lo, jnp.zeros((nv, 128 - 2 * heads), F32)], axis=1)
        for k in range(n_j):
            at = slice(p * nv + k * vl, p * nv + (k + 1) * vl)
            s_ref[j ^ k, p * vl : (p + 1) * vl, :cw] = gv_ref[at, :]
            s_ref[j ^ k, p * vl : (p + 1) * vl, cw:] = pair[k * vl : (k + 1) * vl]
    for s in range(n_j):
        z_ref[s * eb : (s + 1) * eb, :] = s_ref[s].astype(BF16)


def sum_z_kernel(heads, got_ref, out_ref):
    n_p, rc, lanes = got_ref.shape
    cw = lanes - 128
    total = got_ref[0].astype(F32)
    for s in range(1, n_p):
        total = total + got_ref[s].astype(F32)
    main = total[:, :cw].astype(BF16)
    hi, lo = split(total[:, cw : cw + heads] + total[:, cw + heads : cw + 2 * heads])
    pair = jnp.concatenate([hi, lo, jnp.zeros((rc, 128 - 2 * heads), F32)], axis=1).astype(BF16)
    for s in range(n_p):
        out_ref[s, :, :cw] = main
        out_ref[s, :, cw:] = pair


def middle_kernel(eb, vl, n_j, dp, z_ref, vk_ref, ekv_ref, *refs):
    chunks, (g_ref, ge_ref, s_ref) = refs[:n_j], refs[n_j:]
    cw = z_ref.shape[1] - 128
    lanes = -(-dp // 128) * 128
    key, value = ekv_ref[:dp, lanes : lanes + cw], ekv_ref[dp : 2 * dp, lanes : lanes + cw]
    rl = dp // n_j
    heads = cw // HS
    spare = 5 * vl
    half = eb // 2
    j = lax.axis_index("var")
    base = pad16(spare) - 16
    small = vk_ref[base : base + 32, :].astype(F32)[spare - base : spare - base + 3]
    small = small[:, :cw] + small[:, cw:]
    qvec = small[0:1] * SCALE
    g = tn(ekv_ref[:, :dp], z_ref[...])
    gfold = g[:, cw : cw + heads] + g[:, cw + heads : cw + 2 * heads]
    g_ref[:, :cw] = g[:, :cw]
    g_ref[:, cw:] = jnp.concatenate(
        [gfold[:, h : h + 1] * qvec[:, h * HS : (h + 1) * HS] for h in range(heads)], axis=1
    )
    pair = z_ref[:, cw:].astype(F32)
    gs = pair[:, :heads] + pair[:, heads : 2 * heads]
    live = lax.broadcasted_iota(jnp.int32, (n_j * eb, 1), 0) % eb < spare
    ke = jnp.where(live, vk_ref[:, cw:].astype(F32), 0.0)
    gq = jnp.concatenate(
        [jnp.sum(ke[:, h * HS : (h + 1) * HS] * gs[:, h : h + 1], axis=0, keepdims=True) for h in range(heads)], axis=1
    ) * SCALE
    head = lax.broadcasted_iota(jnp.int32, (8, cw), 0) == lax.broadcasted_iota(jnp.int32, (8, cw), 1) // HS
    hi, lo = split(jnp.where(head, qvec, 0.0))
    fold = nt(hi.astype(BF16), key) + nt(lo.astype(BF16), key)
    ge = nt(z_ref[:, :cw], value)
    for h in range(heads):
        ge = ge + gs[:, h : h + 1] * fold[h : h + 1, :]
    ge_ref[...] = ge
    s_ref[...] = jnp.zeros_like(s_ref)
    at = 2 * rl + half
    for i, row in enumerate((gq, small[1:2], small[2:3])):
        s_ref[at + 2 * i : at + 2 * i + 1, :], s_ref[at + 2 * i + 1 : at + 2 * i + 2, :] = split(row)
    for k in range(n_j):
        rows = own_rows(g_ref, j ^ k, rl)
        s_ref[:rl, :] = rows[:, :cw]
        s_ref[rl : 2 * rl, :] = rows[:, cw:]
        block = ge_ref[pl.ds(pl.multiple_of((j ^ k) * eb, eb), eb), :]
        s_ref[2 * rl : 2 * rl + half, :dp] = block[:half]
        s_ref[2 * rl : 2 * rl + half, cw // 2 : cw // 2 + dp] = block[half:]
        chunks[k][...] = s_ref[...].astype(BF16)


def own_rows(ref, index, size):
    if size % 8 == 0:
        return ref[pl.ds(pl.multiple_of(index * size, size), size), :]
    out = ref[:size, :]
    for k in range(1, ref.shape[0] // size):
        out = jnp.where(index == k, ref[k * size : (k + 1) * size, :], out)
    return out


def final_kernel(eb, vl, rl, dp, n_j, wq_ref, q_ref, pk_ref, pg_ref, *refs):
    chunks, (gwv_ref, gwk_ref, gwq_ref, gq_ref, ge_ref, gb_ref, gl_ref, px_ref, f_ref, r_ref, s_ref, x_ref) = refs[:n_j], refs[n_j:]
    s_ref[...] = pk_ref[0].astype(F32) + pg_ref[0].astype(F32)
    vp = s_ref.shape[0] // 4
    for v in range(vl):
        for p in range(4):
            x_ref[4 * v + p : 4 * v + p + 1, :] = s_ref[p * vp + v : p * vp + v + 1, :]
    for v in range(vl):
        px_ref[v] = x_ref[4 * v : 4 * v + 4, :].astype(BF16)
    cw = chunks[0].shape[1]
    half = eb // 2
    j = lax.axis_index("var")
    at_out = lax.axis_index("patch") * n_j + j
    at = 2 * rl + half
    ge = jnp.zeros((half, cw), F32)
    gb = jnp.zeros((1, rl), F32)
    gl = jnp.zeros((1, rl), F32)
    for k in range(n_j):
        c = chunks[k][...].astype(F32)
        cols = pl.ds(pl.multiple_of((j ^ k) * cw, 128), cw)
        gwv_ref[:, cols] = c[:rl]
        gwk_ref[:, cols] = c[rl : 2 * rl]
        ge = ge + c[2 * rl : at]
        r_ref[0:1, cols] = c[at : at + 1] + c[at + 1 : at + 2]
        bias = c[at + 2 : at + 3] + c[at + 3 : at + 4]
        lead = c[at + 4 : at + 5] + c[at + 5 : at + 6]
        for g in range(cw // rl):
            here = at_out == (j ^ k) * (cw // rl) + g
            gb = gb + jnp.where(here, bias[:, g * rl : (g + 1) * rl], 0.0)
            gl = gl + jnp.where(here, lead[:, g * rl : (g + 1) * rl], 0.0)
    f_ref[:half, :] = ge[:, :dp]
    f_ref[half:, :] = ge[:, cw // 2 : cw // 2 + dp]
    for p in range(5):
        ge_ref[p] = f_ref[p * vl : (p + 1) * vl, :]
    gq = r_ref[0:1, :]
    gwq_ref[...] = q_ref[...].astype(BF16).astype(F32) * gq
    hi, lo = split(gq)
    wq = wq_ref[...].astype(BF16)
    both = jnp.concatenate([jnp.broadcast_to(hi, (8, D)), jnp.broadcast_to(lo, (8, D))], axis=0).astype(BF16)
    two = nt(both, wq)
    gq_ref[...] = two[0:1] + two[8:9]
    gb_ref[...] = gb
    gl_ref[...] = gl


def call(kernel, name, out_shape, args, scratch=(), us=0.01, smem=0, after=(), first=False, spill=(), hbm=0):
    n = len(args)
    in_vmem = pl.BlockSpec(memory_space=pltpu.VMEM)
    specs = [pl.BlockSpec(memory_space=pltpu.SMEM)] * smem + [pl.BlockSpec() if first else in_vmem] * (n - smem)
    specs[n - hbm :] = [pl.BlockSpec(memory_space=pl.ANY)] * hbm
    specs += [pl.BlockSpec(memory_space=pl.ANY)] * len(after)
    shapes = list(out_shape) if isinstance(out_shape, (list, tuple)) else [out_shape]
    outs = [pl.BlockSpec(memory_space=pltpu.HBM) if i in spill else in_vmem for i in range(len(shapes))]
    extra = [pltpu.VMEM(shapes[i].shape, shapes[i].dtype) for i in spill]
    if spill:
        extra.append(pltpu.SemaphoreType.DMA((len(spill),)))

    def body(*refs):
        ins, rest = refs[:n], refs[n + len(after) :]
        results, rest = list(rest[: len(shapes)]), rest[len(shapes) :]
        local, sems = rest[: len(spill)], rest[len(extra) - 1 : len(extra)]
        rest = rest[len(extra) :]
        copies = []
        for c, i in enumerate(spill):
            copies.append(pltpu.make_async_copy(local[c], results[i], sems[0].at[c]))
            results[i] = local[c]
        kernel(*ins, *results, *rest)
        for copy in copies:
            copy.start()
        for copy in copies:
            copy.wait()

    result = pl.pallas_call(
        body,
        out_shape=shapes,
        in_specs=specs,
        out_specs=outs,
        scratch_shapes=[*extra, *scratch],
        name=name,
        compiler_params=None if first else pltpu.CompilerParams(vmem_limit_bytes=12 << 20),
        cost_estimate=pl.CostEstimate(flops=int(us * 1.153e9), bytes_accessed=1 << 16, transcendentals=0),
    )(*args, *after)
    return result if isinstance(out_shape, (list, tuple)) else result[0]


def shape(dims, kind=F32):
    return jax.ShapeDtypeStruct(dims, kind)


def shards(pixels, embed, query, w_query, w_key, w_value, w_out, b_out, pos_embed, w_lead, avail, lengths, lead_hours, cotangent):
    n_p = lax.axis_size("patch")
    n_j = lax.axis_size("var")
    p_id = lax.axis_index("patch")
    vl, _, rows = pixels.shape
    nv = vl * n_j
    cw = w_out.shape[1]
    hl = cw // HS
    dp = embed.shape[2]
    rl = w_value.shape[0]
    eb = pad16(5 * vl + 4)
    nr = n_j * eb
    ch = pad16(eb + 2 * rl)
    vp = -(-vl // 8) * 8
    rc = nr // n_p
    others = range(1, n_j)

    *pack, wo_lo = call(
        functools.partial(pack_kernel, eb),
        "pack",
        [shape((ch, cw), BF16)] * n_j + [shape((1, dp, cw), BF16)],
        (w_value, w_key, w_query, query[None, :], embed.transpose(1, 0, 2), b_out[None, :], w_lead[None, :], w_out),
        [pltpu.VMEM((ch, cw), F32)],
        first=True,
    )
    got = [pack[0]] + [flip(pack[k], "var", k) for k in others]

    buf, sums = call(
        rows_kernel,
        "rows",
        (shape((rows + 4 * vp * (rows // cw), cw), BF16), shape((2, cw))),
        (lengths, lead_hours, cotangent, pixels),
        [pltpu.VMEM((4 * vp, rows), F32)],
        smem=2,
        after=(pack[0],),
    )

    bit = n_p // 2
    wo_hi = flip(wo_lo, "patch", bit)
    wo_steps = [wo_hi]
    while bit > 1:
        bit //= 2
        wo_lo = jnp.concatenate([gate(wo_lo, got[-1]), wo_hi], axis=0)
        wo_hi = flip(wo_lo, "patch", bit)
        wo_steps.append(wo_hi)

    part, ekv = call(
        functools.partial(product_kernel, eb, vl, rl, dp),
        "product",
        (shape((nr, 2 * cw), BF16), shape((nr, -(-dp // 128) * 128 + cw), BF16)),
        (*got, sums),
        [pltpu.VMEM((dp, 2 * cw), F32), pltpu.VMEM((nr, 2 * cw), F32)],
        us=0.01,
    )
    got2 = exchange(part, "patch").reshape(n_p, rc, 2 * cw)
    wo, *chunks = call(
        weight_kernel, "weight", [shape((D, cw), BF16)] + [shape((cw, cw), BF16)] * (n_j - 1), (wo_lo, wo_hi)
    )
    copies = call(functools.partial(sum_kernel, vl), "sum", shape((n_p, rc, 2 * cw), BF16), (got2,), after=(wo,))
    vk = exchange(copies.reshape(nr, 2 * cw), "patch")

    bufs = gather_var(gate(buf, part), lambda x: gate(x, copies))
    pix = call(
        functools.partial(pixel_kernel, vl, cw),
        "pixels",
        shape((4, nv, rows), BF16),
        bufs,
        [pltpu.VMEM((4, nv, rows), F32)],
    )

    chunks = [flip(c, "var", k + 1) for k, c in enumerate(chunks)]
    grad_att = call(
        functools.partial(grad_kernel, n_j), "grad_att", shape((cw, rows), BF16), (wo, *chunks, *bufs), after=(vk,)
    )

    parts = GROUP // rows
    owners = n_p // parts
    per = pos_embed.shape[0]
    there = [(k * owners + i, parts * i + k) for i in range(owners) for k in range(parts)]
    back = [(b, a) for a, b in there]
    pos_lo = lax.ppermute(gate(pos_embed, chunks[0]).astype(BF16), "patch", there)[None]
    att, prob, ef, vw = call(
        functools.partial(forward_kernel, 1024, eb),
        "attention_forward",
        (shape((cw, rows), BF16), shape((hl, nv, rows)), shape((5, nv, hl)), shape((5 * nv, cw), BF16)),
        (vk, pix, avail),
        [pltpu.VMEM((n_j, eb, 2 * cw), F32), pltpu.VMEM((5 * nv, 2 * cw), F32)],
        after=(grad_att, pos_lo),
    )
    px_keep, px_send, z = call(
        functools.partial(backward_kernel, 1024, eb, n_j, vp),
        "attention_backward",
        [shape((n_j // 2, 4 * vp, rows), BF16)] * 2 + [shape((nr, cw + 128), BF16)],
        (pix, ef, vw, prob, grad_att),
        [pltpu.VMEM((5 * nv, cw), F32), pltpu.VMEM((5 * hl, nv, 128), F32), pltpu.VMEM((n_j, eb, cw + 128), F32)],
    )

    got3 = exchange(z, "patch").reshape(n_p, rc, cw + 128)
    me = p_id // parts
    pos_hi = flip(gate(pos_lo, z), "patch", n_p // 2)
    g_rows = halve(gate(buf, z)[:rows].reshape(owners, per, cw), me % 2, parts)
    atts = [att] + [flip(gate(att, z), "var", k) for k in others]
    copies_z = call(functools.partial(sum_z_kernel, hl), "sum_z", shape((n_p, rc, cw + 128), BF16), (got3,), after=(g_rows[1],))
    zs = exchange(copies_z.reshape(nr, cw + 128), "patch")

    size = n_p // 2
    send, g_keep = call(
        functools.partial(weight_grad_kernel, n_j),
        "weight_grad",
        [shape((size * dp, cw), BF16), shape((size, dp, cw), BF16)],
        (buf, *atts),
        [pltpu.VMEM((n_p, dp, cw), BF16)],
        after=(copies_z,),
    )
    step = 1
    size //= 2
    send, g_keep = call(
        functools.partial(halve_kernel, step),
        "halve",
        [shape((size * dp, cw), BF16), shape((size, dp, cw), BF16)],
        (g_keep, flip(send, "patch", step)),
    )
    first = send
    bit = n_p // 2
    while bit > parts:
        bit //= 2
        pos_lo = jnp.concatenate([gate(pos_lo, copies_z), pos_hi], axis=0)
        pos_hi = flip(pos_lo, "patch", bit)
    turn = 2
    while turn < owners:
        g_rows = halve(gate(joined(*g_rows), copies_z), (me // turn) % 2, parts * turn)
        turn *= 2
    px_got = flip(gate(px_send, first), "var", 1)
    fh = pad16(2 * rl + eb // 2 + 6)
    last = call(
        functools.partial(middle_kernel, eb, vl, n_j, dp),
        "middle",
        [shape((fh, cw), BF16)] * n_j,
        (zs, vk, ekv),
        [pltpu.VMEM((dp, 2 * cw), F32), pltpu.VMEM((nr, dp), F32), pltpu.VMEM((fh, cw), F32)],
        after=(),
    )

    def late(x):
        return gate(x, last[0])

    while size > 1:
        size //= 2
        step *= 2
        send, g_keep = call(
            functools.partial(halve_kernel, step),
            "halve",
            [shape((size * dp, cw), BF16), shape((size, dp, cw), BF16)],
            (g_keep, flip(send, "patch", step)),
            after=(last[0],),
        )
    grad_pos = lax.ppermute(joined(g_rows[0], gate(g_rows[1], first)).reshape(per, cw), "patch", back)
    grad_w_out, grad_pos = call(
        functools.partial(halve_kernel, 2 * step),
        "halve",
        (shape((dp, cw)), shape((per, cw))),
        (g_keep, flip(send, "patch", 2 * step), grad_pos),
    )

    bit = 1
    while 2 * bit < n_j:
        bit *= 2
        px_keep, px_send = call(
            pixel_add_kernel,
            "pixel_add",
            [shape((n_j // (2 * bit), 4 * vp, rows), BF16)] * 2,
            (px_keep, px_got),
            after=(first,),
        )
        px_got = flip(px_send, "var", bit)
    mixed = call(
        functools.partial(mixed_kernel, vl, n_j),
        "mixed",
        shape((rows, cw), BF16),
        (lengths, lead_hours, wo, vk, pos_lo, pos_hi, *atts),
        [pltpu.VMEM((owners, per, cw), BF16)],
        smem=2,
        after=(first,),
    )

    last = [last[0]] + [flip(last[k], "var", k) for k in others]
    gwv, gwk, gwq, gq, ge, gb, gl, grad_pixels = call(
        functools.partial(final_kernel, eb, vl, rl, dp, n_j),
        "final",
        (
            shape((rl, D)),
            shape((rl, D)),
            shape((rl, D)),
            shape((1, rl)),
            shape((5, vl, dp)),
            shape((1, rl)),
            shape((1, rl)),
            shape((vl, 4, rows), BF16),
        ),
        (w_query, query[:, None], px_keep, px_got, *last),
        [pltpu.VMEM((eb, dp), F32), pltpu.VMEM((8, D), F32), pltpu.VMEM((4 * vp, rows), F32), pltpu.VMEM((4 * vl, rows), F32)],
        after=(send,),
    )
    return (
        mixed,
        grad_pixels,
        ge.transpose(1, 0, 2),
        gq.reshape(rl),
        gwq,
        gwk,
        gwv,
        grad_w_out,
        gb.reshape(rl),
        grad_pos,
        gl.reshape(rl),
    )


def solution(mesh):
    both = P(("patch", "var"))
    rows2 = P(("patch", "var"), None)
    return jax.shard_map(
        shards,
        mesh=mesh,
        in_specs=(
            P("var", None, "patch"),
            P("var", None, "patch"),
            both,
            rows2,
            rows2,
            rows2,
            P("patch", "var"),
            both,
            P("patch", "var"),
            both,
            P(),
            P(),
            P(),
            P("patch", "var"),
        ),
        out_specs=(
            P("patch", "var"),
            P("var", None, "patch"),
            P("var", None, "patch"),
            both,
            rows2,
            rows2,
            rows2,
            P("patch", "var"),
            both,
            P("patch", "var"),
            both,
        ),
        check_vma=False,
    )
```

```python
import functools
import math

import jax
import jax.numpy as jnp
from jax import lax
from jax.experimental import pallas as pl
from jax.experimental.pallas import tpu as pltpu
from jax.sharding import PartitionSpec as P

D = 1024
HEADS = 16
HS = D // HEADS
GROUP = 2048
F32 = jnp.float32
BF16 = jnp.bfloat16
NEG = -1e30
SCALE = 1.0 / math.sqrt(HS)


def exchange(x, axis):
    return lax.all_to_all(x, axis, 0, 0, tiled=True)


def flip(x, axis, bit):
    n = lax.axis_size(axis)
    return lax.ppermute(x, axis, [(i, i ^ bit) for i in range(n)])


def gate(x, after):
    return lax.optimization_barrier((x, after))[0]


def gather_var(x, last):
    n = lax.axis_size("var")
    blocks = {0: x}
    bit = n // 2
    while bit:
        for k, block in list(blocks.items()):
            blocks[k | bit] = flip(last(block) if bit == 1 and k else block, "var", bit)
        bit //= 2
    return [blocks[k] for k in range(n)]


def halve(x, bit, step):
    pair = x.reshape(x.shape[0] // 2, 2, *x.shape[1:])
    send = lax.dynamic_index_in_dim(pair, 1 - bit, 1, False)
    keep = lax.dynamic_index_in_dim(pair, bit, 1, False)
    return keep, flip(send, "patch", step)


def joined(keep, got):
    return (keep.astype(F32) + got.astype(F32)).astype(BF16)


def nt(a, b):
    return lax.dot_general(a, b, (((1,), (1,)), ((), ())), preferred_element_type=F32)


def tn(a, b):
    return lax.dot_general(a, b, (((0,), (0,)), ((), ())), preferred_element_type=F32)


def nn(a, b):
    return jnp.dot(a, b, preferred_element_type=F32)


def pad16(n):
    return -(-n // 16) * 16


def split(value):
    hi = value.astype(BF16).astype(F32)
    return hi, value - hi


def put_pair(ref, row, lanes, value):
    ref[row : row + 1, :lanes], ref[row : row + 1, lanes : 2 * lanes] = split(value)


def put_rows(ref, block, row, lanes, value):
    ref[block, row : row + 1, :lanes], ref[block, row + 1 : row + 2, :lanes] = split(value)


def rows_kernel(length_ref, lead_ref, cot_ref, pix_ref, out_ref, sums_ref, tmp_ref):
    rows, cw = cot_ref.shape
    vl = pix_ref.shape[0]
    vp = tmp_ref.shape[0] // 4
    row0 = lax.axis_index("patch") * rows
    sample = row0 // GROUP
    pos = row0 % GROUP + lax.broadcasted_iota(jnp.int32, cot_ref.shape, 0)
    kept = jnp.where(pos < length_ref[sample], cot_ref[...].astype(F32), 0.0)
    out_ref[:rows] = kept.astype(BF16)
    total = jnp.sum(kept, axis=0, keepdims=True)
    sums_ref[0:1, :] = total
    sums_ref[1:2, :] = total * (lead_ref[sample].astype(F32) / 100.0)
    tmp_ref[...] = jnp.zeros_like(tmp_ref)
    for v in range(vl):
        x = pix_ref[v].astype(F32)
        for p in range(4):
            tmp_ref[p * vp + v : p * vp + v + 1, :] = x[p : p + 1]
    for b in range(rows // cw):
        out_ref[rows + b * 4 * vp : rows + (b + 1) * 4 * vp, :] = tmp_ref[:, b * cw : (b + 1) * cw].astype(BF16)


def pack_kernel(eb, v_ref, k_ref, wq_ref, q_ref, e_ref, b_ref, l_ref, wo_ref, *refs):
    outs, wo_low_ref, tmp_ref = refs[:-2], refs[-2], refs[-1]
    wo_low_ref[0] = wo_ref[...].astype(BF16)
    cw = outs[0].shape[1]
    rl = v_ref.shape[0]
    _, vl, dp = e_ref.shape
    spare = 5 * vl
    j = lax.axis_index("var")
    q = jnp.broadcast_to(q_ref[...].astype(BF16), (16, rl))
    tmp_ref[...] = jnp.zeros_like(tmp_ref)
    for p in range(5):
        tmp_ref[p * vl : (p + 1) * vl, :dp] = e_ref[p]
    own = lax.broadcasted_iota(jnp.int32, (1, dp), 1) // rl == j
    for i, ref in enumerate((b_ref, l_ref)):
        tiled = jnp.concatenate([ref[...]] * (dp // rl), axis=1)
        tmp_ref[spare + 2 + i : spare + 3 + i, :dp] = jnp.where(own, tiled, 0.0)
    for k, out_ref in enumerate(outs):
        cols = pl.ds(pl.multiple_of((j ^ k) * cw, 128), cw)
        hi, lo = split(nn(q, wq_ref[:, cols].astype(BF16))[0:1])
        tmp_ref[spare : spare + 1, :] = hi
        tmp_ref[spare + 1 : spare + 2, :] = lo
        tmp_ref[eb : eb + rl, :] = k_ref[:, cols]
        tmp_ref[eb + rl : eb + 2 * rl, :] = v_ref[:, cols]
        out_ref[...] = tmp_ref[...].astype(BF16)


def place(ref, at, j, size, parts, lanes):
    if size % 16 == 0:
        for k, part in enumerate(parts):
            ref[pl.ds(pl.multiple_of((j ^ k) * size, size), size), lanes] = part
        return
    for s in range(len(parts)):
        value = parts[0]
        for k in range(1, len(parts)):
            value = jnp.where(j ^ k == s, parts[k], value)
        ref[s * size : (s + 1) * size, lanes] = value


def product_kernel(eb, vl, rl, dp, *refs):
    n = len(refs) - 5
    got, (sums_ref, out_ref, ekv_ref, w_ref, p_ref) = refs[:n], refs[n:]
    cw = got[0].shape[1]
    spare = 5 * vl
    lanes = -(-dp // 128) * 128
    p_id = lax.axis_index("patch")
    j = lax.axis_index("var")
    live = lax.broadcasted_iota(jnp.int32, (eb, dp), 0) < spare
    small = jnp.zeros((4, cw), F32)
    gs = [got[k][...].astype(F32) for k in range(n)]
    for k in range(n):
        small = small + gs[k][spare : spare + 4]
        at = pl.ds(pl.multiple_of((j ^ k) * eb, eb), eb)
        ekv_ref[at, :dp] = jnp.where(live, gs[k][:eb, :dp], 0.0).astype(BF16)
    for m in range(2):
        at = eb + m * rl
        place(w_ref, 0, j, rl, [g[at : at + rl] for g in gs], slice(m * cw, (m + 1) * cw))
    key, value = w_ref[:, :cw].astype(BF16), w_ref[:, cw:].astype(BF16)
    ekv_ref[:dp, lanes : lanes + cw] = key
    ekv_ref[dp : 2 * dp, lanes : lanes + cw] = value
    p_ref[...] = nn(ekv_ref[:, :dp], jnp.concatenate([value, key], axis=1))
    put_pair(p_ref, spare, cw, small[0:1] + small[1:2])
    put_pair(p_ref, spare + 1, cw, sums_ref[0:1])
    put_pair(p_ref, spare + 2, cw, sums_ref[1:2])
    per = cw // dp
    here = (lax.broadcasted_iota(jnp.int32, (1, cw), 1) // dp == p_id % per) & (p_id // per == j)
    for i in range(2):
        tiled = jnp.concatenate([small[2 + i : 3 + i, :dp]] * per, axis=1)
        p_ref[spare + 3 : spare + 4, i * cw : (i + 1) * cw] = jnp.where(here, tiled, 0.0)
    out_ref[...] = p_ref[...].astype(BF16)


def sum_kernel(vl, got_ref, out_ref):
    n_p, rc, lanes = got_ref.shape
    cw = lanes // 2
    total = got_ref[0].astype(F32)
    for s in range(1, n_p):
        total = total + got_ref[s].astype(F32)
    row = lax.axis_index("patch") * rc + lax.broadcasted_iota(jnp.int32, (rc, cw), 0)
    paired = (row >= 5 * vl) & (row < 5 * vl + 3)
    a, b = total[:, :cw], total[:, cw:]
    hi, lo = split(a + b)
    a, b = jnp.where(paired, hi, a).astype(BF16), jnp.where(paired, lo, b).astype(BF16)
    for s in range(n_p):
        out_ref[s, :, :cw] = a
        out_ref[s, :, cw:] = b


def forward_kernel(tile, eb, vk_ref, x_ref, avail_ref, att_ref, prob_ref, ef_ref, vw_ref, s_ref, vs_ref):
    nv, rows = x_ref.shape[1:]
    heads = prob_ref.shape[0]
    cw = att_ref.shape[0]
    n_j = vk_ref.shape[0] // eb
    vl = nv // n_j
    spare = 5 * vl
    j = lax.axis_index("var")
    for s in range(n_j):
        s_ref[s] = vk_ref[s * eb : (s + 1) * eb, :].astype(F32)
    q = (s_ref[0, spare : spare + 1, :cw] + s_ref[0, spare : spare + 1, cw:]) * SCALE
    for k in range(n_j):
        for p in range(5):
            vs_ref[p * nv + k * vl : p * nv + (k + 1) * vl, :] = s_ref[j ^ k, p * vl : (p + 1) * vl, :]
    vw_ref[...] = vs_ref[:, :cw].astype(BF16)
    for p in range(5):
        kq = vs_ref[p * nv : (p + 1) * nv, cw:] * q
        ef_ref[p] = jnp.concatenate(
            [jnp.sum(kq[:, h * HS : (h + 1) * HS], axis=1, keepdims=True) for h in range(heads)], axis=1
        )
    sample = lax.axis_index("patch") * rows // GROUP
    row = lax.broadcasted_iota(jnp.int32, (nv, nv), 0)
    shift = jnp.zeros((nv, nv), jnp.int32)
    for k in range(n_j):
        shift = jnp.where((row >= k * vl) & (row < (k + 1) * vl), ((j ^ k) - k) * vl, shift)
    same = row + shift == lax.broadcasted_iota(jnp.int32, (nv, nv), 1)
    flags = jnp.broadcast_to(avail_ref[pl.ds(sample, 1), :], (nv, nv))
    present = jnp.sum(jnp.where(same, flags.astype(F32), 0.0), axis=1, keepdims=True) > 0.5
    vw = [vw_ref[:, h * HS : (h + 1) * HS] for h in range(heads)]

    def step(i, carry):
        cols = pl.ds(pl.multiple_of(i * tile, tile), tile)
        xs = [x_ref[p, :, cols].astype(F32) for p in range(4)]
        for h in range(heads):
            s = jnp.broadcast_to(ef_ref[4, :, h : h + 1], (nv, tile))
            for p in range(4):
                s = s + ef_ref[p, :, h : h + 1] * xs[p]
            s = jnp.where(present, s, NEG)
            w = jnp.where(present, jnp.exp(s - jnp.max(s, axis=0, keepdims=True)), 0.0)
            prob = w / jnp.sum(w, axis=0, keepdims=True)
            prob_ref[h, :, cols] = prob
            a = jnp.concatenate([(prob * x).astype(BF16) for x in xs] + [prob.astype(BF16)], axis=0)
            att_ref[h * HS : (h + 1) * HS, cols] = tn(vw[h], a).astype(BF16)
        return carry

    lax.fori_loop(0, rows // tile, step, 0)


def reversed_bits(x, bits):
    out = 0
    for b in range(bits):
        out = out | (((x >> b) & 1) << (bits - 1 - b))
    return out


def pixel_kernel(vl, cw, *refs):
    bufs, (out_ref, x_ref) = refs[:-2], refs[-2:]
    rows = out_ref.shape[2]
    vp = (bufs[0].shape[0] - rows) // (4 * (rows // cw))
    for k, buf in enumerate(bufs):
        for b in range(rows // cw):
            at = rows + b * 4 * vp
            x = buf[at : at + 4 * vp, :].astype(F32)
            for p in range(4):
                x_ref[p, k * vl : (k + 1) * vl, b * cw : (b + 1) * cw] = x[p * vp : p * vp + vl]
    for p in range(4):
        out_ref[p] = x_ref[p].astype(BF16)


def weight_kernel(lo_ref, hi_ref, full_ref, *chunks):
    half, dp, cw = lo_ref.shape
    p_id = lax.axis_index("patch")
    j = lax.axis_index("var")
    for q in range(2 * half):
        block = reversed_bits(q ^ p_id, (2 * half).bit_length() - 1)
        at = slice(q * dp, (q + 1) * dp)

        @pl.when(block < half)
        def _(at=at, block=block):
            full_ref[at, :] = lo_ref[block]

        @pl.when(block >= half)
        def _(at=at, block=block):
            full_ref[at, :] = hi_ref[block - half]

    for k, ref in enumerate(chunks):
        ref[...] = full_ref[pl.ds(pl.multiple_of((j ^ (k + 1)) * cw, cw), cw), :]


def grad_kernel(n_j, full_ref, *refs):
    ws, cots, (out_ref,) = refs[: n_j - 1], refs[n_j - 1 : -1], refs[-1:]
    cw, rows = out_ref.shape
    j = lax.axis_index("var")
    own = full_ref[pl.ds(pl.multiple_of(j * cw, cw), cw), :]
    tile = 512
    for i in range(rows // tile):
        at = slice(i * tile, (i + 1) * tile)
        total = nt(own, cots[0][at, :])
        for k in range(1, n_j):
            total = total + nt(ws[k - 1][...], cots[k][at, :])
        out_ref[:, at] = total.astype(BF16)


def weight_grad_kernel(n_j, buf_ref, *refs):
    atts, (send_ref, keep_ref, tmp_ref) = refs[:n_j], refs[n_j:]
    cw, rows = atts[0].shape
    half, dp, _ = keep_ref.shape
    j = lax.axis_index("var")
    per = cw // dp
    for k in range(n_j):
        g = nn(atts[k][...], buf_ref[:rows, :]).astype(BF16)
        for t in range(per):
            tmp_ref[(j ^ k) * per + t] = g[t * dp : (t + 1) * dp]
    own = lax.axis_index("patch") & 1
    for b in range(half):
        send_ref[b * dp : (b + 1) * dp, :] = tmp_ref[2 * b + 1 - own]
        keep_ref[b] = tmp_ref[2 * b + own]


def halve_kernel(bit, g_ref, got_ref, *refs):
    count, dp, cw = g_ref.shape
    own = jnp.where(lax.axis_index("patch") & (2 * bit), 1, 0)

    def g_sum(b):
        at = pl.ds(pl.multiple_of(b * dp, dp), dp)
        return g_ref[b].astype(F32) + got_ref[at, :].astype(F32)

    if count == 1:
        pos_ref, out_ref, pos_out_ref = refs
        out_ref[...] = g_sum(0)
        pos_out_ref[...] = pos_ref[...].astype(F32)
        return
    send_ref, g_next = refs
    for b in range(g_next.shape[0]):
        send_ref[b * dp : (b + 1) * dp, :] = g_sum(2 * b + 1 - own).astype(BF16)
        g_next[b] = g_sum(2 * b + own).astype(BF16)


def pixel_add_kernel(keep_ref, got_ref, next_ref, send_ref):
    for i in range(next_ref.shape[0]):
        next_ref[i] = (keep_ref[2 * i].astype(F32) + got_ref[2 * i].astype(F32)).astype(BF16)
        send_ref[i] = (keep_ref[2 * i + 1].astype(F32) + got_ref[2 * i + 1].astype(F32)).astype(BF16)


def mixed_kernel(vl, n_j, length_ref, lead_ref, w_ref, vk_ref, plo_ref, phi_ref, *refs):
    atts, (out_ref, pos_ref) = refs[:n_j], refs[n_j:]
    rows, cw = out_ref.shape
    spare = 5 * vl
    base = pad16(spare) - 16
    row0 = lax.axis_index("patch") * rows
    sample = row0 // GROUP
    me = lax.axis_index("patch") // (GROUP // rows)
    j = lax.axis_index("var")
    half, per, _ = plo_ref.shape
    pos_ref[:half] = plo_ref[...]
    pos_ref[half:] = phi_ref[...]
    bl = vk_ref[base : base + 32, :].astype(F32)[spare - base + 3 : spare - base + 4]
    add = bl[:, :cw] + lead_ref[sample].astype(F32) / 100.0 * bl[:, cw:]
    for b in range(2 * half):
        at = slice(b * per, (b + 1) * per)
        total = add + pos_ref[reversed_bits(b ^ me, (2 * half).bit_length() - 1)].astype(F32)
        for k in range(n_j):
            w = w_ref[pl.ds(pl.multiple_of((j ^ k) * cw, cw), cw), :]
            total = total + tn(atts[k][:, at], w)
        pos = row0 % GROUP + b * per + lax.broadcasted_iota(jnp.int32, (per, cw), 0)
        out_ref[at, :] = jnp.where(pos < length_ref[sample], total, 0.0).astype(BF16)


def backward_kernel(tile, eb, n_j, vp, x_ref, ef_ref, vw_ref, prob_ref, grad_ref, *refs):
    outs, (z_ref, gv_ref, acc_ref, s_ref) = refs[:-4], refs[-4:]
    nv, rows = x_ref.shape[1:]
    heads = prob_ref.shape[0]
    vl = nv // n_j
    cw = gv_ref.shape[1]
    j = lax.axis_index("var")
    gv_ref[...] = jnp.zeros_like(gv_ref)
    acc_ref[...] = jnp.zeros_like(acc_ref)
    blank = jnp.zeros((vp - vl, tile), F32)

    def step(i, carry):
        cols = pl.ds(pl.multiple_of(i * tile, tile), tile)
        xs = [x_ref[p, :, cols].astype(F32) for p in range(4)]
        gx = [jnp.zeros((nv, tile), F32) for _ in range(4)]
        for h in range(heads):
            hc = slice(h * HS, (h + 1) * HS)
            prob = prob_ref[h, :, cols]
            gh = grad_ref[hc, cols]
            g = nn(vw_ref[:, hc], gh)
            gp = [g[p * nv : (p + 1) * nv] for p in range(5)]
            gprob = gp[4]
            for p in range(4):
                gprob = gprob + xs[p] * gp[p]
            inner = jnp.sum(prob * gprob, axis=0, keepdims=True)
            gs = prob * (gprob - inner)
            for p in range(4):
                gx[p] = gx[p] + prob * gp[p] + ef_ref[p, :, h : h + 1] * gs
            a = jnp.concatenate([(prob * x).astype(BF16) for x in xs] + [prob.astype(BF16)], axis=0)
            gv_ref[:, hc] += nt(a, gh)
            for p in range(5):
                t = gs if p == 4 else gs * xs[p]
                part = t[:, :128]
                for k in range(1, tile // 128):
                    part = part + t[:, k * 128 : (k + 1) * 128]
                acc_ref[p * heads + h] += part
        for k in range(n_j):
            ref = outs[k & 1].at[k >> 1]
            piece = jnp.concatenate([t for p in range(4) for t in (gx[p][k * vl : (k + 1) * vl], blank)], axis=0)
            ref[:, cols] = piece.astype(BF16)
        return carry

    lax.fori_loop(0, rows // tile, step, 0)
    s_ref[...] = jnp.zeros_like(s_ref)
    for p in range(5):
        gs = jnp.concatenate(
            [jnp.sum(acc_ref[p * heads + h], axis=1, keepdims=True) for h in range(heads)], axis=1
        )
        hi, lo = split(gs)
        pair = jnp.concatenate([hi, lo, jnp.zeros((nv, 128 - 2 * heads), F32)], axis=1)
        for k in range(n_j):
            at = slice(p * nv + k * vl, p * nv + (k + 1) * vl)
            s_ref[j ^ k, p * vl : (p + 1) * vl, :cw] = gv_ref[at, :]
            s_ref[j ^ k, p * vl : (p + 1) * vl, cw:] = pair[k * vl : (k + 1) * vl]
    for s in range(n_j):
        z_ref[s * eb : (s + 1) * eb, :] = s_ref[s].astype(BF16)


def sum_z_kernel(heads, got_ref, out_ref):
    n_p, rc, lanes = got_ref.shape
    cw = lanes - 128
    total = got_ref[0].astype(F32)
    for s in range(1, n_p):
        total = total + got_ref[s].astype(F32)
    main = total[:, :cw].astype(BF16)
    hi, lo = split(total[:, cw : cw + heads] + total[:, cw + heads : cw + 2 * heads])
    pair = jnp.concatenate([hi, lo, jnp.zeros((rc, 128 - 2 * heads), F32)], axis=1).astype(BF16)
    for s in range(n_p):
        out_ref[s, :, :cw] = main
        out_ref[s, :, cw:] = pair


def middle_kernel(eb, vl, n_j, dp, z_ref, vk_ref, ekv_ref, *refs):
    chunks, (g_ref, ge_ref, s_ref) = refs[:n_j], refs[n_j:]
    cw = z_ref.shape[1] - 128
    lanes = -(-dp // 128) * 128
    key, value = ekv_ref[:dp, lanes : lanes + cw], ekv_ref[dp : 2 * dp, lanes : lanes + cw]
    rl = dp // n_j
    heads = cw // HS
    spare = 5 * vl
    half = eb // 2
    j = lax.axis_index("var")
    base = pad16(spare) - 16
    small = vk_ref[base : base + 32, :].astype(F32)[spare - base : spare - base + 3]
    small = small[:, :cw] + small[:, cw:]
    qvec = small[0:1] * SCALE
    g = tn(ekv_ref[:, :dp], z_ref[...])
    gfold = g[:, cw : cw + heads] + g[:, cw + heads : cw + 2 * heads]
    g_ref[:, :cw] = g[:, :cw]
    g_ref[:, cw:] = jnp.concatenate(
        [gfold[:, h : h + 1] * qvec[:, h * HS : (h + 1) * HS] for h in range(heads)], axis=1
    )
    pair = z_ref[:, cw:].astype(F32)
    gs = pair[:, :heads] + pair[:, heads : 2 * heads]
    live = lax.broadcasted_iota(jnp.int32, (n_j * eb, 1), 0) % eb < spare
    ke = jnp.where(live, vk_ref[:, cw:].astype(F32), 0.0)
    gq = jnp.concatenate(
        [jnp.sum(ke[:, h * HS : (h + 1) * HS] * gs[:, h : h + 1], axis=0, keepdims=True) for h in range(heads)], axis=1
    ) * SCALE
    head = lax.broadcasted_iota(jnp.int32, (8, cw), 0) == lax.broadcasted_iota(jnp.int32, (8, cw), 1) // HS
    hi, lo = split(jnp.where(head, qvec, 0.0))
    fold = nt(hi.astype(BF16), key) + nt(lo.astype(BF16), key)
    ge = nt(z_ref[:, :cw], value)
    for h in range(heads):
        ge = ge + gs[:, h : h + 1] * fold[h : h + 1, :]
    ge_ref[...] = ge
    s_ref[...] = jnp.zeros_like(s_ref)
    at = 2 * rl + half
    for i, row in enumerate((gq, small[1:2], small[2:3])):
        s_ref[at + 2 * i : at + 2 * i + 1, :], s_ref[at + 2 * i + 1 : at + 2 * i + 2, :] = split(row)
    for k in range(n_j):
        rows = own_rows(g_ref, j ^ k, rl)
        s_ref[:rl, :] = rows[:, :cw]
        s_ref[rl : 2 * rl, :] = rows[:, cw:]
        block = ge_ref[pl.ds(pl.multiple_of((j ^ k) * eb, eb), eb), :]
        s_ref[2 * rl : 2 * rl + half, :dp] = block[:half]
        s_ref[2 * rl : 2 * rl + half, cw // 2 : cw // 2 + dp] = block[half:]
        chunks[k][...] = s_ref[...].astype(BF16)


def own_rows(ref, index, size):
    if size % 8 == 0:
        return ref[pl.ds(pl.multiple_of(index * size, size), size), :]
    out = ref[:size, :]
    for k in range(1, ref.shape[0] // size):
        out = jnp.where(index == k, ref[k * size : (k + 1) * size, :], out)
    return out


def final_kernel(eb, vl, rl, dp, n_j, wq_ref, q_ref, pk_ref, pg_ref, *refs):
    chunks, (gwv_ref, gwk_ref, gwq_ref, gq_ref, ge_ref, gb_ref, gl_ref, px_ref, f_ref, r_ref, s_ref, x_ref) = refs[:n_j], refs[n_j:]
    s_ref[...] = pk_ref[0].astype(F32) + pg_ref[0].astype(F32)
    vp = s_ref.shape[0] // 4
    for v in range(vl):
        for p in range(4):
            x_ref[4 * v + p : 4 * v + p + 1, :] = s_ref[p * vp + v : p * vp + v + 1, :]
    for v in range(vl):
        px_ref[v] = x_ref[4 * v : 4 * v + 4, :].astype(BF16)
    cw = chunks[0].shape[1]
    half = eb // 2
    j = lax.axis_index("var")
    at_out = lax.axis_index("patch") * n_j + j
    at = 2 * rl + half
    ge = jnp.zeros((half, cw), F32)
    gb = jnp.zeros((1, rl), F32)
    gl = jnp.zeros((1, rl), F32)
    for k in range(n_j):
        c = chunks[k][...].astype(F32)
        cols = pl.ds(pl.multiple_of((j ^ k) * cw, 128), cw)
        gwv_ref[:, cols] = c[:rl]
        gwk_ref[:, cols] = c[rl : 2 * rl]
        ge = ge + c[2 * rl : at]
        r_ref[0:1, cols] = c[at : at + 1] + c[at + 1 : at + 2]
        bias = c[at + 2 : at + 3] + c[at + 3 : at + 4]
        lead = c[at + 4 : at + 5] + c[at + 5 : at + 6]
        for g in range(cw // rl):
            here = at_out == (j ^ k) * (cw // rl) + g
            gb = gb + jnp.where(here, bias[:, g * rl : (g + 1) * rl], 0.0)
            gl = gl + jnp.where(here, lead[:, g * rl : (g + 1) * rl], 0.0)
    f_ref[:half, :] = ge[:, :dp]
    f_ref[half:, :] = ge[:, cw // 2 : cw // 2 + dp]
    for p in range(5):
        ge_ref[p] = f_ref[p * vl : (p + 1) * vl, :]
    gq = r_ref[0:1, :]
    gwq_ref[...] = q_ref[...].astype(BF16).astype(F32) * gq
    hi, lo = split(gq)
    wq = wq_ref[...].astype(BF16)
    both = jnp.concatenate([jnp.broadcast_to(hi, (8, D)), jnp.broadcast_to(lo, (8, D))], axis=0).astype(BF16)
    two = nt(both, wq)
    gq_ref[...] = two[0:1] + two[8:9]
    gb_ref[...] = gb
    gl_ref[...] = gl


def call(kernel, name, out_shape, args, scratch=(), us=0.01, smem=0, after=(), first=False, spill=(), hbm=0):
    n = len(args)
    in_vmem = pl.BlockSpec(memory_space=pltpu.VMEM)
    specs = [pl.BlockSpec(memory_space=pltpu.SMEM)] * smem + [pl.BlockSpec() if first else in_vmem] * (n - smem)
    specs[n - hbm :] = [pl.BlockSpec(memory_space=pl.ANY)] * hbm
    specs += [pl.BlockSpec(memory_space=pl.ANY)] * len(after)
    shapes = list(out_shape) if isinstance(out_shape, (list, tuple)) else [out_shape]
    outs = [pl.BlockSpec(memory_space=pltpu.HBM) if i in spill else in_vmem for i in range(len(shapes))]
    extra = [pltpu.VMEM(shapes[i].shape, shapes[i].dtype) for i in spill]
    if spill:
        extra.append(pltpu.SemaphoreType.DMA((len(spill),)))

    def body(*refs):
        ins, rest = refs[:n], refs[n + len(after) :]
        results, rest = list(rest[: len(shapes)]), rest[len(shapes) :]
        local, sems = rest[: len(spill)], rest[len(extra) - 1 : len(extra)]
        rest = rest[len(extra) :]
        copies = []
        for c, i in enumerate(spill):
            copies.append(pltpu.make_async_copy(local[c], results[i], sems[0].at[c]))
            results[i] = local[c]
        kernel(*ins, *results, *rest)
        for copy in copies:
            copy.start()
        for copy in copies:
            copy.wait()

    result = pl.pallas_call(
        body,
        out_shape=shapes,
        in_specs=specs,
        out_specs=outs,
        scratch_shapes=[*extra, *scratch],
        name=name,
        compiler_params=None if first else pltpu.CompilerParams(vmem_limit_bytes=12 << 20),
        cost_estimate=pl.CostEstimate(flops=int(us * 1.153e9), bytes_accessed=1 << 16, transcendentals=0),
    )(*args, *after)
    return result if isinstance(out_shape, (list, tuple)) else result[0]


def shape(dims, kind=F32):
    return jax.ShapeDtypeStruct(dims, kind)


def shards(pixels, embed, query, w_query, w_key, w_value, w_out, b_out, pos_embed, w_lead, avail, lengths, lead_hours, cotangent):
    n_p = lax.axis_size("patch")
    n_j = lax.axis_size("var")
    p_id = lax.axis_index("patch")
    vl, _, rows = pixels.shape
    nv = vl * n_j
    cw = w_out.shape[1]
    hl = cw // HS
    dp = embed.shape[2]
    rl = w_value.shape[0]
    eb = pad16(5 * vl + 4)
    nr = n_j * eb
    ch = pad16(eb + 2 * rl)
    vp = -(-vl // 8) * 8
    rc = nr // n_p
    others = range(1, n_j)

    *pack, wo_lo = call(
        functools.partial(pack_kernel, eb),
        "pack",
        [shape((ch, cw), BF16)] * n_j + [shape((1, dp, cw), BF16)],
        (w_value, w_key, w_query, query[None, :], embed.transpose(1, 0, 2), b_out[None, :], w_lead[None, :], w_out),
        [pltpu.VMEM((ch, cw), F32)],
        first=True,
    )
    got = [pack[0]] + [flip(pack[k], "var", k) for k in others]

    buf, sums = call(
        rows_kernel,
        "rows",
        (shape((rows + 4 * vp * (rows // cw), cw), BF16), shape((2, cw))),
        (lengths, lead_hours, cotangent, pixels),
        [pltpu.VMEM((4 * vp, rows), F32)],
        smem=2,
        after=(pack[0],),
    )

    bit = n_p // 2
    wo_hi = flip(wo_lo, "patch", bit)
    wo_steps = [wo_hi]
    while bit > 1:
        bit //= 2
        wo_lo = jnp.concatenate([gate(wo_lo, got[-1]), wo_hi], axis=0)
        wo_hi = flip(wo_lo, "patch", bit)
        wo_steps.append(wo_hi)

    part, ekv = call(
        functools.partial(product_kernel, eb, vl, rl, dp),
        "product",
        (shape((nr, 2 * cw), BF16), shape((nr, -(-dp // 128) * 128 + cw), BF16)),
        (*got, sums),
        [pltpu.VMEM((dp, 2 * cw), F32), pltpu.VMEM((nr, 2 * cw), F32)],
        us=0.01,
    )
    got2 = exchange(part, "patch").reshape(n_p, rc, 2 * cw)
    wo, *chunks = call(
        weight_kernel, "weight", [shape((D, cw), BF16)] + [shape((cw, cw), BF16)] * (n_j - 1), (wo_lo, wo_hi)
    )
    copies = call(functools.partial(sum_kernel, vl), "sum", shape((n_p, rc, 2 * cw), BF16), (got2,), after=(wo,))
    vk = exchange(copies.reshape(nr, 2 * cw), "patch")

    bufs = gather_var(gate(buf, part), lambda x: gate(x, copies))
    pix = call(
        functools.partial(pixel_kernel, vl, cw),
        "pixels",
        shape((4, nv, rows), BF16),
        bufs,
        [pltpu.VMEM((4, nv, rows), F32)],
    )

    chunks = [flip(c, "var", k + 1) for k, c in enumerate(chunks)]
    grad_att = call(
        functools.partial(grad_kernel, n_j), "grad_att", shape((cw, rows), BF16), (wo, *chunks, *bufs), after=(vk,)
    )

    parts = GROUP // rows
    owners = n_p // parts
    per = pos_embed.shape[0]
    there = [(k * owners + i, parts * i + k) for i in range(owners) for k in range(parts)]
    back = [(b, a) for a, b in there]
    pos_lo = lax.ppermute(gate(pos_embed, chunks[0]).astype(BF16), "patch", there)[None]
    att, prob, ef, vw = call(
        functools.partial(forward_kernel, 1024, eb),
        "attention_forward",
        (shape((cw, rows), BF16), shape((hl, nv, rows)), shape((5, nv, hl)), shape((5 * nv, cw), BF16)),
        (vk, pix, avail),
        [pltpu.VMEM((n_j, eb, 2 * cw), F32), pltpu.VMEM((5 * nv, 2 * cw), F32)],
        after=(grad_att, pos_lo),
    )
    px_keep, px_send, z = call(
        functools.partial(backward_kernel, 1024, eb, n_j, vp),
        "attention_backward",
        [shape((n_j // 2, 4 * vp, rows), BF16)] * 2 + [shape((nr, cw + 128), BF16)],
        (pix, ef, vw, prob, grad_att),
        [pltpu.VMEM((5 * nv, cw), F32), pltpu.VMEM((5 * hl, nv, 128), F32), pltpu.VMEM((n_j, eb, cw + 128), F32)],
    )

    got3 = exchange(z, "patch").reshape(n_p, rc, cw + 128)
    me = p_id // parts
    pos_hi = flip(gate(pos_lo, z), "patch", n_p // 2)
    g_rows = halve(gate(buf, z)[:rows].reshape(owners, per, cw), me % 2, parts)
    atts = [att] + [flip(gate(att, z), "var", k) for k in others]
    copies_z = call(functools.partial(sum_z_kernel, hl), "sum_z", shape((n_p, rc, cw + 128), BF16), (got3,), after=(g_rows[1],))
    zs = exchange(copies_z.reshape(nr, cw + 128), "patch")

    size = n_p // 2
    send, g_keep = call(
        functools.partial(weight_grad_kernel, n_j),
        "weight_grad",
        [shape((size * dp, cw), BF16), shape((size, dp, cw), BF16)],
        (buf, *atts),
        [pltpu.VMEM((n_p, dp, cw), BF16)],
        after=(copies_z,),
    )
    step = 1
    size //= 2
    send, g_keep = call(
        functools.partial(halve_kernel, step),
        "halve",
        [shape((size * dp, cw), BF16), shape((size, dp, cw), BF16)],
        (g_keep, flip(send, "patch", step)),
    )
    first = send
    bit = n_p // 2
    while bit > parts:
        bit //= 2
        pos_lo = jnp.concatenate([gate(pos_lo, copies_z), pos_hi], axis=0)
        pos_hi = flip(pos_lo, "patch", bit)
    turn = 2
    while turn < owners:
        g_rows = halve(gate(joined(*g_rows), copies_z), (me // turn) % 2, parts * turn)
        turn *= 2
    px_got = flip(gate(px_send, first), "var", 1)
    fh = pad16(2 * rl + eb // 2 + 6)
    last = call(
        functools.partial(middle_kernel, eb, vl, n_j, dp),
        "middle",
        [shape((fh, cw), BF16)] * n_j,
        (zs, vk, ekv),
        [pltpu.VMEM((dp, 2 * cw), F32), pltpu.VMEM((nr, dp), F32), pltpu.VMEM((fh, cw), F32)],
        after=(),
    )

    def late(x):
        return gate(x, last[0])

    while size > 1:
        size //= 2
        step *= 2
        send, g_keep = call(
            functools.partial(halve_kernel, step),
            "halve",
            [shape((size * dp, cw), BF16), shape((size, dp, cw), BF16)],
            (g_keep, flip(send, "patch", step)),
            after=(last[0],),
        )
    grad_pos = lax.ppermute(joined(g_rows[0], gate(g_rows[1], first)).reshape(per, cw), "patch", back)
    grad_w_out, grad_pos = call(
        functools.partial(halve_kernel, 2 * step),
        "halve",
        (shape((dp, cw)), shape((per, cw))),
        (g_keep, flip(send, "patch", 2 * step), grad_pos),
    )

    bit = 1
    while 2 * bit < n_j:
        bit *= 2
        px_keep, px_send = call(
            pixel_add_kernel,
            "pixel_add",
            [shape((n_j // (2 * bit), 4 * vp, rows), BF16)] * 2,
            (px_keep, px_got),
            after=(first,),
        )
        px_got = flip(px_send, "var", bit)
    mixed = call(
        functools.partial(mixed_kernel, vl, n_j),
        "mixed",
        shape((rows, cw), BF16),
        (lengths, lead_hours, wo, vk, pos_lo, pos_hi, *atts),
        [pltpu.VMEM((owners, per, cw), BF16)],
        smem=2,
        after=(first,),
    )

    last = [last[0]] + [flip(last[k], "var", k) for k in others]
    gwv, gwk, gwq, gq, ge, gb, gl, grad_pixels = call(
        functools.partial(final_kernel, eb, vl, rl, dp, n_j),
        "final",
        (
            shape((rl, D)),
            shape((rl, D)),
            shape((rl, D)),
            shape((1, rl)),
            shape((5, vl, dp)),
            shape((1, rl)),
            shape((1, rl)),
            shape((vl, 4, rows), BF16),
        ),
        (w_query, query[:, None], px_keep, px_got, *last),
        [pltpu.VMEM((eb, dp), F32), pltpu.VMEM((8, D), F32), pltpu.VMEM((4 * vp, rows), F32), pltpu.VMEM((4 * vl, rows), F32)],
        after=(send,),
    )
    return (
        mixed,
        grad_pixels,
        ge.transpose(1, 0, 2),
        gq.reshape(rl),
        gwq,
        gwk,
        gwv,
        grad_w_out,
        gb.reshape(rl),
        grad_pos,
        gl.reshape(rl),
    )


def solution(mesh):
    both = P(("patch", "var"))
    rows2 = P(("patch", "var"), None)
    return jax.shard_map(
        shards,
        mesh=mesh,
        in_specs=(
            P("var", None, "patch"),
            P("var", None, "patch"),
            both,
            rows2,
            rows2,
            rows2,
            P("patch", "var"),
            both,
            P("patch", "var"),
            both,
            P(),
            P(),
            P(),
            P("patch", "var"),
        ),
        out_specs=(
            P("patch", "var"),
            P("var", None, "patch"),
            P("var", None, "patch"),
            both,
            rows2,
            rows2,
            rows2,
            P("patch", "var"),
            both,
            P("patch", "var"),
            both,
        ),
        check_vma=False,
    )
```
